128 devices in a mesh: patch: 16 (over y, x_lo, core), tensor: 8 (over z, x_hi).
Axes of the slice: x: 4 (x_hi: 2, x_lo: 2; x = x_hi * 2 + x_lo), y: 4, z: 4, core: 2. Of those that a mesh axis runs over, the one named last changes fastest.
Arguments:
- patches: float32 [4096, 768], P('patch'), may hold values from -6 to 6
- perms: int32 [2, 768], replicated, may hold values from 0 to 767, each once within a row
- w_in: float32 [2, 384, 1024], replicated, may hold values from -0.3125 to 0.3125
- gain_mix: float32 [2, 1024], replicated, may hold values from 0.5 to 1.5
- w_qkv: float32 [2, 1024, 3, 1024], P(None, None, None, 'tensor'), may hold values from -8 to 8
- w_mix: float32 [2, 1024, 1024], P(None, 'tensor'), may hold values from -0.1875 to 0.1875
- gain_out: float32 [2, 1024], replicated, may hold values from 0.5 to 1.5
- w_head: float32 [2, 1024, 768], P(None, 'tensor'), may hold values from -0.1875 to 0.1875
- order: int32 [4096], P('patch'), may hold values from 0 to 4095, as said below
- w_embed: bfloat16 [768, 2048], P(None, 'tensor'), may hold values from -0.21875 to 0.21875
- gain_attn: float32 [2048], replicated, may hold values from 0.5 to 1.5
- w_query: bfloat16 [2048, 2048], P(None, 'tensor'), may hold values from -5.656854 to 5.656854
- w_keyval: bfloat16 [2048, 512], replicated, may hold values from -0.125 to 0.125
- w_attn: bfloat16 [2048, 2048], P('tensor'), may hold values from -0.125 to 0.125
- gain_mlp: float32 [2048], replicated, may hold values from 0.5 to 1.5
- w_gate: bfloat16 [2048, 8192], P(None, 'tensor'), may hold values from -0.125 to 0.125
- w_up: bfloat16 [2048, 8192], P(None, 'tensor'), may hold values from -0.125 to 0.125
- w_down: bfloat16 [8192, 2048], P('tensor'), may hold values from -0.0625 to 0.0625
Outputs:
- decoded: bfloat16 [4096, 2048], P('patch', 'tensor')
- logdet: float32 [4096], P('patch')
The draws below stay inside these ranges and needn't reach their ends.
Inputs may be any that keep to these rules, and one draw needn't show every extreme that they name: `order`: a permutation of all positions; the tokens of each aligned block of 64 hold exactly that block's positions. `perms`: each row holds every channel once.
All inputs are finite; a program needn't handle non-finite values.
Results may differ from the reference program's by a relative error of at most 0.015.
The reference program's roundings to bfloat16 on the way (of `embedded`, `keyval`, `attended` and `inner`) count: a program that leaves them out, or rounds other values in their place, can miss the bound.
Values may be sent and summed in bfloat16 or wider, within the bound.
No kernel may reach another device: no remote copies, remote signals or barrier semaphores. Data moves between devices by JAX's collectives and lax.ppermute only.
A program may use at most 128 MiB of HBM per device.

```python
import jax
import jax.numpy as jnp
from jax import lax

PD = 768
HALF = 384
W = 1024
HEADS = 16
HD = 64
BLOCKS = 2
DM = 2048
DHEADS = 8
DH = 256
DQ = 2048
FF = 8192
SHUF = 64
PATCHES = 4096


def draw_order(key, part):
    count = PATCHES // SHUF
    keys = jax.random.split(jax.random.fold_in(key, 17), count)
    shuffles = jax.vmap(lambda single: jax.random.permutation(single, SHUF))(keys)
    offsets = (jnp.arange(count, dtype=jnp.int32) * SHUF)[:, None]
    return (shuffles.astype(jnp.int32) + offsets).reshape(PATCHES).astype(jnp.int32)


def draw_w_qkv(key, part):
    base = jnp.clip(jax.random.normal(jax.random.fold_in(key, 31), (BLOCKS, W, 3, W), jnp.float32), -4.0, 4.0) * W ** (-0.5)
    return base


def draw_w_query(key, part):
    base = jnp.clip(jax.random.normal(jax.random.fold_in(key, 41), (DM, DQ), jnp.float32), -4.0, 4.0) * DM ** (-0.5)
    return base.astype(jnp.bfloat16)


def level_of(rng, shape, pieces, low, high):
    level = 1.0
    for axis_at, parts in pieces:
        heights = jax.random.uniform(jax.random.fold_in(jax.random.fold_in(rng, 6), axis_at), (parts,), jnp.float32, low / len(pieces), high / len(pieces))
        level = level * jnp.repeat(jnp.exp(heights), shape[axis_at] // parts).reshape((-1,) + (1,) * (len(shape) - 1 - axis_at))
    return level


def scatter_about(key, dims, scale, bound, pieces=(), kind=jnp.bfloat16):
    values = scale * jax.random.normal(key, dims, jnp.float32)
    if pieces:
        values = values * level_of(key, dims, pieces, -0.22, 0.18)
    return jnp.clip(values, -bound, bound).astype(kind)


def setup_inputs(seed: int = 0) -> dict:
    key_list = jax.random.split(jax.random.key(seed), 19)
    return {
        "patches": scatter_about(key_list[0], (PATCHES, PD), 1.0, 6.0, ((0, 16),), jnp.float32),
        "perms": jax.vmap(lambda own: jax.random.permutation(own, PD))(jax.random.split(key_list[1], BLOCKS)).reshape((BLOCKS, PD)).astype(jnp.int32),
        "w_in": scatter_about(key_list[2], (BLOCKS, HALF, W), HALF ** -0.5, 0.3125, (), jnp.float32),
        "gain_mix": jnp.clip(1.0 + 0.1 * jax.random.normal(key_list[3], (BLOCKS, W), jnp.float32), 0.5, 1.5),
        "w_qkv": draw_w_qkv(jax.random.fold_in(key_list[18], 71), 0),
        "w_mix": scatter_about(key_list[5], (BLOCKS, W, W), W ** -0.5, 0.1875, ((1, 8),), jnp.float32),
        "gain_out": jnp.clip(1.0 + 0.1 * jax.random.normal(key_list[6], (BLOCKS, W), jnp.float32), 0.5, 1.5),
        "w_head": scatter_about(key_list[7], (BLOCKS, W, PD), W ** -0.5, 0.1875, ((1, 8),), jnp.float32),
        "order": draw_order(jax.random.fold_in(key_list[18], 71), 0),
        "w_embed": scatter_about(key_list[9], (PD, DM), PD ** -0.5, 0.21875, ((1, 8),)),
        "gain_attn": jnp.clip(1.0 + 0.1 * jax.random.normal(key_list[10], (DM,), jnp.float32), 0.5, 1.5),
        "w_query": draw_w_query(jax.random.fold_in(key_list[18], 71), 0),
        "w_keyval": scatter_about(key_list[12], (DM, 2 * DH), DM ** -0.5, 0.125),
        "w_attn": scatter_about(key_list[13], (DQ, DM), DQ ** -0.5, 0.125, ((0, 8),)),
        "gain_mlp": jnp.clip(1.0 + 0.1 * jax.random.normal(key_list[14], (DM,), jnp.float32), 0.5, 1.5),
        "w_gate": scatter_about(key_list[15], (DM, FF), DM ** -0.5, 0.125, ((1, 8),)),
        "w_up": scatter_about(key_list[16], (DM, FF), DM ** -0.5, 0.125, ((1, 8),)),
        "w_down": scatter_about(key_list[17], (FF, DM), FF ** -0.5, 0.0625, ((0, 8),)),
    }


highest = lax.Precision.HIGHEST

def normed(value, gain):
    return value * lax.rsqrt(lax.optimization_barrier(jnp.mean(value * value, axis=-1, keepdims=True)) + 1e-06) * gain

def mm32(left, right):
    return jnp.dot(left, right, precision=highest, preferred_element_type=jnp.float32)

def mmbf(left, right):
    return jnp.dot(left.astype(jnp.float32), right.astype(jnp.float32), precision=highest, preferred_element_type=jnp.float32)

def reference(patches, perms, w_in, gain_mix, w_qkv, w_mix, gain_out, w_head, order, w_embed, gain_attn, w_query, w_keyval, w_attn, gain_mlp, w_gate, w_up, w_down):
    field = patches
    total = PATCHES
    logdet = jnp.zeros((total,), jnp.float32)
    for blk in range(BLOCKS):
        perm = perms[blk].astype(jnp.int32)
        inverse = jnp.argsort(perm).astype(jnp.int32)
        shuffled = jnp.take(field, perm, axis=1)
        cond_half = shuffled[:, :HALF]
        moved = shuffled[:, HALF:]
        hidden = mm32(cond_half, w_in[blk])
        unit = normed(hidden, gain_mix[blk])
        query = mm32(unit, w_qkv[blk, :, 0]).reshape(total, HEADS, HD).transpose(1, 0, 2)
        keys = mm32(unit, w_qkv[blk, :, 1]).reshape(total, HEADS, HD).transpose(1, 0, 2)
        values = mm32(unit, w_qkv[blk, :, 2]).reshape(total, HEADS, HD).transpose(1, 0, 2)

        def one_head(trio):
            score = mm32(trio[0], trio[1].T) * HD ** (-0.5)
            probs = jax.nn.softmax(score, axis=-1)
            return mm32(probs, trio[2])
        mixed = lax.map(one_head, (query, keys, values)).transpose(1, 0, 2).reshape(total, W)
        hidden2 = hidden + mm32(mixed, w_mix[blk])
        params = mm32(normed(hidden2, gain_out[blk]), w_head[blk])
        log_scale = jnp.tanh(params[:, :HALF])
        moved2 = moved * jnp.exp(log_scale) + params[:, HALF:]
        logdet = logdet + lax.optimization_barrier(jnp.sum(log_scale, axis=1))
        field = jnp.take(jnp.concatenate([cond_half, moved2], axis=1), inverse, axis=1)
    embedded = mmbf(field.astype(jnp.bfloat16), w_embed).astype(jnp.bfloat16)
    start = embedded.astype(jnp.float32)
    normed_in = normed(start, gain_attn).astype(jnp.bfloat16)
    query = mmbf(normed_in, w_query).astype(jnp.bfloat16)
    query = query.reshape(total, DHEADS, DH).transpose(1, 0, 2)
    keyval = mmbf(normed_in, w_keyval).astype(jnp.bfloat16)
    keys = keyval[:, :DH]
    values = keyval[:, DH:]
    visible = order[None, :] <= order[:, None]

    def causal_head(qhead):
        score = mmbf(qhead, keys.T) * DH ** (-0.5)
        score = jnp.where(visible, score, -jnp.inf)
        top = lax.optimization_barrier(jnp.max(score, axis=-1, keepdims=True))
        weights = jnp.exp(score - top)
        denom = lax.optimization_barrier(jnp.sum(weights, axis=-1, keepdims=True))
        acc = mmbf(weights.astype(jnp.bfloat16), values)
        return (acc / denom).astype(jnp.bfloat16)
    attended = lax.map(causal_head, query).transpose(1, 0, 2).reshape(total, DQ)
    resid = start + mmbf(attended, w_attn)
    normed_mlp = normed(resid, gain_mlp).astype(jnp.bfloat16)
    gate = mmbf(normed_mlp, w_gate)
    upward = mmbf(normed_mlp, w_up)
    inner = (jax.nn.gelu(gate, approximate=True) * upward).astype(jnp.bfloat16)
    decoded = (resid + mmbf(inner, w_down)).astype(jnp.bfloat16)
    return (decoded, logdet)
```

```python
import functools

import jax
import jax.numpy as jnp
from jax import lax
from jax.experimental import pallas as pl
from jax.experimental.pallas import tpu as pltpu
from jax.sharding import PartitionSpec as P

HEADS = 16
BLOCKS = 2
DH = 256
NP = 16
NT = 8


highest = lax.Precision.HIGHEST
bf16 = jnp.bfloat16
f32 = jnp.float32


def normed(value, gain):
    return value * lax.rsqrt(jnp.mean(value * value, axis=-1, keepdims=True) + 1e-06) * gain


def mm32(left, right):
    return jnp.dot(left, right, precision=highest, preferred_element_type=f32)


CORE = [(i, i ^ 1) for i in range(NP)]


def hop(dy, dx):
    def to(i):
        y, x, c = i // 4, (i // 2) % 2, i % 2
        return ((y + dy) % 4 * 2 + (x + dx) % 2) * 2 + c

    return [(i, to(i)) for i in range(NP)]


UP, DOWN, SIDE = hop(1, 0), hop(-1, 0), hop(0, 1)


def over(value, pairs):
    return lax.ppermute(value, "patch", pairs)


def gather_chips(own):
    half = own.shape[0] // 2
    up = over(own, UP)
    down = over(own, DOWN)
    side = over(own, SIDE)
    side_up = over(side, UP)
    side_down = over(down, SIDE)
    far_a = over(up[:half], UP)
    far_b = over(down[half:], DOWN)
    far = jnp.concatenate([far_a, far_b], 0)
    side_far = over(far, SIDE)
    return [own, up, down, side, side_up, side_down, far, side_far]


def exchange(parts):
    return lax.all_to_all(parts, "tensor", 0, 0)


def scatter_rows(partial_value):
    rows, cols = partial_value.shape
    parts = exchange(partial_value.reshape(NT, rows // NT, cols))
    return jnp.sum(parts.astype(f32), axis=0)


def gather_rows(own):
    rows, cols = own.shape
    return exchange(jnp.broadcast_to(own, (NT, rows, cols))).reshape(NT * rows, cols)


def split2(x):
    a = x.astype(bf16)
    b = (x - a.astype(f32)).astype(bf16)
    return a, b


def split3(x):
    a = x.astype(bf16)
    r = x - a.astype(f32)
    b = r.astype(bf16)
    c = (r - b.astype(f32)).astype(bf16)
    return a, b, c


def attend_kernel(q_ref, *refs):
    kv_refs, o_ref, s_ref = refs[:8], refs[8], refs[9]
    hd = q_ref.shape[1]
    q1, q2, q3 = split3(q_ref[...] * (hd ** (-0.5)))
    qs = jnp.concatenate([q1, q1, q2, q1, q2, q3], axis=1)
    top = None
    for j, kv_ref in enumerate(kv_refs):
        k1, k2, k3 = split3(kv_ref[:, :hd])
        ks = jnp.concatenate([k1, k2, k1, k3, k2, k1], axis=1)
        s = lax.dot_general(qs, ks, (((1,), (1,)), ((), ())), preferred_element_type=f32)
        s_ref[j] = s
        m = jnp.max(s, axis=1, keepdims=True)
        top = m if top is None else jnp.maximum(top, m)
    total = None
    acc = None
    for j, kv_ref in enumerate(kv_refs):
        p = jnp.exp(s_ref[j] - top)
        t = jnp.sum(p, axis=1, keepdims=True)
        v1, v2, v3 = split3(kv_ref[:, hd:])
        p1, p2 = split2(p)
        a = jnp.dot(p1, jnp.concatenate([v1, v2, v3], axis=1), preferred_element_type=f32)
        b = jnp.dot(p2, jnp.concatenate([v1, v2], axis=1), preferred_element_type=f32)
        a = a[:, :hd] + (a[:, hd : 2 * hd] + b[:, :hd]) + (a[:, 2 * hd :] + b[:, hd:])
        total = t if total is None else total + t
        acc = a if acc is None else acc + a
    o_ref[...] = acc / total


def attend(query, pieces):
    rows, hd = query.shape
    keys = pieces[0].shape[0]
    block = 256
    return pl.pallas_call(
        attend_kernel,
        grid=(rows // block,),
        in_specs=[pl.BlockSpec((block, hd), lambda i: (i, 0))]
        + [pl.BlockSpec((keys, 2 * hd), lambda i: (0, 0))] * 8,
        out_specs=pl.BlockSpec((block, hd), lambda i: (i, 0)),
        out_shape=jax.ShapeDtypeStruct((rows, hd), f32),
        scratch_shapes=[pltpu.VMEM((8, block, keys), f32)],
        compiler_params=pltpu.CompilerParams(vmem_limit_bytes=32 << 20),
        name="attend",
    )(query, *pieces)


def on_device(
    patches,
    perms,
    w_in,
    gain_mix,
    w_qkv,
    w_mix,
    gain_out,
    w_head,
    order,
    w_embed,
    gain_attn,
    w_query,
    w_keyval,
    w_attn,
    gain_mlp,
    w_gate,
    w_up,
    w_down,
):
    rows = patches.shape[0]
    half = w_in.shape[1]
    local_w = w_qkv.shape[3]
    hd = local_w // 2
    where = lax.axis_index("tensor")
    patch = lax.axis_index("patch")
    even = patch % 2 == 0
    part = rows // NT

    def own_rows(x):
        return lax.dynamic_slice_in_dim(x, where * part, part, 0)

    field = patches
    logdet = jnp.zeros((part,), f32)
    for blk in range(BLOCKS):
        perm = perms[blk]
        inverse = jnp.argsort(perm)
        shuffled = jnp.take(field, perm, axis=1)
        cond_half = shuffled[:, :half]
        hidden = mm32(cond_half, w_in[blk])
        unit = normed(hidden, gain_mix[blk])
        qkv = [mm32(unit, w_qkv[blk, :, i]) for i in range(3)]
        mine = [jnp.where(even, x[:, :hd], x[:, hd:]) for x in qkv]
        other = [jnp.where(even, x[:, hd:], x[:, :hd]) for x in qkv]
        got = over(jnp.concatenate(other, axis=1), CORE)
        query = jnp.concatenate([mine[0], got[:, :hd]], axis=0)
        keyval = jnp.concatenate(
            [jnp.concatenate(mine[1:], axis=1), got[:, hd:]], axis=0
        )
        out = attend(query, gather_chips(keyval))
        back = over(out[rows:], CORE)
        front = out[:rows]
        mixed = jnp.concatenate(
            [jnp.where(even, front, back), jnp.where(even, back, front)], axis=1
        )
        mix = scatter_rows(mm32(mixed, w_mix[blk]))
        normed_out = normed(own_rows(hidden) + mix, gain_out[blk])
        own_cols = exchange(normed_out.reshape(part, NT, local_w).transpose(1, 0, 2))
        params = scatter_rows(mm32(own_cols.reshape(rows, local_w), w_head[blk]))
        log_scale = jnp.tanh(params[:, :half])
        moved = own_rows(shuffled[:, half:])
        moved2 = moved * jnp.exp(log_scale) + params[:, half:]
        logdet = logdet + jnp.sum(log_scale, axis=1)
        if blk == BLOCKS - 1:
            moved2, cond_half = moved2.astype(bf16), cond_half.astype(bf16)
        field = jnp.take(
            jnp.concatenate([cond_half, gather_rows(moved2)], axis=1), inverse, axis=1
        )
    logdet = gather_rows(jnp.broadcast_to(logdet[:, None], (part, 128)))[:, 0]
    embed_part = jnp.dot(field, w_embed, preferred_element_type=f32).astype(bf16)
    embedded = exchange(jnp.broadcast_to(embed_part, (NT,) + embed_part.shape))
    embedded = embedded.transpose(1, 0, 2).reshape(rows, -1)
    start_f = embedded.astype(f32)
    normed_in = normed(start_f, gain_attn).astype(bf16)
    query_dec = jnp.dot(normed_in, w_query, preferred_element_type=f32).astype(bf16)
    keyval = jnp.dot(normed_in, w_keyval, preferred_element_type=f32).astype(bf16)
    pieces = gather_chips(keyval)
    swapped = [over(x, CORE) for x in pieces]
    keyvals = jnp.stack(pieces + swapped)

    def chip(i):
        return i // 4, (i // 2) % 2, i % 2

    y, x, c = chip(patch)
    owners = []
    for dc in (0, 1):
        for dy, dx in ((0, 0), (-1, 0), (1, 0), (0, 1), (-1, 1), (1, 1), (2, 0), (2, 1)):
            owners.append((((y + dy) % 4) * 2 + (x + dx) % 2) * 2 + (c + dc) % 2)
    owners = jnp.stack(owners)
    score = jnp.einsum(
        "qd,nkd->qnk", query_dec, keyvals[:, :, :DH], preferred_element_type=f32
    ) * (DH ** (-0.5))
    inside = (order[None, :] <= order[:, None])[:, None, :]
    before = (owners < patch)[None, :, None]
    same = (owners == patch)[None, :, None]
    score = jnp.where(before | (same & inside), score, -jnp.inf)
    top = jnp.max(score, axis=(1, 2), keepdims=True)
    weights = jnp.exp(score - top)
    run_sum = jnp.sum(weights, axis=(1, 2))
    acc = jnp.einsum(
        "qnk,nkd->qd", weights.astype(bf16), keyvals[:, :, DH:], preferred_element_type=f32
    )
    attended = (acc / run_sum[:, None]).astype(bf16)
    partial_value = jnp.dot(attended, w_attn, preferred_element_type=f32).astype(bf16)
    resid = own_rows(start_f) + scatter_rows(partial_value)
    normed_mlp = gather_rows(normed(resid, gain_mlp).astype(bf16))
    gate = jnp.dot(normed_mlp, w_gate, preferred_element_type=f32)
    upward = jnp.dot(normed_mlp, w_up, preferred_element_type=f32)
    inner = (jax.nn.gelu(gate, approximate=True) * upward).astype(bf16)
    down = jnp.dot(inner, w_down, preferred_element_type=f32)
    cols = down.shape[1] // NT
    parts = exchange(down.astype(bf16).reshape(rows, NT, cols).transpose(1, 0, 2))
    resid_cols = exchange(resid.reshape(part, NT, cols).transpose(1, 0, 2)).reshape(rows, cols)
    decoded = (jnp.sum(parts.astype(f32), axis=0) + resid_cols).astype(bf16)
    return (decoded, logdet)


def solution(mesh):
    return jax.shard_map(
        on_device,
        mesh=mesh,
        in_specs=(
            P("patch", None),
            P(),
            P(),
            P(),
            P(None, None, None, "tensor"),
            P(None, "tensor", None),
            P(),
            P(None, "tensor", None),
            P("patch"),
            P(None, "tensor"),
            P(),
            P(None, "tensor"),
            P(),
            P("tensor", None),
            P(),
            P(None, "tensor"),
            P(None, "tensor"),
            P("tensor", None),
        ),
        out_specs=(P("patch", "tensor"), P("patch")),
        check_vma=False,
    )
```

```python
import functools

import jax
import jax.numpy as jnp
from jax import lax
from jax.experimental import pallas as pl
from jax.experimental.pallas import tpu as pltpu
from jax.sharding import PartitionSpec as P


BLOCKS = 2
DH = 256
NP = 16
NT = 8


highest = lax.Precision.HIGHEST
bf16 = jnp.bfloat16
f32 = jnp.float32


def normed(value, gain):
    return value * lax.rsqrt(jnp.mean(value * value, axis=-1, keepdims=True) + 1e-06) * gain


def mm32(left, right):
    return jnp.dot(left, right, precision=highest, preferred_element_type=f32)


CORE = [(i, i ^ 1) for i in range(NP)]


def hop(dy, dx):
    def to(i):
        y, x, c = i // 4, (i // 2) % 2, i % 2
        return ((y + dy) % 4 * 2 + (x + dx) % 2) * 2 + c

    return [(i, to(i)) for i in range(NP)]


UP, DOWN, SIDE = hop(1, 0), hop(-1, 0), hop(0, 1)


def over(value, pairs):
    return lax.ppermute(value, "patch", pairs)


def gather_chips(own):
    half = own.shape[0] // 2
    up = over(own, UP)
    down = over(own, DOWN)
    side = over(own, SIDE)
    side_up = over(side, UP)
    side_down = over(down, SIDE)
    far_a = over(up[:half], UP)
    far_b = over(down[half:], DOWN)
    far = jnp.concatenate([far_a, far_b], 0)
    side_far = over(far, SIDE)
    return [own, up, down, side, side_up, side_down, far, side_far]


def exchange(parts):
    return lax.all_to_all(parts, "tensor", 0, 0)


def split2(x):
    a = x.astype(bf16)
    b = (x - a.astype(f32)).astype(bf16)
    return a, b


def split3(x):
    a = x.astype(bf16)
    r = x - a.astype(f32)
    b = r.astype(bf16)
    c = (r - b.astype(f32)).astype(bf16)
    return a, b, c


def select(x, one_hot):
    return sum(jnp.dot(p, one_hot, preferred_element_type=f32) for p in reversed(split3(x)))


VMEM = pl.BlockSpec(memory_space=pltpu.VMEM)
SMEM = pl.BlockSpec(memory_space=pltpu.SMEM)


def call(body, outs, *args, scratch=(), flops=0, limit=40, smem=0):
    moved = sum(x.size * x.dtype.itemsize for x in args)
    return pl.pallas_call(
        body,
        in_specs=[SMEM] * smem + [VMEM] * (len(args) - smem),
        out_specs=[VMEM] * len(outs),
        out_shape=[jax.ShapeDtypeStruct(*o) for o in outs],
        scratch_shapes=list(scratch),
        compiler_params=pltpu.CompilerParams(vmem_limit_bytes=limit << 20),
        cost_estimate=pl.CostEstimate(flops=flops, bytes_accessed=moved, transcendentals=0),
    )(*args)


def pre_kernel(ids, field_ref, perm_ref, w_in_ref, gain_ref, w_ref, hidden_ref, q_ref, kv_ref, oth_ref):
    even = ids[0] == 0
    half = w_in_ref.shape[0]
    width = field_ref.shape[1]
    lanes = w_ref.shape[1] // 3
    hd = lanes // 2
    row = lax.broadcasted_iota(jnp.int32, (width, half), 0)
    take = jnp.where(row == perm_ref[...], 1.0, 0.0).astype(bf16)
    cond = select(field_ref[...], take)
    hidden = mm32(cond, w_in_ref[...])
    hidden_ref[...] = hidden
    unit = normed(hidden, gain_ref[...])
    qkv = mm32(unit, w_ref[...])

    def pick(i, first):
        x = qkv[:, i * lanes : (i + 1) * lanes]
        return jnp.where(first, x[:, :hd], x[:, hd:])

    q_ref[...] = pick(0, even)
    kv_ref[...] = jnp.concatenate([pick(1, even), pick(2, even)], axis=1)
    odd = jnp.logical_not(even)
    oth_ref[...] = jnp.concatenate([pick(0, odd), pick(1, odd), pick(2, odd)], axis=1)


def pre(ids, field, perm, w_in, gain, w_qkv):
    rows, full = field.shape[0], w_in.shape[1]
    lanes = w_qkv.shape[1] // 3
    hd = lanes // 2
    return call(
        pre_kernel,
        [((rows, full), f32), ((rows, hd), f32), ((rows, 2 * hd), f32), ((rows, 3 * hd), f32)],
        ids,
        field,
        perm[None, : w_in.shape[0]],
        w_in,
        gain[None],
        w_qkv,
        smem=1,
        flops=3 << 30,
    )


def attend_kernel(count, first, last, q_ref, *refs):
    kv_refs, refs = refs[:count], refs[count:]
    if not first:
        (acc0_ref, top0_ref, sum0_ref), refs = refs[:3], refs[3:]
    hd = q_ref.shape[1]
    s_ref = refs[-1]
    q1, q2, q3 = split3(q_ref[...] * (hd ** (-0.5)))
    qs = jnp.concatenate([q1, q1, q2, q1, q2, q3], axis=1)
    top = None if first else top0_ref[...]
    for j, kv_ref in enumerate(kv_refs):
        k1, k2, k3 = split3(kv_ref[:, :hd])
        ks = jnp.concatenate([k1, k2, k1, k3, k2, k1], axis=1)
        s = lax.dot_general(qs, ks, (((1,), (1,)), ((), ())), preferred_element_type=f32)
        s_ref[j] = s
        m = jnp.max(s, axis=1, keepdims=True)
        top = m if top is None else jnp.maximum(top, m)
    total = acc = None
    if not first:
        factor = jnp.exp(top0_ref[...] - top)
        total, acc = sum0_ref[...] * factor, acc0_ref[...] * factor
    for j, kv_ref in enumerate(kv_refs):
        p = jnp.exp(s_ref[j] - top)
        t = jnp.sum(p, axis=1, keepdims=True)
        v1, v2, v3 = split3(kv_ref[:, hd:])
        p1, p2 = split2(p)
        a = jnp.dot(p1, jnp.concatenate([v1, v2, v3], axis=1), preferred_element_type=f32)
        b = jnp.dot(p2, jnp.concatenate([v1, v2], axis=1), preferred_element_type=f32)
        a = a[:, :hd] + (a[:, hd : 2 * hd] + b[:, :hd]) + (a[:, 2 * hd :] + b[:, hd:])
        total = t if total is None else total + t
        acc = a if acc is None else acc + a
    if last:
        refs[0][...] = acc / total
    else:
        refs[0][...] = acc
        refs[1][...] = top
        refs[2][...] = total


def attend(query, pieces, state, last):
    rows, hd = query.shape
    keys = pieces[0].shape[0]
    block = 256
    count = len(pieces)

    def by_rows(cols):
        return pl.BlockSpec((block, cols), lambda i: (i, 0))

    widths = (hd,) if last else (hd, 1, 1)
    state_specs = [by_rows(hd), by_rows(1), by_rows(1)] if state else []
    return pl.pallas_call(
        functools.partial(attend_kernel, count, not state, last),
        grid=(rows // block,),
        in_specs=[by_rows(hd)]
        + [pl.BlockSpec((keys, 2 * hd), lambda i: (0, 0))] * count
        + state_specs,
        out_specs=[by_rows(w) for w in widths],
        out_shape=[jax.ShapeDtypeStruct((rows, w), f32) for w in widths],
        scratch_shapes=[pltpu.VMEM((count, block, keys), f32)],
        compiler_params=pltpu.CompilerParams(vmem_limit_bytes=32 << 20),
        cost_estimate=pl.CostEstimate(
            flops=4 << 30, bytes_accessed=count * keys * hd * 8, transcendentals=rows * keys * count
        ),
        name="attend",
    )(query, *pieces, *state)


def post_kernel(ids, m_ref, own_ref, oth_ref, hidden_ref, field_ref, perm_ref, gain_ref, out_ref, det_ref):
    even = ids[0] == 0
    nt, _, lanes = m_ref.shape
    full, width = hidden_ref.shape[1], field_ref.shape[1]
    half, mid = width // 2, full // 2
    mixed = jnp.concatenate([m_ref[t] for t in range(nt)], axis=1)

    def product(left, lo, hi):
        a = mm32(left, own_ref[:, :, lo:hi].reshape(nt * lanes, hi - lo))
        b = mm32(left, oth_ref[:, :, lo:hi].reshape(nt * lanes, hi - lo))
        return jnp.where(even, a, b), jnp.where(even, b, a)

    hidden = hidden_ref[...] + jnp.concatenate(product(mixed, 0, mid), axis=1)
    raw, shift = product(normed(hidden, gain_ref[...]), mid, mid + half)
    log_scale = jnp.tanh(raw)
    det_ref[...] = jnp.sum(log_scale, axis=1, keepdims=True)
    col = lax.broadcasted_iota(jnp.int32, (half, width), 1)
    put = jnp.where(col == perm_ref[...], 1.0, 0.0).astype(bf16)
    field = field_ref[...] * jnp.exp(select(log_scale, put)) + select(shift, put)
    out_ref[...] = field.astype(out_ref.dtype)


def post(ids, mixed, own, oth, hidden, field, perm, gain, kind):
    rows, width = field.shape
    return call(
        post_kernel,
        [((rows, width), kind), ((rows, 1), f32)],
        ids,
        mixed,
        own,
        oth,
        hidden,
        field,
        perm[width // 2 :, None],
        gain[None],
        smem=1,
        flops=6 << 30,
    )


def enter_kernel(emb_ref, gain_ref, w_query_ref, w_keyval_ref, q_ref, kv_ref):
    start = jnp.concatenate([emb_ref[t] for t in range(emb_ref.shape[0])], axis=1)
    unit = normed(start.astype(f32), gain_ref[...]).astype(bf16)
    kv_ref[...] = jnp.dot(unit, w_keyval_ref[...], preferred_element_type=f32).astype(bf16)
    q_ref[...] = jnp.dot(unit, w_query_ref[...], preferred_element_type=f32).astype(bf16)


def causal_kernel(ids, q_ref, order_ref, order_row_ref, *refs):
    kv_refs, o_ref, s_ref = refs[:-2], refs[-2], refs[-1]
    dh = q_ref.shape[1]
    patch = ids[1]
    own = order_row_ref[...] <= order_ref[...]
    top = None
    for j, kv_ref in enumerate(kv_refs):
        owner = ids[2 + j]
        s = lax.dot_general(
            q_ref[...], kv_ref[:, :dh], (((1,), (1,)), ((), ())), preferred_element_type=f32
        ) * (dh ** (-0.5))
        if j == 0:
            s = jnp.where(own, s, -jnp.inf)
        else:
            s = jnp.where(owner < patch, s, -jnp.inf)
        s_ref[j] = s
        m = jnp.max(s, axis=1, keepdims=True)
        top = m if top is None else jnp.maximum(top, m)
    total = acc = None
    for j, kv_ref in enumerate(kv_refs):
        p = jnp.exp(s_ref[j] - top)
        t = jnp.sum(p, axis=1, keepdims=True)
        a = jnp.dot(p.astype(bf16), kv_ref[:, dh:], preferred_element_type=f32)
        total = t if total is None else total + t
        acc = a if acc is None else acc + a
    o_ref[...] = (acc / total).astype(bf16)


def mlp_kernel(
    ids, att_ref, emb_ref, own_ref, oth_ref, gain_ref, gate_ref, up_ref, down_ref,
    out_ref, resid_ref, full_ref, inner_ref,
):
    even = ids[0] == 0
    nt, _, lanes = att_ref.shape
    half = own_ref.shape[2]
    att = jnp.concatenate([att_ref[t] for t in range(nt)], axis=1)
    tile = 256

    for start in range(0, half, tile):
        a = jnp.dot(att, own_ref[:, :, start : start + tile].reshape(-1, tile), preferred_element_type=f32)
        b = jnp.dot(att, oth_ref[:, :, start : start + tile].reshape(-1, tile), preferred_element_type=f32)
        for x, at in ((jnp.where(even, a, b), start), (jnp.where(even, b, a), half + start)):
            full_ref[:, at : at + tile] = x + emb_ref[at // lanes].astype(f32)
    mine = pl.multiple_of(ids[1] * lanes, lanes)
    resid_ref[...] = full_ref[:, pl.ds(mine, lanes)]
    unit = normed(full_ref[...], gain_ref[...]).astype(bf16)
    for start in range(0, gate_ref.shape[1], tile):
        cut = slice(start, start + tile)
        gate = jnp.dot(unit, gate_ref[:, cut], preferred_element_type=f32)
        up = jnp.dot(unit, up_ref[:, cut], preferred_element_type=f32)
        inner_ref[:, cut] = (jax.nn.gelu(gate, approximate=True) * up).astype(bf16)
    for t in range(nt):
        out_ref[t] = jnp.dot(
            inner_ref[...], down_ref[:, t * lanes : (t + 1) * lanes], preferred_element_type=f32
        ).astype(bf16)


def tied(value, *others):
    return lax.optimization_barrier((value, *others))[0]


def on_device(
    patches,
    perms,
    w_in,
    gain_mix,
    w_qkv,
    w_mix,
    gain_out,
    w_head,
    order,
    w_embed,
    gain_attn,
    w_query,
    w_keyval,
    w_attn,
    gain_mlp,
    w_gate,
    w_up,
    w_down,
):
    rows = patches.shape[0]
    full = w_in.shape[2]
    local_w = w_qkv.shape[3]
    where = lax.axis_index("tensor")
    patch = lax.axis_index("patch")
    core = patch % 2
    even = core == 0
    ids = jnp.stack([core, where]).astype(jnp.int32)

    def halves(x):
        cols = x.shape[1] // 2
        return lax.dynamic_slice_in_dim(x, core * cols, cols, 1)

    field = patches
    logdet = 0.0
    for blk in range(BLOCKS):
        perm = perms[blk]
        hidden, query, keyval, other = pre(
            ids, field, perm, w_in[blk], gain_mix[blk], w_qkv[blk].reshape(full, 3 * local_w)
        )
        hd = local_w // 2
        got = over(other, CORE)
        query = jnp.concatenate([query, got[:, :hd]], axis=0)
        keyval = jnp.concatenate([keyval, got[:, hd:]], axis=0)
        weight = jnp.concatenate([halves(w_mix[blk]), halves(w_head[blk])], axis=1)
        weight = tied(weight, keyval)
        own_w = exchange(jnp.broadcast_to(weight, (NT,) + weight.shape))
        oth_w = over(own_w, CORE)
        pieces = gather_chips(keyval)
        state = attend(query, pieces[:4], [], False)
        (out,) = attend(query, pieces[4:], state, True)
        back = over(out[rows:], CORE)
        front = out[:rows]
        mixed = jnp.concatenate(
            [jnp.where(even, front, back), jnp.where(even, back, front)], axis=1
        )
        mixed = tied(mixed, own_w)
        mixed = exchange(jnp.broadcast_to(mixed, (NT,) + mixed.shape))
        field, det = post(
            ids, mixed, own_w, oth_w, hidden, field, perm, gain_out[blk],
            bf16 if blk == BLOCKS - 1 else f32,
        )
        logdet = logdet + det[:, 0]
    embed_part = jnp.dot(field, w_embed, preferred_element_type=f32).astype(bf16)
    embedded = exchange(jnp.broadcast_to(embed_part, (NT,) + embed_part.shape))
    query_dec, keyval = call(
        enter_kernel,
        [((rows, DH), bf16), ((rows, 2 * DH), bf16)],
        embedded,
        gain_attn[None],
        w_query,
        w_keyval,
        flops=1 << 30,
    )
    attn_half = tied(halves(w_attn), keyval)
    own_a = exchange(jnp.broadcast_to(attn_half, (NT,) + attn_half.shape))
    oth_a = over(own_a, CORE)
    pieces = gather_chips(keyval)
    pieces = pieces + [over(x, CORE) for x in pieces]

    y, x = patch // 4, (patch // 2) % 2
    owners = [core, patch]
    for dc in (0, 1):
        for dy, dx in ((0, 0), (-1, 0), (1, 0), (0, 1), (-1, 1), (1, 1), (2, 0), (2, 1)):
            owners.append((((y + dy) % 4) * 2 + (x + dx) % 2) * 2 + (core + dc) % 2)
    (attended,) = call(
        causal_kernel,
        [((rows, DH), bf16)],
        jnp.stack(owners).astype(jnp.int32),
        query_dec,
        order[:, None],
        order[None],
        *pieces,
        scratch=[pltpu.VMEM((len(pieces), rows, rows), f32)],
        smem=1,
        flops=2 << 30,
    )
    attended = tied(attended, own_a)
    att = exchange(jnp.broadcast_to(attended, (NT,) + attended.shape))
    cols = w_attn.shape[1] // NT
    down, resid = call(
        mlp_kernel,
        [((NT, rows, cols), bf16), ((rows, cols), f32)],
        ids,
        att,
        embedded,
        own_a,
        oth_a,
        gain_mlp[None],
        w_gate,
        w_up,
        w_down,
        scratch=[
            pltpu.VMEM((rows, w_attn.shape[1]), f32),
            pltpu.VMEM((rows, w_gate.shape[1]), bf16),
        ],
        smem=1,
        flops=6 << 30,
    )
    decoded = (jnp.sum(exchange(down).astype(f32), axis=0) + resid).astype(bf16)
    return (decoded, logdet)


def solution(mesh):
    return jax.shard_map(
        on_device,
        mesh=mesh,
        in_specs=(
            P("patch", None),
            P(),
            P(),
            P(),
            P(None, None, None, "tensor"),
            P(None, "tensor", None),
            P(),
            P(None, "tensor", None),
            P("patch"),
            P(None, "tensor"),
            P(),
            P(None, "tensor"),
            P(),
            P("tensor", None),
            P(),
            P(None, "tensor"),
            P(None, "tensor"),
            P("tensor", None),
        ),
        out_specs=(P("patch", "tensor"), P("patch")),
        check_vma=False,
    )
```

```python
import functools

import jax
import jax.numpy as jnp
from jax import lax
from jax.experimental import pallas as pl
from jax.experimental.pallas import tpu as pltpu
from jax.sharding import PartitionSpec as P


BLOCKS = 2
DH = 256
NP = 16
NT = 8


bf16 = jnp.bfloat16
f32 = jnp.float32


def normed(value, gain):
    return value * lax.rsqrt(jnp.mean(value * value, axis=-1, keepdims=True) + 1e-06) * gain


CORE = [(i, i ^ 1) for i in range(NP)]


def hop(dy, dx):
    def to(i):
        y, x, c = i // 4, (i // 2) % 2, i % 2
        return ((y + dy) % 4 * 2 + (x + dx) % 2) * 2 + c

    return [(i, to(i)) for i in range(NP)]


UP, DOWN, SIDE = hop(1, 0), hop(-1, 0), hop(0, 1)


def over(value, pairs):
    return lax.ppermute(value, "patch", pairs)


def gather_chips(own):
    half = own.shape[0] // 2
    up = over(own, UP)
    down = over(own, DOWN)
    side = over(own, SIDE)
    side_up = over(side, UP)
    side_down = over(down, SIDE)
    far_a = over(up[:half], UP)
    far_b = over(down[half:], DOWN)
    far = jnp.concatenate([far_a, far_b], 0)
    side_far = over(far, SIDE)
    return [own, up, down, side, side_up, side_down, far, side_far]


def exchange(parts):
    return lax.all_to_all(parts, "tensor", 0, 0)


ACROSS = [(i, i ^ 1) for i in range(NT)]
COLUMNS = [[2 * z + x for z in range(NT // 2)] for x in range(2)]


def spread(own, side):
    pair = jnp.stack([own, side])
    parts = jnp.broadcast_to(pair, (NT // 2,) + pair.shape)
    return lax.all_to_all(parts, "tensor", 0, 0, axis_index_groups=COLUMNS)


def split2(x):
    a = x.astype(bf16)
    b = (x - a.astype(f32)).astype(bf16)
    return a, b


def split3(x):
    a = x.astype(bf16)
    r = x - a.astype(f32)
    b = r.astype(bf16)
    c = (r - b.astype(f32)).astype(bf16)
    return a, b, c


def select(x, one_hot, dims=(1, 0)):
    dims = (((dims[0],), (dims[1],)), ((), ()))
    a, b, c = (
        lax.dot_general(p, one_hot, dims, preferred_element_type=f32) for p in split3(x)
    )
    return (c + b) + a


def left6(x):
    a, b, c = split3(x)
    return jnp.concatenate([a, a, b, a, b, c], axis=1)


def right6(x):
    a, b, c = split3(x)
    return jnp.concatenate([a, b, a, c, b, a], axis=0)


def left3(x):
    a, b = split2(x)
    return jnp.concatenate([a, a, b], axis=1)


def right3(x):
    a, b = split2(x)
    return jnp.concatenate([a, b, a], axis=0)


def dot(left, right):
    return jnp.dot(left, right, preferred_element_type=f32)


TILE = 256


def tiles(count, body):
    def step(i, carry):
        body(pl.multiple_of(i * TILE, TILE))
        return carry

    lax.fori_loop(0, count, step, 0)


VMEM = pl.BlockSpec(memory_space=pltpu.VMEM)
SMEM = pl.BlockSpec(memory_space=pltpu.SMEM)


def call(body, outs, *args, scratch=(), flops=0, limit=16, smem=0):
    moved = sum(x.size * x.dtype.itemsize for x in args)
    return pl.pallas_call(
        body,
        in_specs=[SMEM] * smem + [VMEM] * (len(args) - smem),
        out_specs=[VMEM] * len(outs),
        out_shape=[jax.ShapeDtypeStruct(*o) for o in outs],
        scratch_shapes=list(scratch),
        compiler_params=pltpu.CompilerParams(vmem_limit_bytes=limit << 20),
        cost_estimate=pl.CostEstimate(flops=flops, bytes_accessed=moved, transcendentals=0),
    )(*args)


def cut_kernel(ids, mix_ref, head_ref, *refs):
    outs, sems = refs[:BLOCKS], refs[BLOCKS]
    copies = []
    for blk, out in enumerate(outs):
        at = 0
        for i, ref in enumerate((mix_ref, head_ref)):
            cols = ref.shape[2] // 2
            source = ref.at[blk, :, pl.ds(pl.multiple_of(ids[0] * cols, 128), cols)]
            copies.append(
                pltpu.make_async_copy(source, out.at[:, at : at + cols], sems.at[blk, i])
            )
            at += cols
    for copy in copies:
        copy.start()
    for copy in copies:
        copy.wait()


def cut(ids, w_mix, w_head):
    shape = (w_mix.shape[1], (w_mix.shape[2] + w_head.shape[2]) // 2)
    hbm = pl.BlockSpec(memory_space=pl.ANY)
    return pl.pallas_call(
        cut_kernel,
        in_specs=[SMEM, hbm, hbm],
        out_specs=[VMEM] * BLOCKS,
        out_shape=[jax.ShapeDtypeStruct(shape, f32)] * BLOCKS,
        scratch_shapes=[pltpu.SemaphoreType.DMA((BLOCKS, 2))],
        compiler_params=pltpu.CompilerParams(vmem_limit_bytes=4 << 20),
        name="cut",
    )(ids, w_mix, w_head)


def pre_kernel(
    blk, ids, field_ref, perms_ref, w_in_ref, gain_ref, w_ref,
    hidden_ref, q_ref, kv_ref, oth_ref, cond_ref, unit_ref,
):
    even = ids[0] == 0
    half, full = w_in_ref.shape[1:]
    width = field_ref.shape[1]
    hd = w_ref.shape[3] // 2
    row = lax.broadcasted_iota(jnp.int32, (width, half), 0)
    take = jnp.where(row == perms_ref[blk : blk + 1, :half], 1.0, 0.0).astype(bf16)
    cond_ref[...] = left6(select(field_ref[...], take))

    def column(at):
        cut = pl.ds(at, TILE)
        hidden_ref[:, cut] = dot(cond_ref[...], right6(w_in_ref[blk, :, cut]))

    tiles(full // TILE, column)
    unit_ref[...] = left6(normed(hidden_ref[...], gain_ref[blk : blk + 1]))
    qk = jnp.concatenate([w_ref[blk, 0], w_ref[blk, 1]], axis=1)
    qk = dot(unit_ref[...], right6(qk))
    v = dot(unit_ref[...], right6(w_ref[blk, 2]))
    q, k = qk[:, : 2 * hd], qk[:, 2 * hd :]

    def pick(x, first):
        return jnp.where(first, x[:, :hd], x[:, hd:])

    q_ref[...] = pick(q, even)
    kv_ref[...] = jnp.concatenate([pick(k, even), pick(v, even)], axis=1)
    odd = jnp.logical_not(even)
    oth_ref[...] = jnp.concatenate([pick(q, odd), pick(k, odd), pick(v, odd)], axis=1)


def pre(blk, ids, field, perms, w_in, gain, w_qkv):
    rows, (half, full) = field.shape[0], w_in.shape[1:]
    hd = w_qkv.shape[3] // 2
    return call(
        functools.partial(pre_kernel, blk),
        [((rows, full), f32), ((rows, hd), f32), ((rows, 2 * hd), f32), ((rows, 3 * hd), f32)],
        ids,
        field,
        perms,
        w_in,
        gain,
        w_qkv,
        scratch=[pltpu.VMEM((rows, 6 * half), bf16), pltpu.VMEM((rows, 6 * full), bf16)],
        smem=1,
        flops=3 << 30,
    )


def attend_kernel(count, first, last, q_ref, *refs):
    kv_refs, refs = refs[:count], refs[count:]
    if not first:
        (acc0_ref, top0_ref, sum0_ref), refs = refs[:3], refs[3:]
    hd = q_ref.shape[1]
    s_ref = refs[-1]
    q1, q2, q3 = split3(q_ref[...] * (hd ** (-0.5)))
    qs = jnp.concatenate([q1, q1, q2, q1, q2, q3], axis=1)
    top = None if first else top0_ref[...]
    for j, kv_ref in enumerate(kv_refs):
        k1, k2, k3 = split3(kv_ref[:, :hd])
        ks = jnp.concatenate([k1, k2, k1, k3, k2, k1], axis=1)
        s = lax.dot_general(qs, ks, (((1,), (1,)), ((), ())), preferred_element_type=f32)
        s_ref[j] = s
        m = jnp.max(s, axis=1, keepdims=True)
        top = m if top is None else jnp.maximum(top, m)
    total = acc = None
    if not first:
        factor = jnp.exp(top0_ref[...] - top)
        total, acc = sum0_ref[...] * factor, acc0_ref[...] * factor
    for j, kv_ref in enumerate(kv_refs):
        p = jnp.exp(s_ref[j] - top)
        t = jnp.sum(p, axis=1, keepdims=True)
        v1, v2, v3 = split3(kv_ref[:, hd:])
        p1, p2 = split2(p)
        a = jnp.dot(p1, jnp.concatenate([v1, v2, v3], axis=1), preferred_element_type=f32)
        b = jnp.dot(p2, jnp.concatenate([v1, v2], axis=1), preferred_element_type=f32)
        a = a[:, :hd] + (a[:, hd : 2 * hd] + b[:, :hd]) + (a[:, 2 * hd :] + b[:, hd:])
        total = t if total is None else total + t
        acc = a if acc is None else acc + a
    if last:
        refs[0][...] = acc / total
    else:
        refs[0][...] = acc
        refs[1][...] = top
        refs[2][...] = total


def attend(query, pieces, state, last):
    rows, hd = query.shape
    keys = pieces[0].shape[0]
    block = 256
    count = len(pieces)

    def by_rows(cols):
        return pl.BlockSpec((block, cols), lambda i: (i, 0))

    widths = (hd,) if last else (hd, 1, 1)
    state_specs = [by_rows(hd), by_rows(1), by_rows(1)] if state else []
    return pl.pallas_call(
        functools.partial(attend_kernel, count, not state, last),
        grid=(rows // block,),
        in_specs=[by_rows(hd)]
        + [pl.BlockSpec((keys, 2 * hd), lambda i: (0, 0))] * count
        + state_specs,
        out_specs=[by_rows(w) for w in widths],
        out_shape=[jax.ShapeDtypeStruct((rows, w), f32) for w in widths],
        scratch_shapes=[pltpu.VMEM((count, block, keys), f32)],
        compiler_params=pltpu.CompilerParams(vmem_limit_bytes=16 << 20),
        cost_estimate=pl.CostEstimate(
            flops=4 << 30, bytes_accessed=count * keys * hd * 8, transcendentals=rows * keys * count
        ),
        name="attend",
    )(query, *pieces, *state)


def post_kernel(
    blk, ids, m_ref, own_ref, oth_ref, hidden_ref, field_ref, perms_ref, gain_ref,
    out_ref, det_ref, left_ref, sum_ref,
):
    even = ids[0] == 0
    nt, _, lanes = m_ref.shape
    full, width = hidden_ref.shape[1], field_ref.shape[1]
    half, mid = width // 2, full // 2
    order = [2 * (t // 2) + (ids[1] + t) % 2 for t in range(nt)]
    left_ref[...] = left3(jnp.concatenate([m_ref[t] for t in order], axis=1))

    def column(at):
        cut = pl.ds(at, TILE)
        a = dot(left_ref[...], right3(own_ref[:, :, cut].reshape(full, TILE)))
        b = dot(left_ref[...], right3(oth_ref[:, :, cut].reshape(full, TILE)))
        sum_ref[:, cut] = hidden_ref[:, cut] + jnp.where(even, a, b)
        cut = pl.ds(pl.multiple_of(at + mid, TILE), TILE)
        sum_ref[:, cut] = hidden_ref[:, cut] + jnp.where(even, b, a)

    tiles(mid // TILE, column)
    sum_ref[...] = normed(sum_ref[...], gain_ref[blk : blk + 1])
    parts = [sum_ref[:, pl.ds(pl.multiple_of(t * lanes, lanes), lanes)] for t in order]
    left_ref[...] = left3(jnp.concatenate(parts, axis=1))
    a = dot(left_ref[...], right3(own_ref[:, :, mid:].reshape(full, half)))
    b = dot(left_ref[...], right3(oth_ref[:, :, mid:].reshape(full, half)))
    log_scale, shift = jnp.tanh(jnp.where(even, a, b)), jnp.where(even, b, a)
    det_ref[...] = jnp.sum(log_scale, axis=1, keepdims=True)
    row = lax.broadcasted_iota(jnp.int32, (width, half), 0)
    put = jnp.where(row == perms_ref[blk : blk + 1, half:], 1.0, 0.0).astype(bf16)
    field = field_ref[...] * jnp.exp(select(log_scale, put, (1, 1))) + select(shift, put, (1, 1))
    out_ref[...] = field.astype(out_ref.dtype)


def post(blk, ids, mixed, own, oth, hidden, field, perms, gain, kind):
    rows, width = field.shape
    full = hidden.shape[1]
    return call(
        functools.partial(post_kernel, blk),
        [((rows, width), kind), ((rows, 1), f32)],
        ids,
        mixed,
        own.reshape((NT,) + own.shape[2:]),
        oth.reshape((NT,) + oth.shape[2:]),
        hidden,
        field,
        perms,
        gain,
        scratch=[pltpu.VMEM((rows, 3 * full), bf16), pltpu.VMEM((rows, full), f32)],
        smem=1,
        flops=6 << 30,
    )


def enter_kernel(emb_ref, gain_ref, w_query_ref, w_keyval_ref, q_ref, kv_ref):
    start = jnp.concatenate([emb_ref[t] for t in range(emb_ref.shape[0])], axis=1)
    unit = normed(start.astype(f32), gain_ref[...]).astype(bf16)
    kv_ref[...] = jnp.dot(unit, w_keyval_ref[...], preferred_element_type=f32).astype(bf16)
    q_ref[...] = jnp.dot(unit, w_query_ref[...], preferred_element_type=f32).astype(bf16)


def causal_kernel(ids, q_ref, order_ref, order_row_ref, *refs):
    kv_refs, o_ref, s_ref = refs[:-2], refs[-2], refs[-1]
    dh = q_ref.shape[1]
    patch = ids[1]
    own = order_row_ref[...] <= order_ref[...]
    top = None
    for j, kv_ref in enumerate(kv_refs):
        owner = ids[2 + j]
        s = lax.dot_general(
            q_ref[...], kv_ref[:, :dh], (((1,), (1,)), ((), ())), preferred_element_type=f32
        ) * (dh ** (-0.5))
        if j == 0:
            s = jnp.where(own, s, -jnp.inf)
        else:
            s = jnp.where(owner < patch, s, -jnp.inf)
        s_ref[j] = s
        m = jnp.max(s, axis=1, keepdims=True)
        top = m if top is None else jnp.maximum(top, m)
    total = acc = None
    for j, kv_ref in enumerate(kv_refs):
        p = jnp.exp(s_ref[j] - top)
        t = jnp.sum(p, axis=1, keepdims=True)
        a = jnp.dot(p.astype(bf16), kv_ref[:, dh:], preferred_element_type=f32)
        total = t if total is None else total + t
        acc = a if acc is None else acc + a
    o_ref[...] = (acc / total).astype(bf16)


def mlp_kernel(
    ids, att_ref, emb_ref, own_ref, oth_ref, gain_ref, gate_ref, up_ref, down_ref,
    out_ref, resid_ref, full_ref, inner_ref, left_ref,
):
    even = ids[0] == 0
    nt, _, lanes = att_ref.shape
    half = own_ref.shape[2]
    order = [2 * (t // 2) + (ids[1] + t) % 2 for t in range(nt)]
    left_ref[...] = jnp.concatenate([att_ref[t] for t in order], axis=1)

    def project(at):
        cut = pl.ds(at, TILE)
        a = dot(left_ref[...], own_ref[:, :, cut].reshape(nt * lanes, TILE))
        b = dot(left_ref[...], oth_ref[:, :, cut].reshape(nt * lanes, TILE))
        full_ref[:, cut] = jnp.where(even, a, b) + emb_ref[at // lanes].astype(f32)
        cut = pl.ds(pl.multiple_of(at + half, TILE), TILE)
        full_ref[:, cut] = jnp.where(even, b, a) + emb_ref[(at + half) // lanes].astype(f32)

    tiles(half // TILE, project)
    resid_ref[...] = full_ref[:, pl.ds(pl.multiple_of(ids[1] * lanes, lanes), lanes)]
    left_ref[...] = normed(full_ref[...], gain_ref[...]).astype(bf16)

    def expand(at):
        cut = pl.ds(at, TILE)
        gate = dot(left_ref[...], gate_ref[:, cut])
        up = dot(left_ref[...], up_ref[:, cut])
        inner_ref[:, cut] = (jax.nn.gelu(gate, approximate=True) * up).astype(bf16)

    tiles(gate_ref.shape[1] // TILE, expand)

    def contract(at):
        out_ref[at // lanes] = dot(inner_ref[...], down_ref[:, pl.ds(at, TILE)]).astype(bf16)

    tiles(nt * lanes // TILE, contract)


def tied(value, *others):
    return lax.optimization_barrier((value, *others))[0]


def on_device(
    patches,
    perms,
    w_in,
    gain_mix,
    w_qkv,
    w_mix,
    gain_out,
    w_head,
    order,
    w_embed,
    gain_attn,
    w_query,
    w_keyval,
    w_attn,
    gain_mlp,
    w_gate,
    w_up,
    w_down,
):
    rows = patches.shape[0]
    local_w = w_qkv.shape[3]
    where = lax.axis_index("tensor")
    patch = lax.axis_index("patch")
    core = patch % 2
    even = core == 0
    ids = jnp.stack([core, where]).astype(jnp.int32)

    def halves(x):
        cols = x.shape[1] // 2
        return lax.dynamic_slice_in_dim(x, core * cols, cols, 1)

    w_qkv = w_qkv.transpose(0, 2, 1, 3)
    halved = cut(ids, w_mix, w_head)
    own_weights = [halved[0], None]
    side_weights = [lax.ppermute(halved[0], "tensor", ACROSS), None]
    field = patches
    logdet = 0.0
    for blk in range(BLOCKS):
        hidden, query, keyval, other = pre(blk, ids, field, perms, w_in, gain_mix, w_qkv)
        hd = local_w // 2
        got = over(other, CORE)
        query = jnp.concatenate([query, got[:, :hd]], axis=0)
        keyval = jnp.concatenate([keyval, got[:, hd:]], axis=0)
        own_w = spread(tied(own_weights[blk], keyval), side_weights[blk])
        pieces = gather_chips(keyval)
        state = attend(query, pieces[:4], [], False)
        (out,) = attend(query, pieces[4:], state, True)
        back = over(out[rows:], CORE)
        front = out[:rows]
        mixed = jnp.concatenate(
            [jnp.where(even, front, back), jnp.where(even, back, front)], axis=1
        )
        mixed = tied(mixed, own_w)
        oth_w = over(tied(own_w, mixed), CORE)
        mixed = exchange(jnp.broadcast_to(mixed, (NT,) + mixed.shape))
        if blk + 1 < BLOCKS:
            own_weights[blk + 1] = tied(halved[blk + 1], mixed)
            side_weights[blk + 1] = lax.ppermute(own_weights[blk + 1], "tensor", ACROSS)
        else:
            attn_half = tied(halves(w_attn), mixed)
            attn_side = lax.ppermute(attn_half, "tensor", ACROSS)
        field, det = post(
            blk, ids, mixed, own_w, oth_w, hidden, field, perms, gain_out,
            bf16 if blk == BLOCKS - 1 else f32,
        )
        logdet = logdet + det[:, 0]
    embed_part = jnp.dot(field, w_embed, preferred_element_type=f32).astype(bf16)
    embedded = exchange(jnp.broadcast_to(embed_part, (NT,) + embed_part.shape))
    query_dec, keyval = call(
        enter_kernel,
        [((rows, DH), bf16), ((rows, 2 * DH), bf16)],
        embedded,
        gain_attn[None],
        w_query,
        w_keyval,
        flops=1 << 30,
    )
    own_a = spread(tied(attn_half, keyval), attn_side)
    pieces = gather_chips(keyval)
    pieces = pieces + [over(x, CORE) for x in pieces]

    y, x = patch // 4, (patch // 2) % 2
    owners = [core, patch]
    for dc in (0, 1):
        for dy, dx in ((0, 0), (-1, 0), (1, 0), (0, 1), (-1, 1), (1, 1), (2, 0), (2, 1)):
            owners.append((((y + dy) % 4) * 2 + (x + dx) % 2) * 2 + (core + dc) % 2)
    (attended,) = call(
        causal_kernel,
        [((rows, DH), bf16)],
        jnp.stack(owners).astype(jnp.int32),
        query_dec,
        order[:, None],
        order[None],
        *pieces,
        scratch=[pltpu.VMEM((len(pieces), rows, rows), f32)],
        smem=1,
        flops=2 << 30,
    )
    attended = tied(attended, own_a)
    oth_a = over(tied(own_a, attended), CORE)
    att = exchange(jnp.broadcast_to(attended, (NT,) + attended.shape))
    cols = w_attn.shape[1] // NT
    down, resid = call(
        mlp_kernel,
        [((NT, rows, cols), bf16), ((rows, cols), f32)],
        ids,
        att,
        embedded,
        own_a.reshape((NT,) + own_a.shape[2:]),
        oth_a.reshape((NT,) + oth_a.shape[2:]),
        gain_mlp[None],
        w_gate,
        w_up,
        w_down,
        scratch=[
            pltpu.VMEM((rows, w_attn.shape[1]), f32),
            pltpu.VMEM((rows, w_gate.shape[1]), bf16),
            pltpu.VMEM((rows, w_attn.shape[1]), bf16),
        ],
        smem=1,
        flops=6 << 30,
    )
    decoded = (jnp.sum(exchange(down).astype(f32), axis=0) + resid).astype(bf16)
    return (decoded, logdet)


def solution(mesh):
    return jax.shard_map(
        on_device,
        mesh=mesh,
        in_specs=(
            P("patch", None),
            P(),
            P(),
            P(),
            P(None, None, None, "tensor"),
            P(None, "tensor", None),
            P(),
            P(None, "tensor", None),
            P("patch"),
            P(None, "tensor"),
            P(),
            P(None, "tensor"),
            P(),
            P("tensor", None),
            P(),
            P(None, "tensor"),
            P(None, "tensor"),
            P("tensor", None),
        ),
        out_specs=(P("patch", "tensor"), P("patch")),
        check_vma=False,
    )
```

```python
import functools

import jax
import jax.numpy as jnp
from jax import lax
from jax.experimental import pallas as pl
from jax.experimental.pallas import tpu as pltpu
from jax.sharding import PartitionSpec as P


BLOCKS = 2
DH = 256
NP = 16
NT = 8


bf16 = jnp.bfloat16
f32 = jnp.float32


def normed(value, gain):
    return value * lax.rsqrt(jnp.mean(value * value, axis=-1, keepdims=True) + 1e-06) * gain


CORE = [(i, i ^ 1) for i in range(NP)]


def hop(dy, dx):
    def to(i):
        y, x, c = i // 4, (i // 2) % 2, i % 2
        return ((y + dy) % 4 * 2 + (x + dx) % 2) * 2 + c

    return [(i, to(i)) for i in range(NP)]


UP, DOWN, SIDE = hop(1, 0), hop(-1, 0), hop(0, 1)


def over(value, pairs):
    return lax.ppermute(value, "patch", pairs)


def gather_chips(own):
    half = own.shape[0] // 2
    up = over(own, UP)
    down = over(own, DOWN)
    side = over(own, SIDE)
    side_up = over(side, UP)
    side_down = over(down, SIDE)
    far_a = over(up[:half], UP)
    far_b = over(down[half:], DOWN)
    far = jnp.concatenate([far_a, far_b], 0)
    side_far = over(far, SIDE)
    return [own, up, down, side, side_up, side_down, far, side_far]


def exchange(parts):
    return lax.all_to_all(parts, "tensor", 0, 0)


ACROSS = [(i, i ^ 1) for i in range(NT)]
RISE = [(i, (i + 2) % NT) for i in range(NT)]
FALL = [(i, (i - 2) % NT) for i in range(NT)]


def spread(own, side):
    pair = jnp.stack([own, side])
    below = lax.ppermute(pair, "tensor", RISE)
    above = lax.ppermute(pair, "tensor", FALL)
    far_a = lax.ppermute(below[:1], "tensor", RISE)
    far_b = lax.ppermute(above[1:], "tensor", FALL)
    return [pair, below, above, far_a, far_b]


RING = [(0, 0), (0, 1), (-1, 0), (-1, 1), (1, 0), (1, 1), (2, 0), (2, 1)]


def ring_order(where):
    z, x = where // 2, where % 2
    return [(z + dz + NT // 2) % (NT // 2) * 2 + (x + dx) % 2 for dz, dx in RING]


def split2(x):
    a = x.astype(bf16)
    b = (x - a.astype(f32)).astype(bf16)
    return a, b


def split3(x):
    a = x.astype(bf16)
    r = x - a.astype(f32)
    b = r.astype(bf16)
    c = (r - b.astype(f32)).astype(bf16)
    return a, b, c


def select(x, one_hot, dims=(1, 0)):
    dims = (((dims[0],), (dims[1],)), ((), ()))
    a, b, c = (
        lax.dot_general(p, one_hot, dims, preferred_element_type=f32) for p in split3(x)
    )
    return (c + b) + a


def left6(x):
    a, b, c = split3(x)
    return jnp.concatenate([a, a, b, a, b, c], axis=1)


def right6(x):
    a, b, c = split3(x)
    return jnp.concatenate([a, b, a, c, b, a], axis=0)


def left3(x):
    a, b = split2(x)
    return jnp.concatenate([a, a, b], axis=1)


def right3(x):
    a, b = split2(x)
    return jnp.concatenate([a, b, a], axis=0)


def dot(left, right):
    return jnp.dot(left, right, preferred_element_type=f32)


TILE = 256


def tiles(count, body):
    def step(i, carry):
        body(pl.multiple_of(i * TILE, TILE))
        return carry

    lax.fori_loop(0, count, step, 0)


VMEM = pl.BlockSpec(memory_space=pltpu.VMEM)
HBM = pl.BlockSpec(memory_space=pl.ANY)
SMEM = pl.BlockSpec(memory_space=pltpu.SMEM)


def call(body, outs, *args, scratch=(), flops=0, limit=16, smem=0, hbm=0):
    moved = sum(x.size * x.dtype.itemsize for x in args)
    return pl.pallas_call(
        body,
        in_specs=[SMEM] * smem + [VMEM] * (len(args) - smem - hbm) + [HBM] * hbm,
        out_specs=[VMEM] * len(outs),
        out_shape=[jax.ShapeDtypeStruct(*o) for o in outs],
        scratch_shapes=list(scratch),
        compiler_params=pltpu.CompilerParams(vmem_limit_bytes=limit << 20),
        cost_estimate=pl.CostEstimate(flops=flops, bytes_accessed=moved, transcendentals=0),
    )(*args)


def cut_kernel(ids, mix_ref, head_ref, *refs):
    outs, sems = refs[:BLOCKS], refs[BLOCKS]
    copies = []
    for blk, out in enumerate(outs):
        at = 0
        for i, ref in enumerate((mix_ref, head_ref)):
            cols = ref.shape[2] // 2
            source = ref.at[blk, :, pl.ds(pl.multiple_of(ids[0] * cols, 128), cols)]
            copies.append(
                pltpu.make_async_copy(source, out.at[:, at : at + cols], sems.at[blk, i])
            )
            at += cols
    for copy in copies:
        copy.start()
    for copy in copies:
        copy.wait()


def cut(ids, w_mix, w_head):
    shape = (w_mix.shape[1], (w_mix.shape[2] + w_head.shape[2]) // 2)
    return pl.pallas_call(
        cut_kernel,
        in_specs=[SMEM, HBM, HBM],
        out_specs=[VMEM] * BLOCKS,
        out_shape=[jax.ShapeDtypeStruct(shape, f32)] * BLOCKS,
        scratch_shapes=[pltpu.SemaphoreType.DMA((BLOCKS, 2))],
        compiler_params=pltpu.CompilerParams(vmem_limit_bytes=4 << 20),
        name="cut",
    )(ids, w_mix, w_head)


def pre_kernel(
    blk, ids, field_ref, perms_ref, gain_ref, w_in_all, w_all,
    hidden_ref, q_ref, kv_ref, oth_ref, cond_ref, unit_ref, w_in_ref, w_ref, sems,
):
    copy_in = pltpu.make_async_copy(w_in_all.at[blk], w_in_ref, sems.at[0])
    copy_qkv = pltpu.make_async_copy(w_all.at[blk], w_ref, sems.at[1])
    copy_in.start()
    copy_qkv.start()
    even = ids[0] == 0
    half, full = w_in_ref.shape
    width = field_ref.shape[1]
    hd = w_ref.shape[2] // 2
    row = lax.broadcasted_iota(jnp.int32, (width, half), 0)
    take = jnp.where(row == perms_ref[blk : blk + 1, :half], 1.0, 0.0).astype(bf16)
    cond_ref[...] = left6(select(field_ref[...], take))
    copy_in.wait()

    def column(at):
        cut = pl.ds(at, TILE)
        hidden_ref[:, cut] = dot(cond_ref[...], right6(w_in_ref[:, cut]))

    tiles(full // TILE, column)
    unit_ref[...] = left6(normed(hidden_ref[...], gain_ref[blk : blk + 1]))
    copy_qkv.wait()
    qk = jnp.concatenate([w_ref[0], w_ref[1]], axis=1)
    qk = dot(unit_ref[...], right6(qk))
    v = dot(unit_ref[...], right6(w_ref[2]))
    q, k = qk[:, : 2 * hd], qk[:, 2 * hd :]

    def pick(x, first):
        return jnp.where(first, x[:, :hd], x[:, hd:])

    q_ref[...] = pick(q, even)
    kv_ref[...] = jnp.concatenate([pick(k, even), pick(v, even)], axis=1)
    odd = jnp.logical_not(even)
    oth_ref[...] = jnp.concatenate([pick(q, odd), pick(k, odd), pick(v, odd)], axis=1)


def pre(blk, ids, field, perms, w_in, gain, w_qkv):
    rows, (half, full) = field.shape[0], w_in.shape[1:]
    hd = w_qkv.shape[3] // 2
    return call(
        functools.partial(pre_kernel, blk),
        [((rows, full), f32), ((rows, hd), f32), ((rows, 2 * hd), f32), ((rows, 3 * hd), f32)],
        ids,
        field,
        perms,
        gain,
        w_in,
        w_qkv,
        scratch=[
            pltpu.VMEM((rows, 6 * half), bf16),
            pltpu.VMEM((rows, 6 * full), bf16),
            pltpu.VMEM(w_in.shape[1:], f32),
            pltpu.VMEM(w_qkv.shape[1:], f32),
            pltpu.SemaphoreType.DMA((2,)),
        ],
        smem=1,
        hbm=2,
        flops=3 << 30,
    )


def attend_kernel(count, first, last, q_ref, *refs):
    kv_refs, refs = refs[:count], refs[count:]
    if not first:
        (acc0_ref, stat0_ref), refs = refs[:2], refs[2:]
    rows, hd = q_ref.shape
    s_ref = refs[-1]
    block = s_ref.shape[1]

    def some_rows(i, carry):
        at = pl.ds(pl.multiple_of(i * block, block), block)
        q1, q2, q3 = split3(q_ref[at, :] * (hd ** (-0.5)))
        qs = jnp.concatenate([q1, q1, q2, q1, q2, q3], axis=1)
        top = None if first else stat0_ref[at, :1]
        for j, kv_ref in enumerate(kv_refs):
            k1, k2, k3 = split3(kv_ref[:, :hd])
            ks = jnp.concatenate([k1, k2, k1, k3, k2, k1], axis=1)
            s = lax.dot_general(qs, ks, (((1,), (1,)), ((), ())), preferred_element_type=f32)
            s_ref[j] = s
            m = jnp.max(s, axis=1, keepdims=True)
            top = m if top is None else jnp.maximum(top, m)
        total = acc = None
        if not first:
            factor = jnp.exp(stat0_ref[at, :1] - top)
            total, acc = stat0_ref[at, hd : hd + 1] * factor, acc0_ref[at, :] * factor
        for j, kv_ref in enumerate(kv_refs):
            p = jnp.exp(s_ref[j] - top)
            t = jnp.sum(p, axis=1, keepdims=True)
            v1, v2, v3 = split3(kv_ref[:, hd:])
            p1, p2 = split2(p)
            a = dot(p1, jnp.concatenate([v1, v2, v3], axis=1))
            b = dot(p2, jnp.concatenate([v1, v2], axis=1))
            a = a[:, :hd] + (a[:, hd : 2 * hd] + b[:, :hd]) + (a[:, 2 * hd :] + b[:, hd:])
            total = t if total is None else total + t
            acc = a if acc is None else acc + a
        if last:
            refs[0][at, :] = acc / total
        else:
            refs[0][at, :] = acc
            refs[1][at, :] = jnp.concatenate(
                [jnp.broadcast_to(top, (block, hd)), jnp.broadcast_to(total, (block, hd))], axis=1
            )
        return carry

    lax.fori_loop(0, rows // block, some_rows, 0)


def attend(query, pieces, state, last):
    rows, hd = query.shape
    keys = pieces[0].shape[0]
    count = len(pieces)
    outs = [((rows, hd), f32)] if last else [((rows, hd), f32), ((rows, 2 * hd), f32)]
    return call(
        functools.partial(attend_kernel, count, not state, last),
        outs,
        query,
        *pieces,
        *state,
        scratch=[pltpu.VMEM((count, 256, keys), f32)],
        flops=count << 30,
    )


def post_kernel(
    blk, ids, m_ref, hidden_ref, field_ref, perms_ref, gain_ref, *refs,
):
    own_refs, oth_refs, (out_ref, det_ref, left_ref, sum_ref) = refs[:5], refs[5:10], refs[10:]
    even = ids[0] == 0
    _, _, lanes = m_ref.shape
    full, width = hidden_ref.shape[1], field_ref.shape[1]
    half, mid = width // 2, full // 2
    order = ring_order(ids[1])

    def right(refs, cut):
        parts = [ref[j, :, cut] for ref in refs for j in range(ref.shape[0])]
        return right3(jnp.concatenate(parts, axis=0))

    left_ref[...] = left3(jnp.concatenate([m_ref[t] for t in order], axis=1))

    def column(at):
        cut = pl.ds(at, TILE)
        a = dot(left_ref[...], right(own_refs, cut))
        b = dot(left_ref[...], right(oth_refs, cut))
        sum_ref[:, cut] = hidden_ref[:, cut] + jnp.where(even, a, b)
        cut = pl.ds(pl.multiple_of(at + mid, TILE), TILE)
        sum_ref[:, cut] = hidden_ref[:, cut] + jnp.where(even, b, a)

    tiles(mid // TILE, column)
    sum_ref[...] = normed(sum_ref[...], gain_ref[blk : blk + 1])
    parts = [sum_ref[:, pl.ds(pl.multiple_of(t * lanes, lanes), lanes)] for t in order]
    left_ref[...] = left3(jnp.concatenate(parts, axis=1))
    a = dot(left_ref[...], right(own_refs, slice(mid, mid + half)))
    b = dot(left_ref[...], right(oth_refs, slice(mid, mid + half)))
    log_scale, shift = jnp.tanh(jnp.where(even, a, b)), jnp.where(even, b, a)
    det_ref[...] = jnp.sum(log_scale, axis=1, keepdims=True)
    row = lax.broadcasted_iota(jnp.int32, (width, half), 0)
    put = jnp.where(row == perms_ref[blk : blk + 1, half:], 1.0, 0.0).astype(bf16)
    field = field_ref[...] * jnp.exp(select(log_scale, put, (1, 1))) + select(shift, put, (1, 1))
    out_ref[...] = field.astype(out_ref.dtype)


def post(blk, ids, mixed, own, oth, hidden, field, perms, gain, kind):
    rows, width = field.shape
    full = hidden.shape[1]
    return call(
        functools.partial(post_kernel, blk),
        [((rows, width), kind), ((rows, 1), f32)],
        ids,
        mixed,
        hidden,
        field,
        perms,
        gain,
        *own,
        *oth,
        scratch=[pltpu.VMEM((rows, 3 * full), bf16), pltpu.VMEM((rows, full), f32)],
        smem=1,
        flops=6 << 30,
    )


def enter_kernel(emb_ref, gain_ref, w_query_ref, w_keyval_ref, q_ref, kv_ref):
    start = jnp.concatenate([emb_ref[t] for t in range(emb_ref.shape[0])], axis=1)
    unit = normed(start.astype(f32), gain_ref[...]).astype(bf16)
    kv_ref[...] = jnp.dot(unit, w_keyval_ref[...], preferred_element_type=f32).astype(bf16)
    q_ref[...] = jnp.dot(unit, w_query_ref[...], preferred_element_type=f32).astype(bf16)


def causal_kernel(ids, q_ref, order_ref, order_row_ref, w_ref, *refs):
    kv_refs, o_ref, s_ref = refs[:-2], refs[-2], refs[-1]
    dh = q_ref.shape[1]
    patch = ids[1]
    own = order_row_ref[...] <= order_ref[...]
    top = None
    for j, kv_ref in enumerate(kv_refs):
        owner = ids[2 + j]
        s = lax.dot_general(
            q_ref[...], kv_ref[:, :dh], (((1,), (1,)), ((), ())), preferred_element_type=f32
        ) * (dh ** (-0.5))
        if j == 0:
            s = jnp.where(own, s, -jnp.inf)
        else:
            s = jnp.where(owner < patch, s, -jnp.inf)
        s_ref[j] = s
        m = jnp.max(s, axis=1, keepdims=True)
        top = m if top is None else jnp.maximum(top, m)
    total = acc = None
    for j, kv_ref in enumerate(kv_refs):
        p = jnp.exp(s_ref[j] - top)
        t = jnp.sum(p, axis=1, keepdims=True)
        a = jnp.dot(p.astype(bf16), kv_ref[:, dh:], preferred_element_type=f32)
        total = t if total is None else total + t
        acc = a if acc is None else acc + a
    attended = (acc / total).astype(bf16)
    for at in range(0, w_ref.shape[1], 512):
        o_ref[:, at : at + 512] = dot(attended, w_ref[:, at : at + 512]).astype(bf16)


def resid_kernel(ids, parts_ref, emb_ref, gain_ref, resid_ref, unit_ref):
    nt, part, _ = parts_ref.shape
    at = pl.ds(pl.multiple_of(ids[1] * part, part), part)
    start = jnp.concatenate([emb_ref[t, at, :] for t in range(nt)], axis=1).astype(f32)
    resid = start + sum(parts_ref[t].astype(f32) for t in range(nt))
    resid_ref[...] = resid
    unit = normed(resid, gain_ref[...]).astype(bf16)
    for t in range(nt):
        unit_ref[t] = unit


def mlp_kernel(
    ids, unit_ref, resid_ref, gate_all, up_all, down_all,
    out_ref, gate_ref, up_ref, down_ref, inner_ref, sum_ref, sems,
):
    model, hidden = gate_ref.shape
    lanes, part = out_ref.shape[2], resid_ref.shape[0]
    count = hidden // TILE
    copies = []
    for i in range(count):
        cut = slice(i * TILE, (i + 1) * TILE)
        copies.append(
            [
                pltpu.make_async_copy(gate_all.at[:, cut], gate_ref.at[:, cut], sems.at[0, i]),
                pltpu.make_async_copy(up_all.at[:, cut], up_ref.at[:, cut], sems.at[1, i]),
            ]
        )
    for i in range(count):
        cut = slice(i * model // count, (i + 1) * model // count)
        copies.append(
            [pltpu.make_async_copy(down_all.at[:, cut], down_ref.at[:, cut], sems.at[2, i])]
        )
    for group in copies:
        for copy in group:
            copy.start()
    unit = unit_ref[...].reshape(-1, model)
    for i in range(count):
        for copy in copies[i]:
            copy.wait()
        cut = slice(i * TILE, (i + 1) * TILE)
        gate = dot(unit, gate_ref[:, cut])
        up = dot(unit, up_ref[:, cut])
        inner_ref[:, cut] = (jax.nn.gelu(gate, approximate=True) * up).astype(bf16)
    mine = pl.ds(pl.multiple_of(ids[1] * part, part), part)
    for i in range(count):
        copies[count + i][0].wait()
        for at in range(i * model // count, (i + 1) * model // count, lanes):
            cut = slice(at, at + lanes)
            sum_ref[...] = dot(inner_ref[...], down_ref[:, cut])
            sum_ref[mine, :] = sum_ref[mine, :] + resid_ref[:, cut]
            out_ref[at // lanes] = sum_ref[...].astype(bf16)


def tied(value, *others):
    return lax.optimization_barrier((value, *others))[0]


def on_device(
    patches,
    perms,
    w_in,
    gain_mix,
    w_qkv,
    w_mix,
    gain_out,
    w_head,
    order,
    w_embed,
    gain_attn,
    w_query,
    w_keyval,
    w_attn,
    gain_mlp,
    w_gate,
    w_up,
    w_down,
):
    rows = patches.shape[0]
    local_w = w_qkv.shape[3]
    where = lax.axis_index("tensor")
    patch = lax.axis_index("patch")
    core = patch % 2
    even = core == 0
    ids = jnp.stack([core, where]).astype(jnp.int32)

    w_qkv = w_qkv.transpose(0, 2, 1, 3)
    halved = cut(ids, w_mix, w_head)
    own_weights = [halved[0], None]
    side_weights = [lax.ppermute(halved[0], "tensor", ACROSS), None]
    field = patches
    logdet = 0.0
    for blk in range(BLOCKS):
        hidden, query, keyval, other = pre(blk, ids, field, perms, w_in, gain_mix, w_qkv)
        hd = local_w // 2
        got = over(other, CORE)
        query = jnp.concatenate([query, got[:, :hd]], axis=0)
        keyval = jnp.concatenate([keyval, got[:, hd:]], axis=0)
        own_w = spread(tied(own_weights[blk], keyval), side_weights[blk])
        oth_w = [over(w, CORE) for w in own_w]
        pieces = gather_chips(keyval)
        state = attend(query, pieces[:4], [], False)
        state = attend(query, pieces[4:7], state, False)
        (out,) = attend(tied(query, own_w[1], own_w[2]), pieces[7:], state, True)
        back = over(out[rows:], CORE)
        front = out[:rows]
        mixed = jnp.concatenate(
            [jnp.where(even, front, back), jnp.where(even, back, front)], axis=1
        )
        mixed = exchange(jnp.broadcast_to(mixed, (NT,) + mixed.shape))
        if blk + 1 < BLOCKS:
            own_weights[blk + 1] = tied(halved[blk + 1], mixed)
            side_weights[blk + 1] = lax.ppermute(own_weights[blk + 1], "tensor", ACROSS)
        field, det = post(
            blk, ids, mixed, own_w, oth_w, hidden, field, perms, gain_out,
            bf16 if blk == BLOCKS - 1 else f32,
        )
        logdet = logdet + det[:, 0]
    embed_part = jnp.dot(field, w_embed, preferred_element_type=f32).astype(bf16)
    embedded = exchange(jnp.broadcast_to(embed_part, (NT,) + embed_part.shape))
    query_dec, keyval = call(
        enter_kernel,
        [((rows, DH), bf16), ((rows, 2 * DH), bf16)],
        embedded,
        gain_attn[None],
        w_query,
        w_keyval,
        flops=1 << 30,
    )
    pieces = gather_chips(keyval)
    pieces = pieces + [over(x, CORE) for x in pieces]

    y, x = patch // 4, (patch // 2) % 2
    owners = [core, patch]
    for dc in (0, 1):
        for dy, dx in ((0, 0), (-1, 0), (1, 0), (0, 1), (-1, 1), (1, 1), (2, 0), (2, 1)):
            owners.append((((y + dy) % 4) * 2 + (x + dx) % 2) * 2 + (core + dc) % 2)
    model_w = w_attn.shape[1]
    (partial_value,) = call(
        causal_kernel,
        [((rows, model_w), bf16)],
        jnp.stack(owners).astype(jnp.int32),
        query_dec,
        order[:, None],
        order[None],
        w_attn,
        *pieces,
        scratch=[pltpu.VMEM((len(pieces), rows, rows), f32)],
        smem=1,
        flops=2 << 30,
    )
    part, cols = rows // NT, model_w // NT
    resid, unit = call(
        resid_kernel,
        [((part, model_w), f32), ((NT, part, model_w), bf16)],
        ids,
        exchange(partial_value.reshape(NT, part, model_w)),
        embedded,
        gain_mlp[None],
        smem=1,
    )
    (down,) = call(
        mlp_kernel,
        [((NT, rows, cols), bf16)],
        ids,
        exchange(unit),
        resid,
        w_gate,
        w_up,
        w_down,
        scratch=[
            pltpu.VMEM(w_gate.shape, bf16),
            pltpu.VMEM(w_up.shape, bf16),
            pltpu.VMEM(w_down.shape, bf16),
            pltpu.VMEM((rows, w_gate.shape[1]), bf16),
            pltpu.VMEM((rows, cols), f32),
            pltpu.SemaphoreType.DMA((3, w_gate.shape[1] // TILE)),
        ],
        smem=1,
        hbm=3,
        limit=24,
        flops=4 << 30,
    )
    decoded = jnp.sum(exchange(down).astype(f32), axis=0).astype(bf16)
    return (decoded, logdet)


def solution(mesh):
    return jax.shard_map(
        on_device,
        mesh=mesh,
        in_specs=(
            P("patch", None),
            P(),
            P(),
            P(),
            P(None, None, None, "tensor"),
            P(None, "tensor", None),
            P(),
            P(None, "tensor", None),
            P("patch"),
            P(None, "tensor"),
            P(),
            P(None, "tensor"),
            P(),
            P("tensor", None),
            P(),
            P(None, "tensor"),
            P(None, "tensor"),
            P("tensor", None),
        ),
        out_specs=(P("patch", "tensor"), P("patch")),
        check_vma=False,
    )
```

```python
import functools

import jax
import jax.numpy as jnp
from jax import lax
from jax.experimental import pallas as pl
from jax.experimental.pallas import tpu as pltpu
from jax.sharding import PartitionSpec as P


BLOCKS = 2
DH = 256
NP = 16
NT = 8


bf16 = jnp.bfloat16
f32 = jnp.float32


def normed(value, gain):
    return value * lax.rsqrt(jnp.mean(value * value, axis=-1, keepdims=True) + 1e-06) * gain


CORE = [(i, i ^ 1) for i in range(NP)]


def hop(dy, dx):
    def to(i):
        y, x, c = i // 4, (i // 2) % 2, i % 2
        return ((y + dy) % 4 * 2 + (x + dx) % 2) * 2 + c

    return [(i, to(i)) for i in range(NP)]


UP, DOWN, SIDE = hop(1, 0), hop(-1, 0), hop(0, 1)


def over(value, pairs):
    return lax.ppermute(value, "patch", pairs)


def gather_chips(own):
    half = own.shape[0] // 2
    up = over(own, UP)
    down = over(own, DOWN)
    side = over(own, SIDE)
    side_up = over(side, UP)
    side_down = over(down, SIDE)
    far_a = over(up[:half], UP)
    far_b = over(down[half:], DOWN)
    far = jnp.concatenate([far_a, far_b], 0)
    side_far = over(far, SIDE)
    return [own, up, down, side, side_up, side_down, far, side_far]


def exchange(parts):
    return lax.all_to_all(parts, "tensor", 0, 0)


ACROSS = [(i, i ^ 1) for i in range(NT)]
RISE = [(i, (i + 2) % NT) for i in range(NT)]
FALL = [(i, (i - 2) % NT) for i in range(NT)]


def spread(own, side):
    rise, fall = (functools.partial(lax.ppermute, axis_name="tensor", perm=p) for p in (RISE, FALL))
    below, above = rise(own), fall(side)
    below_side, above_own = rise(side), fall(own)
    return [own, side, below, below_side, above_own, above, rise(below), fall(above)]


RING = [(0, 0), (0, 1), (-1, 0), (-1, 1), (1, 0), (1, 1), (2, 0), (2, 1)]


def ring_order(where):
    z, x = where // 2, where % 2
    return [(z + dz + NT // 2) % (NT // 2) * 2 + (x + dx) % 2 for dz, dx in RING]


def split2(x):
    a = x.astype(bf16)
    b = (x - a.astype(f32)).astype(bf16)
    return a, b


def split3(x):
    a = x.astype(bf16)
    r = x - a.astype(f32)
    b = r.astype(bf16)
    c = (r - b.astype(f32)).astype(bf16)
    return a, b, c


def select(x, one_hot, dims=(1, 0)):
    dims = (((dims[0],), (dims[1],)), ((), ()))
    a, b, c = (
        lax.dot_general(p, one_hot, dims, preferred_element_type=f32) for p in split3(x)
    )
    return (c + b) + a


def left6(x):
    a, b, c = split3(x)
    return jnp.concatenate([a, a, b, a, b, c], axis=1)


def right6(x):
    a, b, c = split3(x)
    return jnp.concatenate([a, b, a, c, b, a], axis=0)


def left3(x):
    a, b = split2(x)
    return jnp.concatenate([a, a, b], axis=1)


def dot(left, right):
    return jnp.dot(left, right, preferred_element_type=f32)


TILE = 256


def tiles(count, body):
    def step(i, carry):
        body(pl.multiple_of(i * TILE, TILE))
        return carry

    lax.fori_loop(0, count, step, 0)


VMEM = pl.BlockSpec(memory_space=pltpu.VMEM)
HBM = pl.BlockSpec(memory_space=pltpu.HBM)
ANY = pl.BlockSpec(memory_space=pl.ANY)
SMEM = pl.BlockSpec(memory_space=pltpu.SMEM)


def call(body, outs, *args, scratch=(), flops=0, limit=16, smem=0, left=0, kept=HBM):
    moved = sum(x.size * x.dtype.itemsize for x in args)
    return pl.pallas_call(
        body,
        in_specs=[SMEM] * smem + [VMEM] * (len(args) - smem - left) + [kept] * left,
        out_specs=[VMEM] * len(outs),
        out_shape=[jax.ShapeDtypeStruct(*o) for o in outs],
        scratch_shapes=list(scratch),
        compiler_params=pltpu.CompilerParams(vmem_limit_bytes=limit << 20),
        cost_estimate=pl.CostEstimate(flops=flops, bytes_accessed=moved, transcendentals=0),
    )(*args)


def cut_kernel(ids, mix_ref, head_ref, *refs):
    outs, (buf_ref, sems) = refs[:BLOCKS], refs[BLOCKS:]
    rows = buf_ref.shape[1]
    copies = []
    for blk in range(BLOCKS):
        at = 0
        for i, ref in enumerate((mix_ref, head_ref)):
            cols = ref.shape[2] // 2
            source = ref.at[blk, :, pl.ds(pl.multiple_of(ids[0] * cols, 128), cols)]
            copies.append(
                pltpu.make_async_copy(source, buf_ref.at[blk, :, at : at + cols], sems.at[blk, i])
            )
            at += cols
    for copy in copies:
        copy.start()
    for blk, out in enumerate(outs):
        copies[2 * blk].wait()
        copies[2 * blk + 1].wait()
        high, low = split2(buf_ref[blk])
        out[:rows, :] = high
        out[rows:, :] = low


def cut(ids, w_mix, w_head):
    rows, cols = w_mix.shape[1], (w_mix.shape[2] + w_head.shape[2]) // 2
    return pl.pallas_call(
        cut_kernel,
        in_specs=[SMEM, HBM, HBM],
        out_specs=[VMEM] * BLOCKS,
        out_shape=[jax.ShapeDtypeStruct((2 * rows, cols), bf16)] * BLOCKS,
        scratch_shapes=[
            pltpu.VMEM((BLOCKS, rows, cols), f32),
            pltpu.SemaphoreType.DMA((BLOCKS, 2)),
        ],
        compiler_params=pltpu.CompilerParams(vmem_limit_bytes=8 << 20),
        name="cut",
    )(ids, w_mix, w_head)


def pre_kernel(
    ids, field_ref, perms_ref, gain_ref, w_in_all, w_all,
    hidden_ref, q_ref, kv_ref, oth_ref, cond_ref, unit_ref, w_in_ref, w_ref, sems,
):
    blk = ids[2]
    copy_in = pltpu.make_async_copy(w_in_all.at[blk], w_in_ref, sems.at[0])
    copy_qkv = pltpu.make_async_copy(w_all.at[blk], w_ref, sems.at[1])
    copy_in.start()
    copy_qkv.start()
    even = ids[0] == 0
    half, full = w_in_ref.shape
    width = field_ref.shape[1]
    hd = w_ref.shape[2] // 2
    row = lax.broadcasted_iota(jnp.int32, (width, half), 0)
    take = jnp.where(row == perms_ref[pl.ds(blk, 1), :half], 1.0, 0.0).astype(bf16)
    cond_ref[...] = left6(select(field_ref[...], take))
    copy_in.wait()

    def column(at):
        cut = pl.ds(at, TILE)
        hidden_ref[:, cut] = dot(cond_ref[...], right6(w_in_ref[:, cut]))

    tiles(full // TILE, column)
    unit_ref[...] = left6(normed(hidden_ref[...], gain_ref[pl.ds(blk, 1), :]))
    copy_qkv.wait()
    qk = jnp.concatenate([w_ref[0], w_ref[1]], axis=1)
    qk = dot(unit_ref[...], right6(qk))
    v = dot(unit_ref[...], right6(w_ref[2]))
    q, k = qk[:, : 2 * hd], qk[:, 2 * hd :]

    def pick(x, first):
        return jnp.where(first, x[:, :hd], x[:, hd:])

    q_ref[...] = pick(q, even)
    kv_ref[...] = jnp.concatenate([pick(k, even), pick(v, even)], axis=1)
    odd = jnp.logical_not(even)
    oth_ref[...] = jnp.concatenate([pick(q, odd), pick(k, odd), pick(v, odd)], axis=1)


def pre(ids, field, perms, w_in, gain, w_qkv):
    rows, (half, full) = field.shape[0], w_in.shape[1:]
    hd = w_qkv.shape[3] // 2
    return call(
        pre_kernel,
        [((rows, full), f32), ((rows, hd), f32), ((rows, 2 * hd), f32), ((rows, 3 * hd), f32)],
        ids,
        field,
        perms,
        gain,
        w_in,
        w_qkv,
        scratch=[
            pltpu.VMEM((rows, 6 * half), bf16),
            pltpu.VMEM((rows, 6 * full), bf16),
            pltpu.VMEM(w_in.shape[1:], f32),
            pltpu.VMEM(w_qkv.shape[1:], f32),
            pltpu.SemaphoreType.DMA((2,)),
        ],
        smem=1,
        left=2,
        flops=3 << 30,
    )


def attend_kernel(count, first, last, q_ref, *refs):
    kv_refs, refs = refs[:count], refs[count:]
    if not first:
        (acc0_ref, stat0_ref), refs = refs[:2], refs[2:]
    rows, hd = q_ref.shape
    s_ref = refs[-1]
    block = s_ref.shape[1]

    def some_rows(i, carry):
        at = pl.ds(pl.multiple_of(i * block, block), block)
        q1, q2, q3 = split3(q_ref[at, :] * (hd ** (-0.5)))
        qs = jnp.concatenate([q1, q1, q2, q1, q2, q3], axis=1)
        top = None if first else stat0_ref[at, :1]
        for j, kv_ref in enumerate(kv_refs):
            k1, k2, k3 = split3(kv_ref[:, :hd])
            ks = jnp.concatenate([k1, k2, k1, k3, k2, k1], axis=1)
            s = lax.dot_general(qs, ks, (((1,), (1,)), ((), ())), preferred_element_type=f32)
            s_ref[j] = s
            m = jnp.max(s, axis=1, keepdims=True)
            top = m if top is None else jnp.maximum(top, m)
        total = acc = None
        if not first:
            factor = jnp.exp(stat0_ref[at, :1] - top)
            total, acc = stat0_ref[at, hd : hd + 1] * factor, acc0_ref[at, :] * factor
        for j, kv_ref in enumerate(kv_refs):
            p = jnp.exp(s_ref[j] - top)
            t = jnp.sum(p, axis=1, keepdims=True)
            v1, v2, v3 = split3(kv_ref[:, hd:])
            p1, p2 = split2(p)
            a = dot(p1, jnp.concatenate([v1, v2, v3], axis=1))
            b = dot(p2, jnp.concatenate([v1, v2], axis=1))
            a = a[:, :hd] + (a[:, hd : 2 * hd] + b[:, :hd]) + (a[:, 2 * hd :] + b[:, hd:])
            total = t if total is None else total + t
            acc = a if acc is None else acc + a
        if last:
            refs[0][at, :] = acc / total
        else:
            refs[0][at, :] = acc
            refs[1][at, :] = jnp.concatenate(
                [jnp.broadcast_to(top, (block, hd)), jnp.broadcast_to(total, (block, hd))], axis=1
            )
        return carry

    lax.fori_loop(0, rows // block, some_rows, 0)


def attend(query, pieces, state, last):
    rows, hd = query.shape
    keys = pieces[0].shape[0]
    count = len(pieces)
    outs = [((rows, hd), f32)] if last else [((rows, hd), f32), ((rows, 2 * hd), f32)]
    return call(
        functools.partial(attend_kernel, count, not state, last),
        outs,
        query,
        *pieces,
        *state,
        scratch=[pltpu.VMEM((count, 256, keys), f32)],
        flops=count << 30,
    )


def post_kernel(ids, m_ref, hidden_ref, field_ref, perms_ref, gain_ref, *refs):
    own_refs, far_refs, refs = refs[:NT], refs[NT : 2 * NT], refs[2 * NT :]
    out_ref, det_ref, left_ref, sum_ref, oth_ref, sems = refs
    copies = [
        pltpu.make_async_copy(far, oth_ref.at[j], sems.at[j]) for j, far in enumerate(far_refs)
    ]
    for copy in copies:
        copy.start()
    blk, even = ids[2], ids[0] == 0
    nt, _, lanes = m_ref.shape
    full, width = hidden_ref.shape[1], field_ref.shape[1]
    half, mid = width // 2, full // 2
    order = ring_order(ids[1])
    cuts = [(at, TILE) for at in range(0, mid, TILE)] + [(mid, half)]

    def product(side, k):
        cut = slice(cuts[k][0], sum(cuts[k]))
        high, low = (
            [side[j][i * lanes : (i + 1) * lanes, cut] for j in range(nt)] for i in range(2)
        )
        return dot(left_ref[...], jnp.concatenate(high + low + high, axis=0))

    oth_refs = [oth_ref.at[j] for j in range(nt)]
    left_ref[...] = left3(jnp.concatenate([m_ref[t] for t in order], axis=1))
    near = [product(own_refs, k) for k in range(len(cuts) - 1)]
    for copy in copies:
        copy.wait()
    for k, (at, cols) in enumerate(cuts[:-1]):
        far = product(oth_refs, k)
        cut = slice(at, at + cols)
        sum_ref[:, cut] = hidden_ref[:, cut] + jnp.where(even, near[k], far)
        cut = slice(at + mid, at + mid + cols)
        sum_ref[:, cut] = hidden_ref[:, cut] + jnp.where(even, far, near[k])
    sum_ref[...] = normed(sum_ref[...], gain_ref[pl.ds(blk, 1), :])
    parts = [sum_ref[:, pl.ds(pl.multiple_of(t * lanes, lanes), lanes)] for t in order]
    left_ref[...] = left3(jnp.concatenate(parts, axis=1))
    near, far = product(own_refs, len(cuts) - 1), product(oth_refs, len(cuts) - 1)
    raw, shift = jnp.where(even, near, far), jnp.where(even, far, near)
    log_scale = jnp.tanh(raw)
    det_ref[...] = jnp.sum(log_scale, axis=1, keepdims=True)
    row = lax.broadcasted_iota(jnp.int32, (width, half), 0)
    put = jnp.where(row == perms_ref[pl.ds(blk, 1), half:], 1.0, 0.0).astype(bf16)
    out_ref[...] = field_ref[...] * jnp.exp(select(log_scale, put, (1, 1))) + select(
        shift, put, (1, 1)
    )


def post(ids, mixed, own, oth, hidden, field, perms, gain):
    rows, width = field.shape
    full = hidden.shape[1]
    return call(
        post_kernel,
        [((rows, width), f32), ((rows, 1), f32)],
        ids,
        mixed,
        hidden,
        field,
        perms,
        gain,
        *own,
        *oth,
        scratch=[
            pltpu.VMEM((rows, 3 * full), bf16),
            pltpu.VMEM((rows, full), f32),
            pltpu.VMEM((NT,) + oth[0].shape, bf16),
            pltpu.SemaphoreType.DMA((NT,)),
        ],
        smem=1,
        left=NT,
        flops=4 << 30,
    )


def enter_kernel(emb_ref, gain_ref, w_query_ref, w_keyval_ref, q_ref, kv_ref):
    start = jnp.concatenate([emb_ref[t] for t in range(emb_ref.shape[0])], axis=1)
    unit = normed(start.astype(f32), gain_ref[...]).astype(bf16)
    kv_ref[...] = jnp.dot(unit, w_keyval_ref[...], preferred_element_type=f32).astype(bf16)
    q_ref[...] = jnp.dot(unit, w_query_ref[...], preferred_element_type=f32).astype(bf16)


def causal_kernel(ids, q_ref, order_ref, order_row_ref, w_ref, *refs):
    kv_refs, o_ref, s_ref = refs[:-2], refs[-2], refs[-1]
    dh = q_ref.shape[1]
    patch = ids[1]
    own = order_row_ref[...] <= order_ref[...]
    top = None
    for j, kv_ref in enumerate(kv_refs):
        owner = ids[2 + j]
        s = lax.dot_general(
            q_ref[...], kv_ref[:, :dh], (((1,), (1,)), ((), ())), preferred_element_type=f32
        ) * (dh ** (-0.5))
        if j == 0:
            s = jnp.where(own, s, -jnp.inf)
        else:
            s = jnp.where(owner < patch, s, -jnp.inf)
        s_ref[j] = s
        m = jnp.max(s, axis=1, keepdims=True)
        top = m if top is None else jnp.maximum(top, m)
    total = acc = None
    for j, kv_ref in enumerate(kv_refs):
        p = jnp.exp(s_ref[j] - top)
        t = jnp.sum(p, axis=1, keepdims=True)
        a = jnp.dot(p.astype(bf16), kv_ref[:, dh:], preferred_element_type=f32)
        total = t if total is None else total + t
        acc = a if acc is None else acc + a
    attended = (acc / total).astype(bf16)
    for at in range(0, w_ref.shape[1], 512):
        o_ref[:, at : at + 512] = dot(attended, w_ref[:, at : at + 512]).astype(bf16)


def resid_kernel(ids, parts_ref, emb_ref, gain_ref, resid_ref, unit_ref):
    nt, part, _ = parts_ref.shape
    at = pl.ds(pl.multiple_of(ids[1] * part, part), part)
    start = jnp.concatenate([emb_ref[t, at, :] for t in range(nt)], axis=1).astype(f32)
    resid = start + sum(parts_ref[t].astype(f32) for t in range(nt))
    resid_ref[...] = resid
    unit = normed(resid, gain_ref[...]).astype(bf16)
    for t in range(nt):
        unit_ref[t] = unit


def mlp_kernel(
    ids, unit_ref, resid_ref, gate_ref, up_ref, down_ref, out_ref, inner_ref, sum_ref
):
    model, hidden = gate_ref.shape
    lanes, part = out_ref.shape[2], resid_ref.shape[0]
    unit = unit_ref.reshape(NT * part, model)

    def expand(at):
        cut = pl.ds(at, TILE)
        gate = dot(unit[...], gate_ref[:, cut])
        up = dot(unit[...], up_ref[:, cut])
        inner_ref[:, cut] = (jax.nn.gelu(gate, approximate=True) * up).astype(bf16)

    tiles(hidden // TILE, expand)
    mine = pl.ds(pl.multiple_of(ids[1] * part, part), part)

    def contract(at):
        cut = pl.ds(at, TILE)
        sum_ref[...] = dot(inner_ref[...], down_ref[:, cut])
        sum_ref[mine, :] = sum_ref[mine, :] + resid_ref[:, cut]
        out_ref[at // lanes] = sum_ref[...].astype(bf16)

    tiles(model // TILE, contract)


def in_hbm(value):
    return pltpu.with_memory_space_constraint(value, pltpu.HBM)


def tied(value, *others):
    return lax.optimization_barrier((value, *others))[0]


def on_device(
    patches,
    perms,
    w_in,
    gain_mix,
    w_qkv,
    w_mix,
    gain_out,
    w_head,
    order,
    w_embed,
    gain_attn,
    w_query,
    w_keyval,
    w_attn,
    gain_mlp,
    w_gate,
    w_up,
    w_down,
):
    rows = patches.shape[0]
    local_w = w_qkv.shape[3]
    where = lax.axis_index("tensor")
    patch = lax.axis_index("patch")
    core = patch % 2
    even = core == 0
    ids = jnp.stack([core, where, 0]).astype(jnp.int32)

    w_qkv = w_qkv.transpose(0, 2, 1, 3)
    w_in, w_qkv, w_mix, w_head = map(in_hbm, (w_in, w_qkv, w_mix, w_head))
    halved = cut(ids, w_mix, w_head)
    own_weights = [halved[0], None]
    side_weights = [lax.ppermute(halved[0], "tensor", ACROSS), None]
    field = patches
    logdet = 0.0
    for blk in range(BLOCKS):
        at_blk = jnp.stack([core, where, blk]).astype(jnp.int32)
        hidden, query, keyval, other = pre(at_blk, field, perms, w_in, gain_mix, w_qkv)
        hd = local_w // 2
        got = over(other, CORE)
        query = jnp.concatenate([query, got[:, :hd]], axis=0)
        keyval = jnp.concatenate([keyval, got[:, hd:]], axis=0)
        own_w = spread(tied(own_weights[blk], keyval), side_weights[blk])
        oth_w = [in_hbm(over(w, CORE)) for w in own_w]
        pieces = gather_chips(keyval)
        state = attend(query, pieces[:4], [], False)
        state = attend(query, pieces[4:7], state, False)
        (out,) = attend(tied(query, own_w[2], own_w[5]), pieces[7:], state, True)
        back = over(out[rows:], CORE)
        front = out[:rows]
        mixed = jnp.concatenate(
            [jnp.where(even, front, back), jnp.where(even, back, front)], axis=1
        )
        mixed = exchange(jnp.broadcast_to(mixed, (NT,) + mixed.shape))
        if blk + 1 < BLOCKS:
            own_weights[blk + 1] = tied(halved[blk + 1], mixed)
            side_weights[blk + 1] = lax.ppermute(own_weights[blk + 1], "tensor", ACROSS)
        field, det = post(at_blk, mixed, own_w, oth_w, hidden, field, perms, gain_out)
        logdet = logdet + det[:, 0]
    embed_part = jnp.dot(field.astype(bf16), w_embed, preferred_element_type=f32).astype(bf16)
    embedded = exchange(jnp.broadcast_to(embed_part, (NT,) + embed_part.shape))
    query_dec, keyval = call(
        enter_kernel,
        [((rows, DH), bf16), ((rows, 2 * DH), bf16)],
        embedded,
        gain_attn[None],
        w_query,
        w_keyval,
        flops=1 << 30,
    )
    pieces = gather_chips(keyval)
    pieces = pieces + [over(x, CORE) for x in pieces]

    y, x = patch // 4, (patch // 2) % 2
    owners = [core, patch]
    for dc in (0, 1):
        for dy, dx in ((0, 0), (-1, 0), (1, 0), (0, 1), (-1, 1), (1, 1), (2, 0), (2, 1)):
            owners.append((((y + dy) % 4) * 2 + (x + dx) % 2) * 2 + (core + dc) % 2)
    model_w = w_attn.shape[1]
    (partial_value,) = call(
        causal_kernel,
        [((rows, model_w), bf16)],
        jnp.stack(owners).astype(jnp.int32),
        query_dec,
        order[:, None],
        order[None],
        w_attn,
        *pieces,
        scratch=[pltpu.VMEM((len(pieces), rows, rows), f32)],
        smem=1,
        flops=2 << 30,
    )
    part, cols = rows // NT, model_w // NT
    resid, unit = call(
        resid_kernel,
        [((part, model_w), f32), ((NT, part, model_w), bf16)],
        ids,
        exchange(partial_value.reshape(NT, part, model_w)),
        embedded,
        gain_mlp[None],
        smem=1,
    )
    (down,) = call(
        mlp_kernel,
        [((NT, rows, cols), bf16)],
        ids,
        exchange(unit),
        resid,
        w_gate,
        w_up,
        w_down,
        scratch=[
            pltpu.VMEM((rows, w_gate.shape[1]), bf16),
            pltpu.VMEM((rows, cols), f32),
        ],
        smem=1,
        limit=8,
        flops=4 << 30,
    )
    decoded = jnp.sum(exchange(down).astype(f32), axis=0).astype(bf16)
    return (decoded, logdet)


def solution(mesh):
    return jax.shard_map(
        on_device,
        mesh=mesh,
        in_specs=(
            P("patch", None),
            P(),
            P(),
            P(),
            P(None, None, None, "tensor"),
            P(None, "tensor", None),
            P(),
            P(None, "tensor", None),
            P("patch"),
            P(None, "tensor"),
            P(),
            P(None, "tensor"),
            P(),
            P("tensor", None),
            P(),
            P(None, "tensor"),
            P(None, "tensor"),
            P("tensor", None),
        ),
        out_specs=(P("patch", "tensor"), P("patch")),
        check_vma=False,
    )
```

```python
import functools

import jax
import jax.numpy as jnp
from jax import lax
from jax.experimental import pallas as pl
from jax.experimental.pallas import tpu as pltpu
from jax.sharding import PartitionSpec as P


BLOCKS = 2
DH = 256
NP = 16
NT = 8


bf16 = jnp.bfloat16
f32 = jnp.float32


def normed(value, gain):
    return value * lax.rsqrt(jnp.mean(value * value, axis=-1, keepdims=True) + 1e-06) * gain


CORE = [(i, i ^ 1) for i in range(NP)]


def hop(dy, dx):
    def to(i):
        y, x, c = i // 4, (i // 2) % 2, i % 2
        return ((y + dy) % 4 * 2 + (x + dx) % 2) * 2 + c

    return [(i, to(i)) for i in range(NP)]


UP, DOWN, SIDE = hop(1, 0), hop(-1, 0), hop(0, 1)


def over(value, pairs):
    return lax.ppermute(value, "patch", pairs)


def gather_chips(own):
    half = own.shape[0] // 2
    up = over(own, UP)
    down = over(own, DOWN)
    side = over(own, SIDE)
    side_up = over(side, UP)
    side_down = over(down, SIDE)
    far_a = over(up[:half], UP)
    far_b = over(down[half:], DOWN)
    far = jnp.concatenate([far_a, far_b], 0)
    side_far = over(far, SIDE)
    return [own, up, down, side, side_up, side_down, far, side_far]


def exchange(parts):
    return lax.all_to_all(parts, "tensor", 0, 0)


ACROSS = [(i, i ^ 1) for i in range(NT)]
RISE = [(i, (i + 2) % NT) for i in range(NT)]
FALL = [(i, (i - 2) % NT) for i in range(NT)]


def spread(own, side):
    rise, fall = (functools.partial(lax.ppermute, axis_name="tensor", perm=p) for p in (RISE, FALL))
    below, above = rise(own), fall(side)
    below_side, above_own = rise(side), fall(own)
    far, far_side = rise(below), fall(above)
    return [own, side, below, below_side, above_own, above, far, far_side]


RING = [(0, 0), (0, 1), (-1, 0), (-1, 1), (1, 0), (1, 1), (2, 0), (2, 1)]


def ring_order(where):
    z, x = where // 2, where % 2
    return [(z + dz + NT // 2) % (NT // 2) * 2 + (x + dx) % 2 for dz, dx in RING]


def split2(x):
    a = x.astype(bf16)
    b = (x - a.astype(f32)).astype(bf16)
    return a, b


def split3(x):
    a = x.astype(bf16)
    r = x - a.astype(f32)
    b = r.astype(bf16)
    c = (r - b.astype(f32)).astype(bf16)
    return a, b, c


def select(x, one_hot, dims=(1, 0)):
    dims = (((dims[0],), (dims[1],)), ((), ()))
    a, b, c = (
        lax.dot_general(p, one_hot, dims, preferred_element_type=f32) for p in split3(x)
    )
    return (c + b) + a


def left6(x):
    a, b, c = split3(x)
    return jnp.concatenate([a, a, b, a, b, c], axis=1)


def right6(x):
    a, b, c = split3(x)
    return jnp.concatenate([a, b, a, c, b, a], axis=0)


def left3(x):
    a, b = split2(x)
    return jnp.concatenate([a, a, b], axis=1)


def dot(left, right):
    return jnp.dot(left, right, preferred_element_type=f32)


TILE = 256


def tiles(count, body):
    def step(i, carry):
        body(pl.multiple_of(i * TILE, TILE))
        return carry

    lax.fori_loop(0, count, step, 0)


VMEM = pl.BlockSpec(memory_space=pltpu.VMEM)
HBM = pl.BlockSpec(memory_space=pltpu.HBM)
ANY = pl.BlockSpec(memory_space=pl.ANY)
SMEM = pl.BlockSpec(memory_space=pltpu.SMEM)


def call(body, outs, *args, scratch=(), flops=0, limit=16, smem=0, left=0, kept=HBM):
    moved = sum(x.size * x.dtype.itemsize for x in args)
    return pl.pallas_call(
        body,
        in_specs=[SMEM] * smem + [VMEM] * (len(args) - smem - left) + [kept] * left,
        out_specs=[VMEM] * len(outs),
        out_shape=[jax.ShapeDtypeStruct(*o) for o in outs],
        scratch_shapes=list(scratch),
        compiler_params=pltpu.CompilerParams(vmem_limit_bytes=limit << 20),
        cost_estimate=pl.CostEstimate(flops=flops, bytes_accessed=moved, transcendentals=0),
    )(*args)


def cut_kernel(ids, mix_ref, head_ref, *refs):
    outs, (buf_ref, sems) = refs[:BLOCKS], refs[BLOCKS:]
    rows = buf_ref.shape[1]
    copies = []
    for blk in range(BLOCKS):
        at = 0
        for i, ref in enumerate((mix_ref, head_ref)):
            cols = ref.shape[2] // 2
            source = ref.at[blk, :, pl.ds(pl.multiple_of(ids[0] * cols, 128), cols)]
            copies.append(
                pltpu.make_async_copy(source, buf_ref.at[blk, :, at : at + cols], sems.at[blk, i])
            )
            at += cols
    for copy in copies:
        copy.start()
    for blk, out in enumerate(outs):
        copies[2 * blk].wait()
        copies[2 * blk + 1].wait()
        high, low = split2(buf_ref[blk])
        out[:rows, :] = high
        out[rows:, :] = low


def cut(ids, w_mix, w_head):
    rows, cols = w_mix.shape[1], (w_mix.shape[2] + w_head.shape[2]) // 2
    return pl.pallas_call(
        cut_kernel,
        in_specs=[SMEM, HBM, HBM],
        out_specs=[VMEM] * BLOCKS,
        out_shape=[jax.ShapeDtypeStruct((2 * rows, cols), bf16)] * BLOCKS,
        scratch_shapes=[
            pltpu.VMEM((BLOCKS, rows, cols), f32),
            pltpu.SemaphoreType.DMA((BLOCKS, 2)),
        ],
        compiler_params=pltpu.CompilerParams(vmem_limit_bytes=8 << 20),
        name="cut",
    )(ids, w_mix, w_head)


def pre_kernel(
    ids, field_ref, perms_ref, gain_ref, w_in_all, w_all,
    hidden_ref, q_ref, kv_ref, oth_ref, cond_ref, unit_ref, w_in_ref, w_ref, sems,
):
    blk = ids[2]
    copy_in = pltpu.make_async_copy(w_in_all.at[blk], w_in_ref, sems.at[0])
    copy_qkv = pltpu.make_async_copy(w_all.at[blk], w_ref, sems.at[1])
    copy_in.start()
    copy_qkv.start()
    even = ids[0] == 0
    half, full = w_in_ref.shape
    width = field_ref.shape[1]
    hd = w_ref.shape[2] // 2
    row = lax.broadcasted_iota(jnp.int32, (width, half), 0)
    take = jnp.where(row == perms_ref[pl.ds(blk, 1), :half], 1.0, 0.0).astype(bf16)
    cond_ref[...] = left6(select(field_ref[...], take))
    copy_in.wait()

    def column(at):
        cut = pl.ds(at, TILE)
        hidden_ref[:, cut] = dot(cond_ref[...], right6(w_in_ref[:, cut]))

    tiles(full // TILE, column)
    unit_ref[...] = left6(normed(hidden_ref[...], gain_ref[pl.ds(blk, 1), :]))
    copy_qkv.wait()
    qk = jnp.concatenate([w_ref[0], w_ref[1]], axis=1)
    qk = dot(unit_ref[...], right6(qk))
    v = dot(unit_ref[...], right6(w_ref[2]))
    q, k = qk[:, : 2 * hd], qk[:, 2 * hd :]

    def pick(x, first):
        return jnp.where(first, x[:, :hd], x[:, hd:])

    q_ref[...] = pick(q, even)
    kv_ref[...] = jnp.concatenate([pick(k, even), pick(v, even)], axis=1)
    odd = jnp.logical_not(even)
    oth_ref[...] = jnp.concatenate([pick(q, odd), pick(k, odd), pick(v, odd)], axis=1)


def pre(ids, field, perms, w_in, gain, w_qkv):
    rows, (half, full) = field.shape[0], w_in.shape[1:]
    hd = w_qkv.shape[3] // 2
    return call(
        pre_kernel,
        [((rows, full), f32), ((rows, hd), f32), ((rows, 2 * hd), f32), ((rows, 3 * hd), f32)],
        ids,
        field,
        perms,
        gain,
        w_in,
        w_qkv,
        scratch=[
            pltpu.VMEM((rows, 6 * half), bf16),
            pltpu.VMEM((rows, 6 * full), bf16),
            pltpu.VMEM(w_in.shape[1:], f32),
            pltpu.VMEM(w_qkv.shape[1:], f32),
            pltpu.SemaphoreType.DMA((2,)),
        ],
        smem=1,
        left=2,
        flops=3 << 30,
    )


def attend_kernel(count, first, last, q_ref, *refs):
    kv_refs, refs = refs[:count], refs[count:]
    if not first:
        (acc0_ref, stat0_ref), refs = refs[:2], refs[2:]
    rows, hd = q_ref.shape
    s_ref = refs[-1]
    block = s_ref.shape[1]

    def some_rows(i, carry):
        at = pl.ds(pl.multiple_of(i * block, block), block)
        q1, q2, q3 = split3(q_ref[at, :] * (hd ** (-0.5)))
        qs = jnp.concatenate([q1, q1, q2, q1, q2, q3], axis=1)
        top = None if first else stat0_ref[at, :1]
        for j, kv_ref in enumerate(kv_refs):
            k1, k2, k3 = split3(kv_ref[:, :hd])
            ks = jnp.concatenate([k1, k2, k1, k3, k2, k1], axis=1)
            s = lax.dot_general(qs, ks, (((1,), (1,)), ((), ())), preferred_element_type=f32)
            s_ref[j] = s
            m = jnp.max(s, axis=1, keepdims=True)
            top = m if top is None else jnp.maximum(top, m)
        total = acc = None
        if not first:
            factor = jnp.exp(stat0_ref[at, :1] - top)
            total, acc = stat0_ref[at, hd : hd + 1] * factor, acc0_ref[at, :] * factor
        for j, kv_ref in enumerate(kv_refs):
            p = jnp.exp(s_ref[j] - top)
            t = jnp.sum(p, axis=1, keepdims=True)
            v1, v2, v3 = split3(kv_ref[:, hd:])
            p1, p2 = split2(p)
            a = dot(p1, jnp.concatenate([v1, v2, v3], axis=1))
            b = dot(p2, jnp.concatenate([v1, v2], axis=1))
            a = a[:, :hd] + (a[:, hd : 2 * hd] + b[:, :hd]) + (a[:, 2 * hd :] + b[:, hd:])
            total = t if total is None else total + t
            acc = a if acc is None else acc + a
        if last:
            refs[0][at, :] = acc / total
        else:
            refs[0][at, :] = acc
            refs[1][at, :] = jnp.concatenate(
                [jnp.broadcast_to(top, (block, hd)), jnp.broadcast_to(total, (block, hd))], axis=1
            )
        return carry

    lax.fori_loop(0, rows // block, some_rows, 0)


def attend(query, pieces, state, last):
    rows, hd = query.shape
    keys = pieces[0].shape[0]
    count = len(pieces)
    outs = [((rows, hd), f32)] if last else [((rows, hd), f32), ((rows, 2 * hd), f32)]
    return call(
        functools.partial(attend_kernel, count, not state, last),
        outs,
        query,
        *pieces,
        *state,
        scratch=[pltpu.VMEM((count, 256, keys), f32)],
        flops=count << 30,
    )


def post_kernel(ids, m_ref, hidden_ref, field_ref, perms_ref, gain_ref, *refs):
    own_refs, far_refs, refs = refs[:NT], refs[NT : 2 * NT], refs[2 * NT :]
    out_ref, det_ref, left_ref, sum_ref, oth_ref, sems = refs
    copies = [
        pltpu.make_async_copy(far, oth_ref.at[j], sems.at[j]) for j, far in enumerate(far_refs)
    ]
    for copy in copies:
        copy.start()
    blk, even = ids[2], ids[0] == 0
    nt, _, lanes = m_ref.shape
    full, width = hidden_ref.shape[1], field_ref.shape[1]
    half, mid = width // 2, full // 2
    order = ring_order(ids[1])
    cuts = [(at, TILE) for at in range(0, mid, TILE)] + [(mid, half)]

    def product(side, k):
        cut = slice(cuts[k][0], sum(cuts[k]))
        high, low = (
            [side[j][i * lanes : (i + 1) * lanes, cut] for j in range(nt)] for i in range(2)
        )
        return dot(left_ref[...], jnp.concatenate(high + low + high, axis=0))

    oth_refs = [oth_ref.at[j] for j in range(nt)]
    left_ref[...] = left3(jnp.concatenate([m_ref[t] for t in order], axis=1))
    near = [product(own_refs, k) for k in range(len(cuts) - 1)]
    for copy in copies:
        copy.wait()
    for k, (at, cols) in enumerate(cuts[:-1]):
        far = product(oth_refs, k)
        cut = slice(at, at + cols)
        sum_ref[:, cut] = hidden_ref[:, cut] + jnp.where(even, near[k], far)
        cut = slice(at + mid, at + mid + cols)
        sum_ref[:, cut] = hidden_ref[:, cut] + jnp.where(even, far, near[k])
    sum_ref[...] = normed(sum_ref[...], gain_ref[pl.ds(blk, 1), :])
    parts = [sum_ref[:, pl.ds(pl.multiple_of(t * lanes, lanes), lanes)] for t in order]
    left_ref[...] = left3(jnp.concatenate(parts, axis=1))
    near, far = product(own_refs, len(cuts) - 1), product(oth_refs, len(cuts) - 1)
    raw, shift = jnp.where(even, near, far), jnp.where(even, far, near)
    log_scale = jnp.tanh(raw)
    det_ref[...] = jnp.sum(log_scale, axis=1, keepdims=True)
    row = lax.broadcasted_iota(jnp.int32, (width, half), 0)
    put = jnp.where(row == perms_ref[pl.ds(blk, 1), half:], 1.0, 0.0).astype(bf16)
    out_ref[...] = field_ref[...] * jnp.exp(select(log_scale, put, (1, 1))) + select(
        shift, put, (1, 1)
    )


def post(ids, mixed, own, oth, hidden, field, perms, gain):
    rows, width = field.shape
    full = hidden.shape[1]
    return call(
        post_kernel,
        [((rows, width), f32), ((rows, 1), f32)],
        ids,
        mixed,
        hidden,
        field,
        perms,
        gain,
        *own,
        *oth,
        scratch=[
            pltpu.VMEM((rows, 3 * full), bf16),
            pltpu.VMEM((rows, full), f32),
            pltpu.VMEM((NT,) + oth[0].shape, bf16),
            pltpu.SemaphoreType.DMA((NT,)),
        ],
        smem=1,
        left=NT,
        flops=4 << 30,
    )


def enter_kernel(emb_ref, gain_ref, w_query_ref, w_keyval_ref, q_ref, kv_ref):
    start = jnp.concatenate([emb_ref[t] for t in range(emb_ref.shape[0])], axis=1)
    unit = normed(start.astype(f32), gain_ref[...]).astype(bf16)
    kv_ref[...] = jnp.dot(unit, w_keyval_ref[...], preferred_element_type=f32).astype(bf16)
    q_ref[...] = jnp.dot(unit, w_query_ref[...], preferred_element_type=f32).astype(bf16)


def causal_kernel(ids, q_ref, order_ref, order_row_ref, w_ref, *refs):
    kv_refs, o_ref, s_ref = refs[:-2], refs[-2], refs[-1]
    dh = q_ref.shape[1]
    patch = ids[1]
    own = order_row_ref[...] <= order_ref[...]
    top = None
    for j, kv_ref in enumerate(kv_refs):
        owner = ids[2 + j]
        s = lax.dot_general(
            q_ref[...], kv_ref[:, :dh], (((1,), (1,)), ((), ())), preferred_element_type=f32
        ) * (dh ** (-0.5))
        if j == 0:
            s = jnp.where(own, s, -jnp.inf)
        else:
            s = jnp.where(owner < patch, s, -jnp.inf)
        s_ref[j] = s
        m = jnp.max(s, axis=1, keepdims=True)
        top = m if top is None else jnp.maximum(top, m)
    total = acc = None
    for j, kv_ref in enumerate(kv_refs):
        p = jnp.exp(s_ref[j] - top)
        t = jnp.sum(p, axis=1, keepdims=True)
        a = jnp.dot(p.astype(bf16), kv_ref[:, dh:], preferred_element_type=f32)
        total = t if total is None else total + t
        acc = a if acc is None else acc + a
    attended = (acc / total).astype(bf16)
    for at in range(0, w_ref.shape[1], 512):
        o_ref[:, at : at + 512] = dot(attended, w_ref[:, at : at + 512]).astype(bf16)


def resid_kernel(ids, parts_ref, emb_ref, gain_ref, resid_ref, unit_ref):
    nt, part, _ = parts_ref.shape
    at = pl.ds(pl.multiple_of(ids[1] * part, part), part)
    start = jnp.concatenate([emb_ref[t, at, :] for t in range(nt)], axis=1).astype(f32)
    resid = start + sum(parts_ref[t].astype(f32) for t in range(nt))
    resid_ref[...] = resid
    unit = normed(resid, gain_ref[...]).astype(bf16)
    for t in range(nt):
        unit_ref[t] = unit


def mlp_kernel(
    ids, unit_ref, resid_ref, gate_ref, up_ref, down_ref, out_ref, inner_ref, sum_ref
):
    model, hidden = gate_ref.shape
    lanes, part = out_ref.shape[2], resid_ref.shape[0]
    unit = unit_ref.reshape(NT * part, model)

    def expand(at):
        cut = pl.ds(at, TILE)
        gate = dot(unit[...], gate_ref[:, cut])
        up = dot(unit[...], up_ref[:, cut])
        inner_ref[:, cut] = (jax.nn.gelu(gate, approximate=True) * up).astype(bf16)

    tiles(hidden // TILE, expand)
    mine = pl.ds(pl.multiple_of(ids[1] * part, part), part)

    def contract(at):
        cut = pl.ds(at, TILE)
        sum_ref[...] = dot(inner_ref[...], down_ref[:, cut])
        sum_ref[mine, :] = sum_ref[mine, :] + resid_ref[:, cut]
        out_ref[at // lanes] = sum_ref[...].astype(bf16)

    tiles(model // TILE, contract)


def in_hbm(value):
    return pltpu.with_memory_space_constraint(value, pltpu.HBM)


def tied(value, *others):
    return lax.optimization_barrier((value, *others))[0]


def on_device(
    patches,
    perms,
    w_in,
    gain_mix,
    w_qkv,
    w_mix,
    gain_out,
    w_head,
    order,
    w_embed,
    gain_attn,
    w_query,
    w_keyval,
    w_attn,
    gain_mlp,
    w_gate,
    w_up,
    w_down,
):
    rows = patches.shape[0]
    local_w = w_qkv.shape[3]
    where = lax.axis_index("tensor")
    patch = lax.axis_index("patch")
    core = patch % 2
    even = core == 0
    ids = jnp.stack([core, where, 0]).astype(jnp.int32)

    w_qkv = w_qkv.transpose(0, 2, 1, 3)
    w_in, w_qkv, w_mix, w_head = map(in_hbm, (w_in, w_qkv, w_mix, w_head))
    halved = cut(ids, w_mix, w_head)
    own_weights = [halved[0], None]
    side_weights = [lax.ppermute(halved[0], "tensor", ACROSS), None]
    field = patches
    logdet = 0.0
    for blk in range(BLOCKS):
        at_blk = jnp.stack([core, where, blk]).astype(jnp.int32)
        hidden, query, keyval, other = pre(at_blk, field, perms, w_in, gain_mix, w_qkv)
        hd = local_w // 2
        got = over(other, CORE)
        query = jnp.concatenate([query, got[:, :hd]], axis=0)
        keyval = jnp.concatenate([keyval, got[:, hd:]], axis=0)
        own_w = spread(tied(own_weights[blk], keyval), side_weights[blk])
        oth_w = []
        for w in own_w:
            oth_w.append(in_hbm(over(w, CORE)))
        pieces = gather_chips(keyval)
        state = attend(query, pieces[:4], [], False)
        query = tied(query, own_w[2], own_w[5])
        state = attend(query, pieces[4:7], state, False)
        (out,) = attend(query, pieces[7:], state, True)
        back = over(out[rows:], CORE)
        front = out[:rows]
        mixed = jnp.concatenate(
            [jnp.where(even, front, back), jnp.where(even, back, front)], axis=1
        )
        mixed = exchange(jnp.broadcast_to(mixed, (NT,) + mixed.shape))
        if blk + 1 < BLOCKS:
            own_weights[blk + 1] = tied(halved[blk + 1], mixed)
            side_weights[blk + 1] = lax.ppermute(own_weights[blk + 1], "tensor", ACROSS)
        field, det = post(at_blk, mixed, own_w, oth_w, hidden, field, perms, gain_out)
        logdet = logdet + det[:, 0]
    embed_part = jnp.dot(field.astype(bf16), w_embed, preferred_element_type=f32).astype(bf16)
    embedded = exchange(jnp.broadcast_to(embed_part, (NT,) + embed_part.shape))
    query_dec, keyval = call(
        enter_kernel,
        [((rows, DH), bf16), ((rows, 2 * DH), bf16)],
        embedded,
        gain_attn[None],
        w_query,
        w_keyval,
        flops=1 << 30,
    )
    pieces = gather_chips(keyval)
    pieces = pieces + [over(x, CORE) for x in pieces]

    y, x = patch // 4, (patch // 2) % 2
    owners = [core, patch]
    for dc in (0, 1):
        for dy, dx in ((0, 0), (-1, 0), (1, 0), (0, 1), (-1, 1), (1, 1), (2, 0), (2, 1)):
            owners.append((((y + dy) % 4) * 2 + (x + dx) % 2) * 2 + (core + dc) % 2)
    model_w = w_attn.shape[1]
    (partial_value,) = call(
        causal_kernel,
        [((rows, model_w), bf16)],
        jnp.stack(owners).astype(jnp.int32),
        query_dec,
        order[:, None],
        order[None],
        w_attn,
        *pieces,
        scratch=[pltpu.VMEM((len(pieces), rows, rows), f32)],
        smem=1,
        flops=2 << 30,
    )
    part, cols = rows // NT, model_w // NT
    resid, unit = call(
        resid_kernel,
        [((part, model_w), f32), ((NT, part, model_w), bf16)],
        ids,
        exchange(partial_value.reshape(NT, part, model_w)),
        embedded,
        gain_mlp[None],
        smem=1,
    )
    (down,) = call(
        mlp_kernel,
        [((NT, rows, cols), bf16)],
        ids,
        exchange(unit),
        resid,
        w_gate,
        w_up,
        w_down,
        scratch=[
            pltpu.VMEM((rows, w_gate.shape[1]), bf16),
            pltpu.VMEM((rows, cols), f32),
        ],
        smem=1,
        limit=8,
        flops=4 << 30,
    )
    decoded = jnp.sum(exchange(down).astype(f32), axis=0).astype(bf16)
    return (decoded, logdet)


def solution(mesh):
    return jax.shard_map(
        on_device,
        mesh=mesh,
        in_specs=(
            P("patch", None),
            P(),
            P(),
            P(),
            P(None, None, None, "tensor"),
            P(None, "tensor", None),
            P(),
            P(None, "tensor", None),
            P("patch"),
            P(None, "tensor"),
            P(),
            P(None, "tensor"),
            P(),
            P("tensor", None),
            P(),
            P(None, "tensor"),
            P(None, "tensor"),
            P("tensor", None),
        ),
        out_specs=(P("patch", "tensor"), P("patch")),
        check_vma=False,
    )
```

```python
import functools

import jax
import jax.numpy as jnp
from jax import lax
from jax.experimental import pallas as pl
from jax.experimental.pallas import tpu as pltpu
from jax.sharding import PartitionSpec as P


BLOCKS = 2
DH = 256
NP = 16
NT = 8


bf16 = jnp.bfloat16
f32 = jnp.float32


def normed(value, gain):
    return value * lax.rsqrt(jnp.mean(value * value, axis=-1, keepdims=True) + 1e-06) * gain


CORE = [(i, i ^ 1) for i in range(NP)]


def hop(dy, dx):
    def to(i):
        y, x, c = i // 4, (i // 2) % 2, i % 2
        return ((y + dy) % 4 * 2 + (x + dx) % 2) * 2 + c

    return [(i, to(i)) for i in range(NP)]


UP, DOWN, SIDE = hop(1, 0), hop(-1, 0), hop(0, 1)


def over(value, pairs):
    return lax.ppermute(value, "patch", pairs)


def gather_chips(own):
    half = own.shape[0] // 2
    up = over(own, UP)
    down = over(own, DOWN)
    side = over(own, SIDE)
    side_up = over(side, UP)
    side_down = over(down, SIDE)
    far_a = over(up[:half], UP)
    far_b = over(down[half:], DOWN)
    far = jnp.concatenate([far_a, far_b], 0)
    side_far = over(far, SIDE)
    return [own, up, down, side, side_up, side_down, far, side_far]


def exchange(parts):
    return lax.all_to_all(parts, "tensor", 0, 0)


ACROSS = [(i, i ^ 1) for i in range(NT)]
RISE = [(i, (i + 2) % NT) for i in range(NT)]
FALL = [(i, (i - 2) % NT) for i in range(NT)]


def spread(own, side):
    rise, fall = (functools.partial(lax.ppermute, axis_name="tensor", perm=p) for p in (RISE, FALL))
    rows = own.shape[0]
    pair = jnp.concatenate([own, side], axis=0)
    below, above = rise(pair), fall(pair)
    far, far_side = rise(below[:rows]), fall(above[rows:])
    return [pair, below, above, far, far_side]


RING = [(0, 0), (0, 1), (-1, 0), (-1, 1), (1, 0), (1, 1), (2, 0), (2, 1)]


def ring_order(where):
    z, x = where // 2, where % 2
    return [(z + dz + NT // 2) % (NT // 2) * 2 + (x + dx) % 2 for dz, dx in RING]


def split2(x):
    a = x.astype(bf16)
    b = (x - a.astype(f32)).astype(bf16)
    return a, b


def split3(x):
    a = x.astype(bf16)
    r = x - a.astype(f32)
    b = r.astype(bf16)
    c = (r - b.astype(f32)).astype(bf16)
    return a, b, c


def select(xs, one_hot, dims=(1, 0)):
    rows = xs[0].shape[0]
    parts = jnp.concatenate([part for x in xs for part in split3(x)], axis=0)
    dims = (((dims[0],), (dims[1],)), ((), ()))
    out = lax.dot_general(parts, one_hot, dims, preferred_element_type=f32)
    cut = [out[i * rows : (i + 1) * rows] for i in range(3 * len(xs))]
    return [(cut[3 * i + 2] + cut[3 * i + 1]) + cut[3 * i] for i in range(len(xs))]


def left6(x):
    a, b, c = split3(x)
    return jnp.concatenate([a, a, b, a, b, c], axis=1)


def right6(x):
    a, b, c = split3(x)
    return jnp.concatenate([a, b, a, c, b, a], axis=0)


def left3(x):
    a, b = split2(x)
    return jnp.concatenate([a, a, b], axis=1)


def dot(left, right):
    return jnp.dot(left, right, preferred_element_type=f32)


TILE = 256


def tiles(count, body):
    def step(i, carry):
        body(pl.multiple_of(i * TILE, TILE))
        return carry

    lax.fori_loop(0, count, step, 0)


VMEM = pl.BlockSpec(memory_space=pltpu.VMEM)
HBM = pl.BlockSpec(memory_space=pltpu.HBM)
ANY = pl.BlockSpec(memory_space=pl.ANY)
SMEM = pl.BlockSpec(memory_space=pltpu.SMEM)


def call(body, outs, *args, scratch=(), flops=0, limit=16, smem=0, left=0, kept=HBM):
    moved = sum(x.size * x.dtype.itemsize for x in args)
    return pl.pallas_call(
        body,
        in_specs=[SMEM] * smem + [VMEM] * (len(args) - smem - left) + [kept] * left,
        out_specs=[VMEM] * len(outs),
        out_shape=[jax.ShapeDtypeStruct(*o) for o in outs],
        scratch_shapes=list(scratch),
        compiler_params=pltpu.CompilerParams(vmem_limit_bytes=limit << 20),
        cost_estimate=pl.CostEstimate(flops=flops, bytes_accessed=moved, transcendentals=0),
    )(*args)


def cut_kernel(ids, mix_ref, head_ref, *refs):
    outs, (buf_ref, sems) = refs[:BLOCKS], refs[BLOCKS:]
    rows = buf_ref.shape[1]
    copies = []
    for blk in range(BLOCKS):
        at = 0
        for i, ref in enumerate((mix_ref, head_ref)):
            cols = ref.shape[2] // 2
            source = ref.at[blk, :, pl.ds(pl.multiple_of(ids[0] * cols, 128), cols)]
            copies.append(
                pltpu.make_async_copy(source, buf_ref.at[blk, :, at : at + cols], sems.at[blk, i])
            )
            at += cols
    for copy in copies:
        copy.start()
    for blk, out in enumerate(outs):
        copies[2 * blk].wait()
        copies[2 * blk + 1].wait()
        high, low = split2(buf_ref[blk])
        out[:rows, :] = high
        out[rows:, :] = low


def cut(ids, w_mix, w_head):
    rows, cols = w_mix.shape[1], (w_mix.shape[2] + w_head.shape[2]) // 2
    return pl.pallas_call(
        cut_kernel,
        in_specs=[SMEM, HBM, HBM],
        out_specs=[VMEM] * BLOCKS,
        out_shape=[jax.ShapeDtypeStruct((2 * rows, cols), bf16)] * BLOCKS,
        scratch_shapes=[
            pltpu.VMEM((BLOCKS, rows, cols), f32),
            pltpu.SemaphoreType.DMA((BLOCKS, 2)),
        ],
        compiler_params=pltpu.CompilerParams(vmem_limit_bytes=8 << 20),
        name="cut",
    )(ids, w_mix, w_head)


def pre_kernel(
    ids, field_ref, perms_all, gain_all, w_in_all, w_all,
    hidden_ref, q_ref, kv_ref, oth_ref,
    cond_ref, unit_ref, w_in_ref, w_ref, perms_ref, gain_ref, sems,
):
    blk = ids[2]
    copy_in = pltpu.make_async_copy(w_in_all.at[blk], w_in_ref, sems.at[0])
    copy_qkv = pltpu.make_async_copy(w_all.at[blk], w_ref, sems.at[1])
    copy_perms = pltpu.make_async_copy(perms_all, perms_ref, sems.at[2])
    copy_gain = pltpu.make_async_copy(gain_all, gain_ref, sems.at[3])
    for copy in (copy_perms, copy_in, copy_qkv, copy_gain):
        copy.start()
    even = ids[0] == 0
    half, full = w_in_ref.shape
    width = field_ref.shape[1]
    hd = w_ref.shape[2] // 2
    row = lax.broadcasted_iota(jnp.int32, (width, half), 0)
    copy_perms.wait()
    take = jnp.where(row == perms_ref[pl.ds(blk, 1), :half], 1.0, 0.0).astype(bf16)
    cond_ref[...] = left6(select([field_ref[...]], take)[0])
    copy_in.wait()

    def column(at):
        cut = pl.ds(at, TILE)
        hidden_ref[:, cut] = dot(cond_ref[...], right6(w_in_ref[:, cut]))

    tiles(full // TILE, column)
    copy_gain.wait()
    unit_ref[...] = left6(normed(hidden_ref[...], gain_ref[pl.ds(blk, 1), :]))
    copy_qkv.wait()
    qk = jnp.concatenate([w_ref[0], w_ref[1]], axis=1)
    qk = dot(unit_ref[...], right6(qk))
    v = dot(unit_ref[...], right6(w_ref[2]))
    q, k = qk[:, : 2 * hd], qk[:, 2 * hd :]

    def pick(x, first):
        return jnp.where(first, x[:, :hd], x[:, hd:])

    q_ref[...] = pick(q, even)
    kv_ref[...] = jnp.concatenate([pick(k, even), pick(v, even)], axis=1)
    odd = jnp.logical_not(even)
    oth_ref[...] = jnp.concatenate([pick(q, odd), pick(k, odd), pick(v, odd)], axis=1)


def pre(ids, field, perms, w_in, gain, w_qkv):
    rows, (half, full) = field.shape[0], w_in.shape[1:]
    hd = w_qkv.shape[3] // 2
    return call(
        pre_kernel,
        [((rows, full), f32), ((rows, hd), f32), ((rows, 2 * hd), f32), ((rows, 3 * hd), f32)],
        ids,
        field,
        perms,
        gain,
        w_in,
        w_qkv,
        scratch=[
            pltpu.VMEM((rows, 6 * half), bf16),
            pltpu.VMEM((rows, 6 * full), bf16),
            pltpu.VMEM(w_in.shape[1:], f32),
            pltpu.VMEM(w_qkv.shape[1:], f32),
            pltpu.VMEM(perms.shape, jnp.int32),
            pltpu.VMEM(gain.shape, f32),
            pltpu.SemaphoreType.DMA((4,)),
        ],
        smem=1,
        left=4,
        flops=3 << 30,
    )


def attend_kernel(count, first, last, q_ref, *refs):
    kv_refs, refs = refs[:count], refs[count:]
    if not first:
        (acc0_ref, stat0_ref), refs = refs[:2], refs[2:]
    rows, hd = q_ref.shape
    s_ref = refs[-1]
    block = s_ref.shape[1]

    def some_rows(i, carry):
        at = pl.ds(pl.multiple_of(i * block, block), block)
        q1, q2, q3 = split3(q_ref[at, :] * (hd ** (-0.5)))
        qs = jnp.concatenate([q1, q1, q2, q1, q2, q3], axis=1)
        top = None if first else stat0_ref[at, :1]
        for j, kv_ref in enumerate(kv_refs):
            k1, k2, k3 = split3(kv_ref[:, :hd])
            ks = jnp.concatenate([k1, k2, k1, k3, k2, k1], axis=1)
            s = lax.dot_general(qs, ks, (((1,), (1,)), ((), ())), preferred_element_type=f32)
            s_ref[j] = s
            m = jnp.max(s, axis=1, keepdims=True)
            top = m if top is None else jnp.maximum(top, m)
        total = acc = None
        if not first:
            factor = jnp.exp(stat0_ref[at, :1] - top)
            total, acc = stat0_ref[at, hd : hd + 1] * factor, acc0_ref[at, :] * factor
        for j, kv_ref in enumerate(kv_refs):
            p = jnp.exp(s_ref[j] - top)
            t = jnp.sum(p, axis=1, keepdims=True)
            v1, v2, v3 = split3(kv_ref[:, hd:])
            p1, p2 = split2(p)
            a = dot(p1, jnp.concatenate([v1, v2, v3], axis=1))
            b = dot(p2, jnp.concatenate([v1, v2], axis=1))
            a = a[:, :hd] + (a[:, hd : 2 * hd] + b[:, :hd]) + (a[:, 2 * hd :] + b[:, hd:])
            total = t if total is None else total + t
            acc = a if acc is None else acc + a
        if last:
            refs[0][at, :] = acc / total
        else:
            refs[0][at, :] = acc
            refs[1][at, :] = jnp.concatenate(
                [jnp.broadcast_to(top, (block, hd)), jnp.broadcast_to(total, (block, hd))], axis=1
            )
        return carry

    lax.fori_loop(0, rows // block, some_rows, 0)


def attend(query, pieces, state, last):
    rows, hd = query.shape
    keys = pieces[0].shape[0]
    count = len(pieces)
    outs = [((rows, hd), f32)] if last else [((rows, hd), f32), ((rows, 2 * hd), f32)]
    return call(
        functools.partial(attend_kernel, count, not state, last),
        outs,
        query,
        *pieces,
        *state,
        scratch=[pltpu.VMEM((count, 256, keys), f32)],
        flops=count << 30,
    )


def post_kernel(ids, m_ref, hidden_ref, field_ref, perms_ref, gain_ref, *refs):
    own_refs, far_refs, refs = refs[:5], refs[5:10], refs[10:]
    out_ref, det_ref, left_ref, sum_ref, oth_ref, sems = refs
    copies, at = [], 0
    for j, far in enumerate(far_refs):
        target = oth_ref.at[at : at + far.shape[0], :]
        copies.append(pltpu.make_async_copy(far, target, sems.at[j]))
        at += far.shape[0]
    for copy in copies:
        copy.start()
    blk, even = ids[2], ids[0] == 0
    _, _, lanes = m_ref.shape
    full, width = hidden_ref.shape[1], field_ref.shape[1]
    half, mid = width // 2, full // 2
    order = ring_order(ids[1])
    cuts = [(at, TILE) for at in range(0, mid, TILE)] + [(mid, half)]

    def product(side, k):
        cut = slice(cuts[k][0], sum(cuts[k]))
        high, low = (
            [
                ref[at + i * lanes : at + (i + 1) * lanes, cut]
                for ref in side
                for at in range(0, ref.shape[0], 2 * lanes)
            ]
            for i in range(2)
        )
        return dot(left_ref[...], jnp.concatenate(high + low + high, axis=0))

    oth_refs = [oth_ref]
    left_ref[...] = left3(jnp.concatenate([m_ref[t] for t in order], axis=1))
    near = [product(own_refs, k) for k in range(len(cuts) - 1)]
    for copy in copies:
        copy.wait()
    for k, (at, cols) in enumerate(cuts[:-1]):
        far = product(oth_refs, k)
        cut = slice(at, at + cols)
        sum_ref[:, cut] = hidden_ref[:, cut] + jnp.where(even, near[k], far)
        cut = slice(at + mid, at + mid + cols)
        sum_ref[:, cut] = hidden_ref[:, cut] + jnp.where(even, far, near[k])
    sum_ref[...] = normed(sum_ref[...], gain_ref[pl.ds(blk, 1), :])
    parts = [sum_ref[:, pl.ds(pl.multiple_of(t * lanes, lanes), lanes)] for t in order]
    left_ref[...] = left3(jnp.concatenate(parts, axis=1))
    near, far = product(own_refs, len(cuts) - 1), product(oth_refs, len(cuts) - 1)
    raw, shift = jnp.where(even, near, far), jnp.where(even, far, near)
    log_scale = jnp.tanh(raw)
    det_ref[...] = jnp.sum(log_scale, axis=1, keepdims=True)
    row = lax.broadcasted_iota(jnp.int32, (width, half), 0)
    put = jnp.where(row == perms_ref[pl.ds(blk, 1), half:], 1.0, 0.0).astype(bf16)
    log_scale, shift = select([log_scale, shift], put, (1, 1))
    out_ref[...] = field_ref[...] * jnp.exp(log_scale) + shift


def post(ids, mixed, own, oth, hidden, field, perms, gain):
    rows, width = field.shape
    full = hidden.shape[1]
    return call(
        post_kernel,
        [((rows, width), f32), ((rows, 1), f32)],
        ids,
        mixed,
        hidden,
        field,
        perms,
        gain,
        *own,
        *oth,
        scratch=[
            pltpu.VMEM((rows, 3 * full), bf16),
            pltpu.VMEM((rows, full), f32),
            pltpu.VMEM((2 * full, oth[0].shape[1]), bf16),
            pltpu.SemaphoreType.DMA((5,)),
        ],
        smem=1,
        left=5,
        limit=20,
        flops=4 << 30,
    )


def enter_kernel(emb_ref, gain_ref, w_query_ref, w_keyval_ref, q_ref, kv_ref):
    start = jnp.concatenate([emb_ref[t] for t in range(emb_ref.shape[0])], axis=1)
    unit = normed(start.astype(f32), gain_ref[...]).astype(bf16)
    kv_ref[...] = jnp.dot(unit, w_keyval_ref[...], preferred_element_type=f32).astype(bf16)
    q_ref[...] = jnp.dot(unit, w_query_ref[...], preferred_element_type=f32).astype(bf16)


def causal_kernel(ids, q_ref, order_ref, order_row_ref, w_ref, *refs):
    kv_refs, o_ref, s_ref = refs[:-2], refs[-2], refs[-1]
    rows = q_ref.shape[0]
    kv_refs = [
        ref.at[at : at + rows, :] for ref in kv_refs for at in range(0, ref.shape[0], rows)
    ]
    dh = q_ref.shape[1]
    patch = ids[1]
    own = order_row_ref[...] <= order_ref[...]
    top = None
    for j, kv_ref in enumerate(kv_refs):
        owner = ids[2 + j]
        s = lax.dot_general(
            q_ref[...], kv_ref[:, :dh], (((1,), (1,)), ((), ())), preferred_element_type=f32
        ) * (dh ** (-0.5))
        if j == 0:
            s = jnp.where(own, s, -jnp.inf)
        else:
            s = jnp.where(owner < patch, s, -jnp.inf)
        s_ref[j] = s
        m = jnp.max(s, axis=1, keepdims=True)
        top = m if top is None else jnp.maximum(top, m)
    total = acc = None
    for j, kv_ref in enumerate(kv_refs):
        p = jnp.exp(s_ref[j] - top)
        t = jnp.sum(p, axis=1, keepdims=True)
        a = jnp.dot(p.astype(bf16), kv_ref[:, dh:], preferred_element_type=f32)
        total = t if total is None else total + t
        acc = a if acc is None else acc + a
    attended = (acc / total).astype(bf16)
    for at in range(0, w_ref.shape[1], 512):
        o_ref[:, at : at + 512] = dot(attended, w_ref[:, at : at + 512]).astype(bf16)


def resid_kernel(ids, parts_ref, emb_ref, gain_ref, resid_ref, unit_ref):
    nt, part, _ = parts_ref.shape
    at = pl.ds(pl.multiple_of(ids[1] * part, part), part)
    start = jnp.concatenate([emb_ref[t, at, :] for t in range(nt)], axis=1).astype(f32)
    resid = start + sum(parts_ref[t].astype(f32) for t in range(nt))
    resid_ref[...] = resid
    unit = normed(resid, gain_ref[...]).astype(bf16)
    for t in range(nt):
        unit_ref[t] = unit


def mlp_kernel(
    ids, unit_ref, resid_ref, gate_ref, up_ref, down_ref, out_ref, inner_ref, sum_ref
):
    model, hidden = gate_ref.shape
    lanes, part = out_ref.shape[2], resid_ref.shape[0]
    unit = unit_ref.reshape(NT * part, model)

    def expand(at):
        cut = pl.ds(at, TILE)
        gate = dot(unit[...], gate_ref[:, cut])
        up = dot(unit[...], up_ref[:, cut])
        inner_ref[:, cut] = (jax.nn.gelu(gate, approximate=True) * up).astype(bf16)

    tiles(hidden // TILE, expand)
    mine = pl.ds(pl.multiple_of(ids[1] * part, part), part)

    def contract(at):
        cut = pl.ds(at, TILE)
        sum_ref[...] = dot(inner_ref[...], down_ref[:, cut])
        sum_ref[mine, :] = sum_ref[mine, :] + resid_ref[:, cut]
        out_ref[at // lanes] = sum_ref[...].astype(bf16)

    tiles(model // TILE, contract)


def in_hbm(value):
    return pltpu.with_memory_space_constraint(value, pltpu.HBM)


def tied(value, *others):
    return lax.optimization_barrier((value, *others))[0]


def on_device(
    patches,
    perms,
    w_in,
    gain_mix,
    w_qkv,
    w_mix,
    gain_out,
    w_head,
    order,
    w_embed,
    gain_attn,
    w_query,
    w_keyval,
    w_attn,
    gain_mlp,
    w_gate,
    w_up,
    w_down,
):
    rows = patches.shape[0]
    local_w = w_qkv.shape[3]
    where = lax.axis_index("tensor")
    patch = lax.axis_index("patch")
    core = patch % 2
    even = core == 0
    ids = jnp.stack([core, where, 0]).astype(jnp.int32)

    w_qkv = w_qkv.transpose(0, 2, 1, 3)
    w_in, w_qkv, w_mix, w_head, perms, gain_mix = map(
        in_hbm, (w_in, w_qkv, w_mix, w_head, perms, gain_mix)
    )
    halved = cut(ids, w_mix, w_head)
    own_weights = [halved[0], None]
    side_weights = [lax.ppermute(halved[0], "tensor", ACROSS), None]
    field = patches
    logdet = 0.0
    for blk in range(BLOCKS):
        at_blk = jnp.stack([core, where, blk]).astype(jnp.int32)
        hidden, query, keyval, other = pre(at_blk, field, perms, w_in, gain_mix, w_qkv)
        hd = local_w // 2
        got = over(other, CORE)
        query = jnp.concatenate([query, got[:, :hd]], axis=0)
        keyval = jnp.concatenate([keyval, got[:, hd:]], axis=0)
        own_w = spread(tied(own_weights[blk], keyval), side_weights[blk])
        oth_w = [in_hbm(over(w, CORE)) for w in own_w]
        pieces = gather_chips(keyval)
        state = attend(query, pieces[:4], [], False)
        state = attend(query, pieces[4:7], state, False)
        (out,) = attend(tied(query, own_w[1], own_w[2]), pieces[7:], state, True)
        back = over(out[rows:], CORE)
        front = out[:rows]
        mixed = jnp.concatenate(
            [jnp.where(even, front, back), jnp.where(even, back, front)], axis=1
        )
        mixed = exchange(jnp.broadcast_to(mixed, (NT,) + mixed.shape))
        if blk + 1 < BLOCKS:
            own_weights[blk + 1] = tied(halved[blk + 1], mixed)
            side_weights[blk + 1] = lax.ppermute(own_weights[blk + 1], "tensor", ACROSS)
        field, det = post(at_blk, mixed, own_w, oth_w, hidden, field, perms, gain_out)
        logdet = logdet + det[:, 0]
    embed_part = jnp.dot(field.astype(bf16), w_embed, preferred_element_type=f32).astype(bf16)
    embedded = exchange(jnp.broadcast_to(embed_part, (NT,) + embed_part.shape))
    query_dec, keyval = call(
        enter_kernel,
        [((rows, DH), bf16), ((rows, 2 * DH), bf16)],
        embedded,
        gain_attn[None],
        w_query,
        w_keyval,
        flops=1 << 30,
    )
    pieces = gather_chips(keyval)
    for first, last in ((0, 4), (4, 7), (7, 8)):
        pieces.append(over(jnp.concatenate(pieces[first:last], axis=0), CORE))

    y, x = patch // 4, (patch // 2) % 2
    owners = [core, patch]
    for dc in (0, 1):
        for dy, dx in ((0, 0), (-1, 0), (1, 0), (0, 1), (-1, 1), (1, 1), (2, 0), (2, 1)):
            owners.append((((y + dy) % 4) * 2 + (x + dx) % 2) * 2 + (core + dc) % 2)
    model_w = w_attn.shape[1]
    (partial_value,) = call(
        causal_kernel,
        [((rows, model_w), bf16)],
        jnp.stack(owners).astype(jnp.int32),
        query_dec,
        order[:, None],
        order[None],
        w_attn,
        *pieces,
        scratch=[pltpu.VMEM((NP, rows, rows), f32)],
        smem=1,
        flops=2 << 30,
    )
    part, cols = rows // NT, model_w // NT
    resid, unit = call(
        resid_kernel,
        [((part, model_w), f32), ((NT, part, model_w), bf16)],
        ids,
        exchange(partial_value.reshape(NT, part, model_w)),
        embedded,
        gain_mlp[None],
        smem=1,
    )
    (down,) = call(
        mlp_kernel,
        [((NT, rows, cols), bf16)],
        ids,
        exchange(unit),
        resid,
        w_gate,
        w_up,
        w_down,
        scratch=[
            pltpu.VMEM((rows, w_gate.shape[1]), bf16),
            pltpu.VMEM((rows, cols), f32),
        ],
        smem=1,
        limit=8,
        flops=4 << 30,
    )
    decoded = jnp.sum(exchange(down).astype(f32), axis=0).astype(bf16)
    return (decoded, logdet)


def solution(mesh):
    return jax.shard_map(
        on_device,
        mesh=mesh,
        in_specs=(
            P("patch", None),
            P(),
            P(),
            P(),
            P(None, None, None, "tensor"),
            P(None, "tensor", None),
            P(),
            P(None, "tensor", None),
            P("patch"),
            P(None, "tensor"),
            P(),
            P(None, "tensor"),
            P(),
            P("tensor", None),
            P(),
            P(None, "tensor"),
            P(None, "tensor"),
            P("tensor", None),
        ),
        out_specs=(P("patch", "tensor"), P("patch")),
        check_vma=False,
    )
```

```python
import functools

import jax
import jax.numpy as jnp
from jax import lax
from jax.experimental import pallas as pl
from jax.experimental.pallas import tpu as pltpu
from jax.sharding import PartitionSpec as P


BLOCKS = 2
DH = 256
NP = 16
NT = 8


bf16 = jnp.bfloat16
f32 = jnp.float32


def normed(value, gain):
    return value * lax.rsqrt(jnp.mean(value * value, axis=-1, keepdims=True) + 1e-06) * gain


CORE = [(i, i ^ 1) for i in range(NP)]


def hop(dy, dx):
    def to(i):
        y, x, c = i // 4, (i // 2) % 2, i % 2
        return ((y + dy) % 4 * 2 + (x + dx) % 2) * 2 + c

    return [(i, to(i)) for i in range(NP)]


UP, DOWN, SIDE = hop(1, 0), hop(-1, 0), hop(0, 1)


def over(value, pairs):
    return lax.ppermute(value, "patch", pairs)


def gather_chips(own):
    half = own.shape[0] // 2
    up = over(own, UP)
    down = over(own, DOWN)
    side = over(own, SIDE)
    side_up = over(side, UP)
    side_down = over(down, SIDE)
    far_a = over(up[:half], UP)
    far_b = over(down[half:], DOWN)
    far = jnp.concatenate([far_a, far_b], 0)
    side_far = over(far, SIDE)
    return [own, up, down, side, side_up, side_down, far, side_far]


def exchange(parts):
    return lax.all_to_all(parts, "tensor", 0, 0)


ACROSS = [(i, i ^ 1) for i in range(NT)]
RISE = [(i, (i + 2) % NT) for i in range(NT)]
FALL = [(i, (i - 2) % NT) for i in range(NT)]


def spread(own, side):
    rise, fall = (functools.partial(lax.ppermute, axis_name="tensor", perm=p) for p in (RISE, FALL))
    below, below_side = rise(own), rise(side)
    above = fall(side)
    above_own = fall(own)
    far, far_side = rise(below), fall(above)
    return [own, side, below, below_side, above_own, above, far, far_side]


RING = [(0, 0), (0, 1), (-1, 0), (-1, 1), (1, 0), (1, 1), (2, 0), (2, 1)]


def ring_order(where):
    z, x = where // 2, where % 2
    return [(z + dz + NT // 2) % (NT // 2) * 2 + (x + dx) % 2 for dz, dx in RING]


def split2(x):
    a = x.astype(bf16)
    b = (x - a.astype(f32)).astype(bf16)
    return a, b


def split3(x):
    a = x.astype(bf16)
    r = x - a.astype(f32)
    b = r.astype(bf16)
    c = (r - b.astype(f32)).astype(bf16)
    return a, b, c


def select(xs, one_hot, dims=(1, 0)):
    rows = xs[0].shape[0]
    parts = jnp.concatenate([part for x in xs for part in split3(x)], axis=0)
    dims = (((dims[0],), (dims[1],)), ((), ()))
    out = lax.dot_general(parts, one_hot, dims, preferred_element_type=f32)
    cut = [out[i * rows : (i + 1) * rows] for i in range(3 * len(xs))]
    return [(cut[3 * i + 2] + cut[3 * i + 1]) + cut[3 * i] for i in range(len(xs))]


def left6(x):
    a, b, c = split3(x)
    return jnp.concatenate([a, a, b, a, b, c], axis=1)


def right6(x):
    a, b, c = split3(x)
    return jnp.concatenate([a, b, a, c, b, a], axis=0)


def left3(x):
    a, b = split2(x)
    return jnp.concatenate([a, a, b], axis=1)


def dot(left, right):
    return jnp.dot(left, right, preferred_element_type=f32)


TILE = 256


def tiles(count, body):
    def step(i, carry):
        body(pl.multiple_of(i * TILE, TILE))
        return carry

    lax.fori_loop(0, count, step, 0)


VMEM = pl.BlockSpec(memory_space=pltpu.VMEM)
HBM = pl.BlockSpec(memory_space=pltpu.HBM)
ANY = pl.BlockSpec(memory_space=pl.ANY)
SMEM = pl.BlockSpec(memory_space=pltpu.SMEM)


def call(body, outs, *args, scratch=(), flops=0, limit=16, smem=0, left=0, kept=HBM):
    moved = sum(x.size * x.dtype.itemsize for x in args)
    return pl.pallas_call(
        body,
        in_specs=[SMEM] * smem + [VMEM] * (len(args) - smem - left) + [kept] * left,
        out_specs=[VMEM] * len(outs),
        out_shape=[jax.ShapeDtypeStruct(*o) for o in outs],
        scratch_shapes=list(scratch),
        compiler_params=pltpu.CompilerParams(vmem_limit_bytes=limit << 20),
        cost_estimate=pl.CostEstimate(flops=flops, bytes_accessed=moved, transcendentals=0),
    )(*args)


def cut_kernel(ids, mix_ref, head_ref, *refs):
    outs, (buf_ref, sems) = refs[:BLOCKS], refs[BLOCKS:]
    rows = buf_ref.shape[1]
    copies = []
    for blk in range(BLOCKS):
        at = 0
        for i, ref in enumerate((mix_ref, head_ref)):
            cols = ref.shape[2] // 2
            source = ref.at[blk, :, pl.ds(pl.multiple_of(ids[0] * cols, 128), cols)]
            copies.append(
                pltpu.make_async_copy(source, buf_ref.at[blk, :, at : at + cols], sems.at[blk, i])
            )
            at += cols
    for copy in copies:
        copy.start()
    for blk, out in enumerate(outs):
        copies[2 * blk].wait()
        copies[2 * blk + 1].wait()
        high, low = split2(buf_ref[blk])
        out[:rows, :] = high
        out[rows:, :] = low


def cut(ids, w_mix, w_head):
    rows, cols = w_mix.shape[1], (w_mix.shape[2] + w_head.shape[2]) // 2
    return pl.pallas_call(
        cut_kernel,
        in_specs=[SMEM, HBM, HBM],
        out_specs=[VMEM] * BLOCKS,
        out_shape=[jax.ShapeDtypeStruct((2 * rows, cols), bf16)] * BLOCKS,
        scratch_shapes=[
            pltpu.VMEM((BLOCKS, rows, cols), f32),
            pltpu.SemaphoreType.DMA((BLOCKS, 2)),
        ],
        compiler_params=pltpu.CompilerParams(vmem_limit_bytes=8 << 20),
        name="cut",
    )(ids, w_mix, w_head)


def pre_kernel(
    ids, field_ref, perms_all, gain_all, w_in_all, w_all,
    hidden_ref, q_ref, kv_ref, oth_ref,
    cond_ref, unit_ref, w_in_ref, w_ref, perms_ref, gain_ref, sems,
):
    blk = ids[2]
    copy_in = pltpu.make_async_copy(w_in_all.at[blk], w_in_ref, sems.at[0])
    copy_qkv = pltpu.make_async_copy(w_all.at[blk], w_ref, sems.at[1])
    copy_perms = pltpu.make_async_copy(perms_all, perms_ref, sems.at[2])
    copy_gain = pltpu.make_async_copy(gain_all, gain_ref, sems.at[3])
    for copy in (copy_perms, copy_in, copy_qkv, copy_gain):
        copy.start()
    even = ids[0] == 0
    half, full = w_in_ref.shape
    width = field_ref.shape[1]
    hd = w_ref.shape[2] // 2
    row = lax.broadcasted_iota(jnp.int32, (width, half), 0)
    copy_perms.wait()
    take = jnp.where(row == perms_ref[pl.ds(blk, 1), :half], 1.0, 0.0).astype(bf16)
    cond_ref[...] = left6(select([field_ref[...]], take)[0])
    copy_in.wait()

    def column(at):
        cut = pl.ds(at, TILE)
        hidden_ref[:, cut] = dot(cond_ref[...], right6(w_in_ref[:, cut]))

    tiles(full // TILE, column)
    copy_gain.wait()
    unit_ref[...] = left6(normed(hidden_ref[...], gain_ref[pl.ds(blk, 1), :]))
    copy_qkv.wait()
    qk = jnp.concatenate([w_ref[0], w_ref[1]], axis=1)
    qk = dot(unit_ref[...], right6(qk))
    v = dot(unit_ref[...], right6(w_ref[2]))
    q, k = qk[:, : 2 * hd], qk[:, 2 * hd :]

    def pick(x, first):
        return jnp.where(first, x[:, :hd], x[:, hd:])

    q_ref[...] = pick(q, even)
    kv_ref[...] = jnp.concatenate([pick(k, even), pick(v, even)], axis=1)
    odd = jnp.logical_not(even)
    oth_ref[...] = jnp.concatenate([pick(q, odd), pick(k, odd), pick(v, odd)], axis=1)


def pre(ids, field, perms, w_in, gain, w_qkv):
    rows, (half, full) = field.shape[0], w_in.shape[1:]
    hd = w_qkv.shape[3] // 2
    return call(
        pre_kernel,
        [((rows, full), f32), ((rows, hd), f32), ((rows, 2 * hd), f32), ((rows, 3 * hd), f32)],
        ids,
        field,
        perms,
        gain,
        w_in,
        w_qkv,
        scratch=[
            pltpu.VMEM((rows, 6 * half), bf16),
            pltpu.VMEM((rows, 6 * full), bf16),
            pltpu.VMEM(w_in.shape[1:], f32),
            pltpu.VMEM(w_qkv.shape[1:], f32),
            pltpu.VMEM(perms.shape, jnp.int32),
            pltpu.VMEM(gain.shape, f32),
            pltpu.SemaphoreType.DMA((4,)),
        ],
        smem=1,
        left=4,
        flops=3 << 30,
    )


def attend_kernel(count, first, last, q_ref, *refs):
    kv_refs, refs = refs[:count], refs[count:]
    if not first:
        (acc0_ref, stat0_ref), refs = refs[:2], refs[2:]
    rows, hd = q_ref.shape
    s_ref = refs[-1]
    block = s_ref.shape[1]

    def some_rows(i, carry):
        at = pl.ds(pl.multiple_of(i * block, block), block)
        q1, q2, q3 = split3(q_ref[at, :] * (hd ** (-0.5)))
        qs = jnp.concatenate([q1, q1, q2, q1, q2, q3], axis=1)
        top = None if first else stat0_ref[at, :1]
        for j, kv_ref in enumerate(kv_refs):
            k1, k2, k3 = split3(kv_ref[:, :hd])
            ks = jnp.concatenate([k1, k2, k1, k3, k2, k1], axis=1)
            s = lax.dot_general(qs, ks, (((1,), (1,)), ((), ())), preferred_element_type=f32)
            s_ref[j] = s
            m = jnp.max(s, axis=1, keepdims=True)
            top = m if top is None else jnp.maximum(top, m)
        total = acc = None
        if not first:
            factor = jnp.exp(stat0_ref[at, :1] - top)
            total, acc = stat0_ref[at, hd : hd + 1] * factor, acc0_ref[at, :] * factor
        for j, kv_ref in enumerate(kv_refs):
            p = jnp.exp(s_ref[j] - top)
            t = jnp.sum(p, axis=1, keepdims=True)
            v1, v2, v3 = split3(kv_ref[:, hd:])
            p1, p2 = split2(p)
            a = dot(p1, jnp.concatenate([v1, v2, v3], axis=1))
            b = dot(p2, jnp.concatenate([v1, v2], axis=1))
            a = a[:, :hd] + (a[:, hd : 2 * hd] + b[:, :hd]) + (a[:, 2 * hd :] + b[:, hd:])
            total = t if total is None else total + t
            acc = a if acc is None else acc + a
        if last:
            refs[0][at, :] = acc / total
        else:
            refs[0][at, :] = acc
            refs[1][at, :] = jnp.concatenate(
                [jnp.broadcast_to(top, (block, hd)), jnp.broadcast_to(total, (block, hd))], axis=1
            )
        return carry

    lax.fori_loop(0, rows // block, some_rows, 0)


def attend(query, pieces, state, last):
    rows, hd = query.shape
    keys = pieces[0].shape[0]
    count = len(pieces)
    outs = [((rows, hd), f32)] if last else [((rows, hd), f32), ((rows, 2 * hd), f32)]
    return call(
        functools.partial(attend_kernel, count, not state, last),
        outs,
        query,
        *pieces,
        *state,
        scratch=[pltpu.VMEM((count, 256, keys), f32)],
        flops=count << 30,
    )


def post_kernel(ids, m_ref, hidden_ref, field_ref, perms_ref, gain_ref, *refs):
    own_refs, far_refs, refs = refs[:NT], refs[NT : 2 * NT], refs[2 * NT :]
    out_ref, det_ref, left_ref, sum_ref, oth_ref, sems = refs
    copies, at = [], 0
    for j, far in enumerate(far_refs):
        target = oth_ref.at[at : at + far.shape[0], :]
        copies.append(pltpu.make_async_copy(far, target, sems.at[j]))
        at += far.shape[0]
    for copy in copies:
        copy.start()
    blk, even = ids[2], ids[0] == 0
    _, _, lanes = m_ref.shape
    full, width = hidden_ref.shape[1], field_ref.shape[1]
    half, mid = width // 2, full // 2
    order = ring_order(ids[1])
    cuts = [(at, TILE) for at in range(0, mid, TILE)] + [(mid, half)]

    def product(side, k):
        cut = slice(cuts[k][0], sum(cuts[k]))
        high, low = (
            [
                ref[at + i * lanes : at + (i + 1) * lanes, cut]
                for ref in side
                for at in range(0, ref.shape[0], 2 * lanes)
            ]
            for i in range(2)
        )
        return dot(left_ref[...], jnp.concatenate(high + low + high, axis=0))

    oth_refs = [oth_ref]
    left_ref[...] = left3(jnp.concatenate([m_ref[t] for t in order], axis=1))
    near = [product(own_refs, k) for k in range(len(cuts) - 1)]
    for copy in copies:
        copy.wait()
    for k, (at, cols) in enumerate(cuts[:-1]):
        far = product(oth_refs, k)
        cut = slice(at, at + cols)
        sum_ref[:, cut] = hidden_ref[:, cut] + jnp.where(even, near[k], far)
        cut = slice(at + mid, at + mid + cols)
        sum_ref[:, cut] = hidden_ref[:, cut] + jnp.where(even, far, near[k])
    sum_ref[...] = normed(sum_ref[...], gain_ref[pl.ds(blk, 1), :])
    parts = [sum_ref[:, pl.ds(pl.multiple_of(t * lanes, lanes), lanes)] for t in order]
    left_ref[...] = left3(jnp.concatenate(parts, axis=1))
    near, far = product(own_refs, len(cuts) - 1), product(oth_refs, len(cuts) - 1)
    raw, shift = jnp.where(even, near, far), jnp.where(even, far, near)
    log_scale = jnp.tanh(raw)
    det_ref[...] = jnp.sum(log_scale, axis=1, keepdims=True)
    row = lax.broadcasted_iota(jnp.int32, (width, half), 0)
    put = jnp.where(row == perms_ref[pl.ds(blk, 1), half:], 1.0, 0.0).astype(bf16)
    log_scale, shift = select([log_scale, shift], put, (1, 1))
    out_ref[...] = field_ref[...] * jnp.exp(log_scale) + shift


def post(ids, mixed, own, oth, hidden, field, perms, gain):
    rows, width = field.shape
    full = hidden.shape[1]
    return call(
        post_kernel,
        [((rows, width), f32), ((rows, 1), f32)],
        ids,
        mixed,
        hidden,
        field,
        perms,
        gain,
        *own,
        *oth,
        scratch=[
            pltpu.VMEM((rows, 3 * full), bf16),
            pltpu.VMEM((rows, full), f32),
            pltpu.VMEM((2 * full, oth[0].shape[1]), bf16),
            pltpu.SemaphoreType.DMA((NT,)),
        ],
        smem=1,
        left=NT,
        limit=20,
        flops=4 << 30,
    )


def enter_kernel(emb_ref, gain_ref, w_query_ref, w_keyval_ref, q_ref, kv_ref):
    start = jnp.concatenate([emb_ref[t] for t in range(emb_ref.shape[0])], axis=1)
    unit = normed(start.astype(f32), gain_ref[...]).astype(bf16)
    kv_ref[...] = jnp.dot(unit, w_keyval_ref[...], preferred_element_type=f32).astype(bf16)
    q_ref[...] = jnp.dot(unit, w_query_ref[...], preferred_element_type=f32).astype(bf16)


def causal_kernel(ids, q_ref, order_ref, order_row_ref, w_ref, *refs):
    kv_refs, o_ref, s_ref = refs[:-2], refs[-2], refs[-1]
    rows = q_ref.shape[0]
    kv_refs = [
        ref.at[at : at + rows, :] for ref in kv_refs for at in range(0, ref.shape[0], rows)
    ]
    dh = q_ref.shape[1]
    patch = ids[1]
    own = order_row_ref[...] <= order_ref[...]
    top = None
    for j, kv_ref in enumerate(kv_refs):
        owner = ids[2 + j]
        s = lax.dot_general(
            q_ref[...], kv_ref[:, :dh], (((1,), (1,)), ((), ())), preferred_element_type=f32
        ) * (dh ** (-0.5))
        if j == 0:
            s = jnp.where(own, s, -jnp.inf)
        else:
            s = jnp.where(owner < patch, s, -jnp.inf)
        s_ref[j] = s
        m = jnp.max(s, axis=1, keepdims=True)
        top = m if top is None else jnp.maximum(top, m)
    total = acc = None
    for j, kv_ref in enumerate(kv_refs):
        p = jnp.exp(s_ref[j] - top)
        t = jnp.sum(p, axis=1, keepdims=True)
        a = jnp.dot(p.astype(bf16), kv_ref[:, dh:], preferred_element_type=f32)
        total = t if total is None else total + t
        acc = a if acc is None else acc + a
    attended = (acc / total).astype(bf16)
    for at in range(0, w_ref.shape[1], 512):
        o_ref[:, at : at + 512] = dot(attended, w_ref[:, at : at + 512]).astype(bf16)


def resid_kernel(ids, parts_ref, emb_ref, gain_ref, resid_ref, unit_ref):
    nt, part, _ = parts_ref.shape
    at = pl.ds(pl.multiple_of(ids[1] * part, part), part)
    start = jnp.concatenate([emb_ref[t, at, :] for t in range(nt)], axis=1).astype(f32)
    resid = start + sum(parts_ref[t].astype(f32) for t in range(nt))
    resid_ref[...] = resid
    unit = normed(resid, gain_ref[...]).astype(bf16)
    for t in range(nt):
        unit_ref[t] = unit


def mlp_kernel(
    ids, unit_ref, resid_ref, gate_ref, up_ref, down_ref, out_ref, inner_ref, sum_ref
):
    model, hidden = gate_ref.shape
    lanes, part = out_ref.shape[2], resid_ref.shape[0]
    unit = unit_ref.reshape(NT * part, model)

    def expand(at):
        cut = pl.ds(at, TILE)
        gate = dot(unit[...], gate_ref[:, cut])
        up = dot(unit[...], up_ref[:, cut])
        inner_ref[:, cut] = (jax.nn.gelu(gate, approximate=True) * up).astype(bf16)

    tiles(hidden // TILE, expand)
    mine = pl.ds(pl.multiple_of(ids[1] * part, part), part)

    def contract(at):
        cut = pl.ds(at, TILE)
        sum_ref[...] = dot(inner_ref[...], down_ref[:, cut])
        sum_ref[mine, :] = sum_ref[mine, :] + resid_ref[:, cut]
        out_ref[at // lanes] = sum_ref[...].astype(bf16)

    tiles(model // TILE, contract)


def in_hbm(value):
    return pltpu.with_memory_space_constraint(value, pltpu.HBM)


def tied(value, *others):
    return lax.optimization_barrier((value, *others))[0]


def on_device(
    patches,
    perms,
    w_in,
    gain_mix,
    w_qkv,
    w_mix,
    gain_out,
    w_head,
    order,
    w_embed,
    gain_attn,
    w_query,
    w_keyval,
    w_attn,
    gain_mlp,
    w_gate,
    w_up,
    w_down,
):
    rows = patches.shape[0]
    local_w = w_qkv.shape[3]
    where = lax.axis_index("tensor")
    patch = lax.axis_index("patch")
    core = patch % 2
    even = core == 0
    ids = jnp.stack([core, where, 0]).astype(jnp.int32)

    w_qkv = w_qkv.transpose(0, 2, 1, 3)
    w_in, w_qkv, w_mix, w_head, perms, gain_mix = map(
        in_hbm, (w_in, w_qkv, w_mix, w_head, perms, gain_mix)
    )
    halved = cut(ids, w_mix, w_head)
    own_weights = [halved[0], None]
    side_weights = [lax.ppermute(halved[0], "tensor", ACROSS), None]
    field = patches
    logdet = 0.0
    for blk in range(BLOCKS):
        at_blk = jnp.stack([core, where, blk]).astype(jnp.int32)
        hidden, query, keyval, other = pre(at_blk, field, perms, w_in, gain_mix, w_qkv)
        hd = local_w // 2
        got = over(other, CORE)
        query = jnp.concatenate([query, got[:, :hd]], axis=0)
        keyval = jnp.concatenate([keyval, got[:, hd:]], axis=0)
        own_w = spread(tied(own_weights[blk], keyval), side_weights[blk])
        oth_w = [in_hbm(over(w, CORE)) for w in own_w]
        pieces = gather_chips(keyval)
        state = attend(query, pieces[:4], [], False)
        state = attend(query, pieces[4:7], state, False)
        (out,) = attend(query, pieces[7:], state, True)
        back = over(out[rows:], CORE)
        front = out[:rows]
        mixed = jnp.concatenate(
            [jnp.where(even, front, back), jnp.where(even, back, front)], axis=1
        )
        mixed = exchange(jnp.broadcast_to(mixed, (NT,) + mixed.shape))
        if blk + 1 < BLOCKS:
            own_weights[blk + 1] = tied(halved[blk + 1], mixed)
            side_weights[blk + 1] = lax.ppermute(own_weights[blk + 1], "tensor", ACROSS)
        field, det = post(at_blk, mixed, own_w, oth_w, hidden, field, perms, gain_out)
        logdet = logdet + det[:, 0]
    embed_part = jnp.dot(field.astype(bf16), w_embed, preferred_element_type=f32).astype(bf16)
    embedded = exchange(jnp.broadcast_to(embed_part, (NT,) + embed_part.shape))
    query_dec, keyval = call(
        enter_kernel,
        [((rows, DH), bf16), ((rows, 2 * DH), bf16)],
        embedded,
        gain_attn[None],
        w_query,
        w_keyval,
        flops=1 << 30,
    )
    pieces = gather_chips(keyval)
    pieces = pieces + [over(x, CORE) for x in pieces]

    y, x = patch // 4, (patch // 2) % 2
    owners = [core, patch]
    for dc in (0, 1):
        for dy, dx in ((0, 0), (-1, 0), (1, 0), (0, 1), (-1, 1), (1, 1), (2, 0), (2, 1)):
            owners.append((((y + dy) % 4) * 2 + (x + dx) % 2) * 2 + (core + dc) % 2)
    model_w = w_attn.shape[1]
    (partial_value,) = call(
        causal_kernel,
        [((rows, model_w), bf16)],
        jnp.stack(owners).astype(jnp.int32),
        query_dec,
        order[:, None],
        order[None],
        w_attn,
        *pieces,
        scratch=[pltpu.VMEM((NP, rows, rows), f32)],
        smem=1,
        flops=2 << 30,
    )
    part, cols = rows // NT, model_w // NT
    resid, unit = call(
        resid_kernel,
        [((part, model_w), f32), ((NT, part, model_w), bf16)],
        ids,
        exchange(partial_value.reshape(NT, part, model_w)),
        embedded,
        gain_mlp[None],
        smem=1,
    )
    (down,) = call(
        mlp_kernel,
        [((NT, rows, cols), bf16)],
        ids,
        exchange(unit),
        resid,
        w_gate,
        w_up,
        w_down,
        scratch=[
            pltpu.VMEM((rows, w_gate.shape[1]), bf16),
            pltpu.VMEM((rows, cols), f32),
        ],
        smem=1,
        limit=8,
        flops=4 << 30,
    )
    decoded = jnp.sum(exchange(down).astype(f32), axis=0).astype(bf16)
    return (decoded, logdet)


def solution(mesh):
    return jax.shard_map(
        on_device,
        mesh=mesh,
        in_specs=(
            P("patch", None),
            P(),
            P(),
            P(),
            P(None, None, None, "tensor"),
            P(None, "tensor", None),
            P(),
            P(None, "tensor", None),
            P("patch"),
            P(None, "tensor"),
            P(),
            P(None, "tensor"),
            P(),
            P("tensor", None),
            P(),
            P(None, "tensor"),
            P(None, "tensor"),
            P("tensor", None),
        ),
        out_specs=(P("patch", "tensor"), P("patch")),
        check_vma=False,
    )
```

```python
import functools

import jax
import jax.numpy as jnp
from jax import lax
from jax.experimental import pallas as pl
from jax.experimental.pallas import tpu as pltpu
from jax.sharding import PartitionSpec as P


BLOCKS = 2
DH = 256
NP = 16
NT = 8


bf16 = jnp.bfloat16
f32 = jnp.float32


def normed(value, gain):
    return value * lax.rsqrt(jnp.mean(value * value, axis=-1, keepdims=True) + 1e-06) * gain


CORE = [(i, i ^ 1) for i in range(NP)]


def hop(dy, dx):
    def to(i):
        y, x, c = i // 4, (i // 2) % 2, i % 2
        return ((y + dy) % 4 * 2 + (x + dx) % 2) * 2 + c

    return [(i, to(i)) for i in range(NP)]


UP, DOWN, SIDE = hop(1, 0), hop(-1, 0), hop(0, 1)


def over(value, pairs):
    return lax.ppermute(value, "patch", pairs)


def gather_chips(own):
    up = over(own, UP)
    down = over(own, DOWN)
    side = over(own, SIDE)
    side_up = over(side, UP)
    far = over(down, DOWN)
    side_down = over(down, SIDE)
    return [own, up, down, side, side_up, side_down, far, over(far, SIDE)]


def exchange(parts):
    return lax.all_to_all(parts, "tensor", 0, 0)


ACROSS = [(i, i ^ 1) for i in range(NT)]
RISE = [(i, (i + 2) % NT) for i in range(NT)]
FALL = [(i, (i - 2) % NT) for i in range(NT)]


def spread(own, side):
    rise, fall = (functools.partial(lax.ppermute, axis_name="tensor", perm=p) for p in (RISE, FALL))
    below, below_side = rise(own), rise(side)
    above = fall(side)
    above_own = fall(own)
    far, far_side = rise(below), fall(above)
    return [own, side, below, below_side, above_own, above, far, far_side]


RING = [(0, 0), (0, 1), (-1, 0), (-1, 1), (1, 0), (1, 1), (2, 0), (2, 1)]


def ring_order(where):
    z, x = where // 2, where % 2
    return [(z + dz + NT // 2) % (NT // 2) * 2 + (x + dx) % 2 for dz, dx in RING]


def split2(x):
    a = x.astype(bf16)
    b = (x - a.astype(f32)).astype(bf16)
    return a, b


def split3(x):
    a = x.astype(bf16)
    r = x - a.astype(f32)
    b = r.astype(bf16)
    c = (r - b.astype(f32)).astype(bf16)
    return a, b, c


def select(xs, one_hot, dims=(1, 0)):
    rows = xs[0].shape[0]
    parts = jnp.concatenate([part for x in xs for part in split3(x)], axis=0)
    dims = (((dims[0],), (dims[1],)), ((), ()))
    out = lax.dot_general(parts, one_hot, dims, preferred_element_type=f32)
    cut = [out[i * rows : (i + 1) * rows] for i in range(3 * len(xs))]
    return [(cut[3 * i + 2] + cut[3 * i + 1]) + cut[3 * i] for i in range(len(xs))]


def left6(x):
    a, b, c = split3(x)
    return jnp.concatenate([a, a, b, a, b, c], axis=1)


def right6(x):
    a, b, c = split3(x)
    return jnp.concatenate([a, b, a, c, b, a], axis=0)


def left3(x):
    a, b = split2(x)
    return jnp.concatenate([a, a, b], axis=1)


def right3(x):
    a, b = split2(x)
    return jnp.concatenate([a, b, a], axis=0)


def dot(left, right):
    return jnp.dot(left, right, preferred_element_type=f32)


TILE = 256


def tiles(count, body):
    def step(i, carry):
        body(pl.multiple_of(i * TILE, TILE))
        return carry

    lax.fori_loop(0, count, step, 0)


VMEM = pl.BlockSpec(memory_space=pltpu.VMEM)
HBM = pl.BlockSpec(memory_space=pltpu.HBM)
ANY = pl.BlockSpec(memory_space=pl.ANY)
SMEM = pl.BlockSpec(memory_space=pltpu.SMEM)


def call(body, outs, *args, scratch=(), flops=0, limit=16, smem=0, left=0, kept=HBM):
    moved = sum(x.size * x.dtype.itemsize for x in args)
    return pl.pallas_call(
        body,
        in_specs=[SMEM] * smem + [VMEM] * (len(args) - smem - left) + [kept] * left,
        out_specs=[VMEM] * len(outs),
        out_shape=[jax.ShapeDtypeStruct(*o) for o in outs],
        scratch_shapes=list(scratch),
        compiler_params=pltpu.CompilerParams(vmem_limit_bytes=limit << 20),
        cost_estimate=pl.CostEstimate(flops=flops, bytes_accessed=moved, transcendentals=0),
    )(*args)


def cut_kernel(ids, mix_ref, head_ref, out, buf_ref, sems):
    rows = buf_ref.shape[0]
    copies, at = [], 0
    for i, ref in enumerate((mix_ref, head_ref)):
        cols = ref.shape[2] // 2
        source = ref.at[ids[2], :, pl.ds(pl.multiple_of(ids[0] * cols, 128), cols)]
        copies.append(pltpu.make_async_copy(source, buf_ref.at[:, at : at + cols], sems.at[i]))
        at += cols
    for copy in copies:
        copy.start()
    for copy in copies:
        copy.wait()
    high, low = split2(buf_ref[...])
    out[:rows, :] = high
    out[rows:, :] = low


def cut(ids, w_mix, w_head):
    rows, cols = w_mix.shape[1], (w_mix.shape[2] + w_head.shape[2]) // 2
    return call(
        cut_kernel,
        [((2 * rows, cols), bf16)],
        ids,
        w_mix,
        w_head,
        scratch=[pltpu.VMEM((rows, cols), f32), pltpu.SemaphoreType.DMA((2,))],
        smem=1,
        left=2,
        limit=4,
    )[0]


def lay_kernel(ids, out_ref, back_ref, m_ref):
    even = ids[0] == 0
    front, back = out_ref[: m_ref.shape[1], :], back_ref[...]
    mixed = jnp.concatenate(
        [jnp.where(even, front, back), jnp.where(even, back, front)], axis=1
    )
    for t in range(m_ref.shape[0]):
        m_ref[t] = mixed


def pre_kernel(
    ids, field_ref, perms_all, gain_all, w_in_all, w_all,
    hidden_ref, q_ref, kv_ref, oth_ref,
    cond_ref, unit_ref, w_in_ref, w_ref, perms_ref, gain_ref, sems,
):
    blk = ids[2]
    copy_in = pltpu.make_async_copy(w_in_all.at[blk], w_in_ref, sems.at[0])
    copy_qkv = pltpu.make_async_copy(w_all.at[blk], w_ref, sems.at[1])
    copy_perms = pltpu.make_async_copy(perms_all, perms_ref, sems.at[2])
    copy_gain = pltpu.make_async_copy(gain_all, gain_ref, sems.at[3])
    for copy in (copy_perms, copy_in, copy_qkv, copy_gain):
        copy.start()
    even = ids[0] == 0
    half, full = w_in_ref.shape
    width = field_ref.shape[1]
    hd = w_ref.shape[2] // 2
    row = lax.broadcasted_iota(jnp.int32, (width, half), 0)
    copy_perms.wait()
    take = jnp.where(row == perms_ref[pl.ds(blk, 1), :half], 1.0, 0.0).astype(bf16)
    cond_ref[...] = left6(select([field_ref[...]], take)[0])
    copy_in.wait()

    def column(at):
        cut = pl.ds(at, TILE)
        hidden_ref[:, cut] = dot(cond_ref[...], right6(w_in_ref[:, cut]))

    tiles(full // TILE, column)
    copy_gain.wait()
    unit_ref[...] = left6(normed(hidden_ref[...], gain_ref[pl.ds(blk, 1), :]))
    copy_qkv.wait()
    qk = jnp.concatenate([w_ref[0], w_ref[1]], axis=1)
    qk = dot(unit_ref[...], right6(qk))
    v = dot(unit_ref[:, : 3 * full], right3(w_ref[2]))
    q, k = qk[:, : 2 * hd], qk[:, 2 * hd :]

    def pick(x, first):
        return jnp.where(first, x[:, :hd], x[:, hd:])

    q_ref[...] = pick(q, even)
    kv_ref[...] = jnp.concatenate([pick(k, even), pick(v, even)], axis=1)
    odd = jnp.logical_not(even)
    oth_ref[...] = jnp.concatenate([pick(q, odd), pick(k, odd), pick(v, odd)], axis=1)


def pre(ids, field, perms, w_in, gain, w_qkv):
    rows, (half, full) = field.shape[0], w_in.shape[1:]
    hd = w_qkv.shape[3] // 2
    return call(
        pre_kernel,
        [((rows, full), f32), ((rows, hd), f32), ((rows, 2 * hd), f32), ((rows, 3 * hd), f32)],
        ids,
        field,
        perms,
        gain,
        w_in,
        w_qkv,
        scratch=[
            pltpu.VMEM((rows, 6 * half), bf16),
            pltpu.VMEM((rows, 6 * full), bf16),
            pltpu.VMEM(w_in.shape[1:], f32),
            pltpu.VMEM(w_qkv.shape[1:], f32),
            pltpu.VMEM(perms.shape, jnp.int32),
            pltpu.VMEM(gain.shape, f32),
            pltpu.SemaphoreType.DMA((4,)),
        ],
        smem=1,
        left=4,
        flops=3 << 30,
    )


def attend_kernel(count, first, last, q_ref, *refs):
    kv_refs, refs = refs[:count], refs[count:]
    if not first:
        (acc0_ref, stat0_ref), refs = refs[:2], refs[2:]
    rows, hd = q_ref.shape
    s_ref = refs[-1]
    block = s_ref.shape[1]

    def some_rows(i, carry):
        at = pl.ds(pl.multiple_of(i * block, block), block)
        q1, q2, q3 = split3(q_ref[at, :] * (hd ** (-0.5)))
        qs = jnp.concatenate([q1, q1, q2, q1, q2, q3], axis=1)
        top = None if first else stat0_ref[at, :1]
        for j, kv_ref in enumerate(kv_refs):
            k1, k2, k3 = split3(kv_ref[:, :hd])
            ks = jnp.concatenate([k1, k2, k1, k3, k2, k1], axis=1)
            s = lax.dot_general(qs, ks, (((1,), (1,)), ((), ())), preferred_element_type=f32)
            s_ref[j] = s
            m = jnp.max(s, axis=1, keepdims=True)
            top = m if top is None else jnp.maximum(top, m)
        total = acc = None
        if not first:
            factor = jnp.exp(stat0_ref[at, :1] - top)
            total, acc = stat0_ref[at, hd : hd + 1] * factor, acc0_ref[at, :] * factor
        for j, kv_ref in enumerate(kv_refs):
            p = jnp.exp(s_ref[j] - top)
            t = jnp.sum(p, axis=1, keepdims=True)
            v1, v2, v3 = split3(kv_ref[:, hd:])
            p1, p2 = split2(p)
            a = dot(p1, jnp.concatenate([v1, v2, v3], axis=1))
            b = dot(p2, jnp.concatenate([v1, v2], axis=1))
            a = a[:, :hd] + (a[:, hd : 2 * hd] + b[:, :hd]) + (a[:, 2 * hd :] + b[:, hd:])
            total = t if total is None else total + t
            acc = a if acc is None else acc + a
        if last:
            refs[0][at, :] = acc / total
        else:
            refs[0][at, :] = acc
            refs[1][at, :] = jnp.concatenate(
                [jnp.broadcast_to(top, (block, hd)), jnp.broadcast_to(total, (block, hd))], axis=1
            )
        return carry

    lax.fori_loop(0, rows // block, some_rows, 0)


def attend(query, pieces, state, last):
    rows, hd = query.shape
    keys = pieces[0].shape[0]
    count = len(pieces)
    outs = [((rows, hd), f32)] if last else [((rows, hd), f32), ((rows, 2 * hd), f32)]
    return call(
        functools.partial(attend_kernel, count, not state, last),
        outs,
        query,
        *pieces,
        *state,
        scratch=[pltpu.VMEM((count, 256, keys), f32)],
        flops=count << 30,
    )


def post_kernel(ids, m_ref, perms_ref, gain_ref, *refs):
    own_refs, far_refs, refs = refs[:NT], refs[NT : 2 * NT], refs[2 * NT :]
    hidden_all, field_all, out_ref, det_ref, left_ref, sum_ref, field_ref, oth_ref, sems = refs
    copies, at = [pltpu.make_async_copy(hidden_all, sum_ref, sems.at[NT])], 0
    for j, far in enumerate(far_refs):
        target = oth_ref.at[at : at + far.shape[0], :]
        copies.append(pltpu.make_async_copy(far, target, sems.at[j]))
        at += far.shape[0]
    copy_field = pltpu.make_async_copy(field_all, field_ref, sems.at[NT + 1])
    for copy in (*copies, copy_field):
        copy.start()
    blk, even = ids[2], ids[0] == 0
    _, _, lanes = m_ref.shape
    full, width = sum_ref.shape[1], field_ref.shape[1]
    half, mid = width // 2, full // 2
    order = ring_order(ids[1])
    cuts = [(at, TILE) for at in range(0, mid, TILE)] + [(mid, half)]

    def right(side, k):
        cut = slice(cuts[k][0], sum(cuts[k]))
        high, low = (
            [
                ref[at + i * lanes : at + (i + 1) * lanes, cut]
                for ref in side
                for at in range(0, ref.shape[0], 2 * lanes)
            ]
            for i in range(2)
        )
        return jnp.concatenate(high + low + high, axis=0)

    def product(side, k):
        return dot(left_ref[...], right(side, k))

    oth_refs = [oth_ref]
    left_ref[...] = left3(jnp.concatenate([m_ref[t] for t in order], axis=1))
    near = [product(own_refs, k) for k in range(len(cuts) - 1)]
    for copy in copies:
        copy.wait()
    for k, (at, cols) in enumerate(cuts[:-1]):
        far = product(oth_refs, k)
        cut = slice(at, at + cols)
        sum_ref[:, cut] = sum_ref[:, cut] + jnp.where(even, near[k], far)
        cut = slice(at + mid, at + mid + cols)
        sum_ref[:, cut] = sum_ref[:, cut] + jnp.where(even, far, near[k])
    sum_ref[...] = normed(sum_ref[...], gain_ref[pl.ds(blk, 1), :])
    parts = [sum_ref[:, pl.ds(pl.multiple_of(t * lanes, lanes), lanes)] for t in order]
    left_ref[...] = left3(jnp.concatenate(parts, axis=1))
    k = len(cuts) - 1
    both = dot(left_ref[...], jnp.concatenate([right(own_refs, k), right(oth_refs, k)], axis=1))
    near, far = both[:, :half], both[:, half:]
    raw, shift = jnp.where(even, near, far), jnp.where(even, far, near)
    log_scale = jnp.tanh(raw)
    det_ref[...] = jnp.sum(log_scale, axis=1, keepdims=True)
    row = lax.broadcasted_iota(jnp.int32, (width, half), 0)
    put = jnp.where(row == perms_ref[pl.ds(blk, 1), half:], 1.0, 0.0).astype(bf16)
    log_scale, shift = select([log_scale, shift], put, (1, 1))
    copy_field.wait()
    out_ref[...] = field_ref[...] * jnp.exp(log_scale) + shift


def post(ids, mixed, own, oth, hidden, field, perms, gain):
    rows, width = field.shape
    full = hidden.shape[1]
    return call(
        post_kernel,
        [((rows, width), f32), ((rows, 1), f32)],
        ids,
        mixed,
        perms,
        gain,
        *own,
        *oth,
        in_hbm(hidden),
        in_hbm(field),
        scratch=[
            pltpu.VMEM((rows, 3 * full), bf16),
            pltpu.VMEM((rows, full), f32),
            pltpu.VMEM((rows, width), f32),
            pltpu.VMEM((2 * full, oth[0].shape[1]), bf16),
            pltpu.SemaphoreType.DMA((NT + 2,)),
        ],
        smem=1,
        left=NT + 2,
        limit=20,
        flops=4 << 30,
    )


def enter_kernel(emb_ref, gain_ref, w_query_ref, w_keyval_ref, q_ref, kv_ref):
    start = jnp.concatenate([emb_ref[t] for t in range(emb_ref.shape[0])], axis=1)
    unit = normed(start.astype(f32), gain_ref[...]).astype(bf16)
    kv_ref[...] = jnp.dot(unit, w_keyval_ref[...], preferred_element_type=f32).astype(bf16)
    q_ref[...] = jnp.dot(unit, w_query_ref[...], preferred_element_type=f32).astype(bf16)


def causal_kernel(ids, q_ref, order_ref, order_row_ref, *refs):
    kv_refs, (w_all, o_ref, s_ref, w_ref, sem) = refs[:-5], refs[-5:]
    copy_w = pltpu.make_async_copy(w_all, w_ref, sem)
    copy_w.start()
    rows = q_ref.shape[0]
    kv_refs = [
        ref.at[at : at + rows, :] for ref in kv_refs for at in range(0, ref.shape[0], rows)
    ]
    dh = q_ref.shape[1]
    patch = ids[1]
    own = order_row_ref[...] <= order_ref[...]
    top = None
    for j, kv_ref in enumerate(kv_refs):
        owner = ids[2 + j]
        s = lax.dot_general(
            q_ref[...], kv_ref[:, :dh], (((1,), (1,)), ((), ())), preferred_element_type=f32
        ) * (dh ** (-0.5))
        if j == 0:
            s = jnp.where(own, s, -jnp.inf)
        else:
            s = jnp.where(owner < patch, s, -jnp.inf)
        s_ref[j] = s
        m = jnp.max(s, axis=1, keepdims=True)
        top = m if top is None else jnp.maximum(top, m)
    total = acc = None
    for j, kv_ref in enumerate(kv_refs):
        p = jnp.exp(s_ref[j] - top)
        t = jnp.sum(p, axis=1, keepdims=True)
        a = jnp.dot(p.astype(bf16), kv_ref[:, dh:], preferred_element_type=f32)
        total = t if total is None else total + t
        acc = a if acc is None else acc + a
    attended = (acc / total).astype(bf16)
    copy_w.wait()
    for at in range(0, w_ref.shape[1], 512):
        o_ref[:, at : at + 512] = dot(attended, w_ref[:, at : at + 512]).astype(bf16)


def resid_kernel(ids, parts_ref, emb_ref, gain_ref, resid_ref, unit_ref):
    nt, part, _ = parts_ref.shape
    at = pl.ds(pl.multiple_of(ids[1] * part, part), part)
    start = jnp.concatenate([emb_ref[t, at, :] for t in range(nt)], axis=1).astype(f32)
    resid = start + sum(parts_ref[t].astype(f32) for t in range(nt))
    resid_ref[...] = resid
    unit = normed(resid, gain_ref[...]).astype(bf16)
    for t in range(nt):
        unit_ref[t] = unit


def mlp_kernel(
    ids, unit_ref, resid_ref, gate_ref, up_ref, down_ref, out_ref, inner_ref, sum_ref
):
    model, hidden = gate_ref.shape
    lanes, part = out_ref.shape[2], resid_ref.shape[0]
    unit = unit_ref.reshape(NT * part, model)

    def expand(at):
        cut = pl.ds(at, TILE)
        gate = dot(unit[...], gate_ref[:, cut])
        up = dot(unit[...], up_ref[:, cut])
        inner_ref[:, cut] = (jax.nn.gelu(gate, approximate=True) * up).astype(bf16)

    tiles(hidden // TILE, expand)
    mine = pl.ds(pl.multiple_of(ids[1] * part, part), part)

    def contract(at):
        cut = pl.ds(at, TILE)
        sum_ref[...] = dot(inner_ref[...], down_ref[:, cut])
        sum_ref[mine, :] = sum_ref[mine, :] + resid_ref[:, cut]
        out_ref[at // lanes] = sum_ref[...].astype(bf16)

    tiles(model // TILE, contract)


def in_hbm(value):
    return pltpu.with_memory_space_constraint(value, pltpu.HBM)


def tied(value, *others):
    return lax.optimization_barrier((value, *others))[0]


def on_device(
    patches,
    perms,
    w_in,
    gain_mix,
    w_qkv,
    w_mix,
    gain_out,
    w_head,
    order,
    w_embed,
    gain_attn,
    w_query,
    w_keyval,
    w_attn,
    gain_mlp,
    w_gate,
    w_up,
    w_down,
):
    rows = patches.shape[0]
    local_w = w_qkv.shape[3]
    where = lax.axis_index("tensor")
    patch = lax.axis_index("patch")
    core = patch % 2
    ids = jnp.stack([core, where, 0]).astype(jnp.int32)

    w_qkv = w_qkv.transpose(0, 2, 1, 3)
    w_in, w_qkv, w_mix, w_head, perms, gain_mix = map(
        in_hbm, (w_in, w_qkv, w_mix, w_head, perms, gain_mix)
    )
    own_weights = [cut(ids, w_mix, w_head), None]
    side_weights = [lax.ppermute(own_weights[0], "tensor", ACROSS), None]
    field = patches
    logdet = 0.0
    for blk in range(BLOCKS):
        at_blk = jnp.stack([core, where, blk]).astype(jnp.int32)
        hidden, query, keyval, other = pre(at_blk, field, perms, w_in, gain_mix, w_qkv)
        hd = local_w // 2
        got = over(other, CORE)
        query = jnp.concatenate([query, got[:, :hd]], axis=0)
        keyval = jnp.concatenate([keyval, got[:, hd:]], axis=0)
        own_w = spread(tied(own_weights[blk], keyval), side_weights[blk])
        oth_w = [in_hbm(over(w, CORE)) for w in own_w]
        pieces = gather_chips(keyval)
        state = attend(query, pieces[:4], [], False)
        state = attend(query, pieces[4:7], state, False)
        (out,) = attend(query, pieces[7:], state, True)
        back = over(out[rows:], CORE)
        (mixed,) = call(lay_kernel, [((NT, rows, local_w), f32)], ids, out, back, smem=1, limit=4)
        mixed = exchange(mixed)
        if blk + 1 < BLOCKS:
            next_blk = tied(jnp.stack([core, where, blk + 1]).astype(jnp.int32), out)
            own_weights[blk + 1] = tied(cut(next_blk, w_mix, w_head), mixed)
            side_weights[blk + 1] = lax.ppermute(own_weights[blk + 1], "tensor", ACROSS)
        field, det = post(at_blk, mixed, own_w, oth_w, hidden, field, perms, gain_out)
        logdet = logdet + det[:, 0]
    embed_part = jnp.dot(field.astype(bf16), w_embed, preferred_element_type=f32).astype(bf16)
    embedded = exchange(jnp.broadcast_to(embed_part, (NT,) + embed_part.shape))
    query_dec, keyval = call(
        enter_kernel,
        [((rows, DH), bf16), ((rows, 2 * DH), bf16)],
        embedded,
        gain_attn[None],
        w_query,
        w_keyval,
        flops=1 << 30,
    )
    pieces = gather_chips(keyval)
    pieces = pieces + [over(x, CORE) for x in pieces]

    y, x = patch // 4, (patch // 2) % 2
    owners = [core, patch]
    for dc in (0, 1):
        for dy, dx in ((0, 0), (-1, 0), (1, 0), (0, 1), (-1, 1), (1, 1), (2, 0), (2, 1)):
            owners.append((((y + dy) % 4) * 2 + (x + dx) % 2) * 2 + (core + dc) % 2)
    model_w = w_attn.shape[1]
    (partial_value,) = call(
        causal_kernel,
        [((rows, model_w), bf16)],
        jnp.stack(owners).astype(jnp.int32),
        query_dec,
        order[:, None],
        order[None],
        *pieces,
        in_hbm(w_attn),
        scratch=[
            pltpu.VMEM((NP, rows, rows), f32),
            pltpu.VMEM(w_attn.shape, bf16),
            pltpu.SemaphoreType.DMA,
        ],
        smem=1,
        left=1,
        flops=2 << 30,
    )
    part, cols = rows // NT, model_w // NT
    resid, unit = call(
        resid_kernel,
        [((part, model_w), f32), ((NT, part, model_w), bf16)],
        ids,
        exchange(partial_value.reshape(NT, part, model_w)),
        embedded,
        gain_mlp[None],
        smem=1,
    )
    (down,) = call(
        mlp_kernel,
        [((NT, rows, cols), bf16)],
        ids,
        exchange(unit),
        resid,
        w_gate,
        w_up,
        w_down,
        scratch=[
            pltpu.VMEM((rows, w_gate.shape[1]), bf16),
            pltpu.VMEM((rows, cols), f32),
        ],
        smem=1,
        limit=8,
        flops=4 << 30,
    )
    decoded = jnp.sum(exchange(down).astype(f32), axis=0).astype(bf16)
    return (decoded, logdet)


def solution(mesh):
    return jax.shard_map(
        on_device,
        mesh=mesh,
        in_specs=(
            P("patch", None),
            P(),
            P(),
            P(),
            P(None, None, None, "tensor"),
            P(None, "tensor", None),
            P(),
            P(None, "tensor", None),
            P("patch"),
            P(None, "tensor"),
            P(),
            P(None, "tensor"),
            P(),
            P("tensor", None),
            P(),
            P(None, "tensor"),
            P(None, "tensor"),
            P("tensor", None),
        ),
        out_specs=(P("patch", "tensor"), P("patch")),
        check_vma=False,
    )
```

```python
import functools

import jax
import jax.numpy as jnp
from jax import lax
from jax.experimental import pallas as pl
from jax.experimental.pallas import tpu as pltpu
from jax.sharding import PartitionSpec as P


BLOCKS = 2
DH = 256
NP = 16
NT = 8


bf16 = jnp.bfloat16
f32 = jnp.float32


def normed(value, gain):
    return value * lax.rsqrt(jnp.mean(value * value, axis=-1, keepdims=True) + 1e-06) * gain


CORE = [(i, i ^ 1) for i in range(NP)]


def hop(dy, dx):
    def to(i):
        y, x, c = i // 4, (i // 2) % 2, i % 2
        return ((y + dy) % 4 * 2 + (x + dx) % 2) * 2 + c

    return [(i, to(i)) for i in range(NP)]


UP, DOWN, SIDE = hop(1, 0), hop(-1, 0), hop(0, 1)


def over(value, pairs):
    return lax.ppermute(value, "patch", pairs)


def gather_chips(own, halves):
    up = over(own, UP)
    down = over(own, DOWN)
    side = over(own, SIDE)
    side_up = over(side, UP)
    side_down = over(down, SIDE)
    if halves:
        half = own.shape[0] // 2
        far = jnp.concatenate([over(up[:half], UP), over(down[half:], DOWN)], 0)
    else:
        far = over(down, DOWN)
    return [own, up, down, side, side_up, side_down, far, over(far, SIDE)]


def exchange(parts):
    return lax.all_to_all(parts, "tensor", 0, 0)


ACROSS = [(i, i ^ 1) for i in range(NT)]
RISE = [(i, (i + 2) % NT) for i in range(NT)]
FALL = [(i, (i - 2) % NT) for i in range(NT)]


def spread(own, side):
    rise, fall = (functools.partial(lax.ppermute, axis_name="tensor", perm=p) for p in (RISE, FALL))
    below = rise(own)
    above = fall(side)
    below_side = rise(side)
    above_own = fall(own)
    far = rise(below)
    far_side = fall(above)
    return [own, side, below, below_side, above_own, above, far, far_side]


RING = [(0, 0), (0, 1), (-1, 0), (-1, 1), (1, 0), (1, 1), (2, 0), (2, 1)]


def ring_order(where):
    z, x = where // 2, where % 2
    return [(z + dz + NT // 2) % (NT // 2) * 2 + (x + dx) % 2 for dz, dx in RING]


def split2(x):
    a = x.astype(bf16)
    b = (x - a.astype(f32)).astype(bf16)
    return a, b


def split3(x):
    a = x.astype(bf16)
    r = x - a.astype(f32)
    b = r.astype(bf16)
    c = (r - b.astype(f32)).astype(bf16)
    return a, b, c


def select(xs, one_hot, dims=(1, 0)):
    rows = xs[0].shape[0]
    parts = jnp.concatenate([part for x in xs for part in split3(x)], axis=0)
    dims = (((dims[0],), (dims[1],)), ((), ()))
    out = lax.dot_general(parts, one_hot, dims, preferred_element_type=f32)
    cut = [out[i * rows : (i + 1) * rows] for i in range(3 * len(xs))]
    return [(cut[3 * i + 2] + cut[3 * i + 1]) + cut[3 * i] for i in range(len(xs))]


def left6(x):
    a, b, c = split3(x)
    return jnp.concatenate([a, a, b, a, b, c], axis=1)


def right6(x):
    a, b, c = split3(x)
    return jnp.concatenate([a, b, a, c, b, a], axis=0)


def left3(x):
    a, b = split2(x)
    return jnp.concatenate([a, a, b], axis=1)


def right3(x):
    a, b = split2(x)
    return jnp.concatenate([a, b, a], axis=0)


def dot(left, right):
    return jnp.dot(left, right, preferred_element_type=f32)


TILE = 256


def tiles(count, body):
    def step(i, carry):
        body(pl.multiple_of(i * TILE, TILE))
        return carry

    lax.fori_loop(0, count, step, 0)


VMEM = pl.BlockSpec(memory_space=pltpu.VMEM)
HBM = pl.BlockSpec(memory_space=pltpu.HBM)
ANY = pl.BlockSpec(memory_space=pl.ANY)
SMEM = pl.BlockSpec(memory_space=pltpu.SMEM)


def call(body, outs, *args, scratch=(), flops=0, limit=16, smem=0, left=0, kept=HBM):
    moved = sum(x.size * x.dtype.itemsize for x in args)
    return pl.pallas_call(
        body,
        in_specs=[SMEM] * smem + [VMEM] * (len(args) - smem - left) + [kept] * left,
        out_specs=[VMEM] * len(outs),
        out_shape=[jax.ShapeDtypeStruct(*o) for o in outs],
        scratch_shapes=list(scratch),
        compiler_params=pltpu.CompilerParams(vmem_limit_bytes=limit << 20),
        cost_estimate=pl.CostEstimate(flops=flops, bytes_accessed=moved, transcendentals=0),
    )(*args)


def cut_kernel(ids, mix_ref, head_ref, out, buf_ref, sems):
    rows = buf_ref.shape[0]
    copies, at = [], 0
    for i, ref in enumerate((mix_ref, head_ref)):
        cols = ref.shape[2] // 2
        source = ref.at[ids[2], :, pl.ds(pl.multiple_of(ids[0] * cols, 128), cols)]
        copies.append(pltpu.make_async_copy(source, buf_ref.at[:, at : at + cols], sems.at[i]))
        at += cols
    for copy in copies:
        copy.start()
    for copy in copies:
        copy.wait()
    high, low = split2(buf_ref[...])
    out[:rows, :] = high
    out[rows:, :] = low


def cut(ids, w_mix, w_head):
    rows, cols = w_mix.shape[1], (w_mix.shape[2] + w_head.shape[2]) // 2
    return call(
        cut_kernel,
        [((2 * rows, cols), bf16)],
        ids,
        w_mix,
        w_head,
        scratch=[pltpu.VMEM((rows, cols), f32), pltpu.SemaphoreType.DMA((2,))],
        smem=1,
        left=2,
        limit=4,
    )[0]


def pre_kernel(
    ids, field_ref, perms_all, gain_all, w_in_all, w_all,
    hidden_ref, q_ref, kv_ref, oth_ref,
    cond_ref, unit_ref, w_in_ref, w_ref, perms_ref, gain_ref, sems,
):
    blk = ids[2]
    copy_in = pltpu.make_async_copy(w_in_all.at[blk], w_in_ref, sems.at[0])
    copy_qkv = pltpu.make_async_copy(w_all.at[blk], w_ref, sems.at[1])
    copy_perms = pltpu.make_async_copy(perms_all, perms_ref, sems.at[2])
    copy_gain = pltpu.make_async_copy(gain_all, gain_ref, sems.at[3])
    for copy in (copy_perms, copy_in, copy_qkv, copy_gain):
        copy.start()
    even = ids[0] == 0
    half, full = w_in_ref.shape
    width = field_ref.shape[1]
    hd = w_ref.shape[2] // 2
    row = lax.broadcasted_iota(jnp.int32, (width, half), 0)
    copy_perms.wait()
    take = jnp.where(row == perms_ref[pl.ds(blk, 1), :half], 1.0, 0.0).astype(bf16)
    cond_ref[...] = left6(select([field_ref[...]], take)[0])
    copy_in.wait()

    def column(at):
        cut = pl.ds(at, TILE)
        hidden_ref[:, cut] = dot(cond_ref[...], right6(w_in_ref[:, cut]))

    tiles(full // TILE, column)
    copy_gain.wait()
    unit_ref[...] = left6(normed(hidden_ref[...], gain_ref[pl.ds(blk, 1), :]))
    copy_qkv.wait()
    qk = jnp.concatenate([w_ref[0], w_ref[1]], axis=1)
    qk = dot(unit_ref[...], right6(qk))
    v = dot(unit_ref[:, : 3 * full], right3(w_ref[2]))
    q, k = qk[:, : 2 * hd], qk[:, 2 * hd :]

    def pick(x, first):
        return jnp.where(first, x[:, :hd], x[:, hd:])

    q_ref[...] = pick(q, even)
    kv_ref[...] = jnp.concatenate([pick(k, even), pick(v, even)], axis=1)
    odd = jnp.logical_not(even)
    oth_ref[...] = jnp.concatenate([pick(q, odd), pick(k, odd), pick(v, odd)], axis=1)


def pre(ids, field, perms, w_in, gain, w_qkv):
    rows, (half, full) = field.shape[0], w_in.shape[1:]
    hd = w_qkv.shape[3] // 2
    return call(
        pre_kernel,
        [((rows, full), f32), ((rows, hd), f32), ((rows, 2 * hd), f32), ((rows, 3 * hd), f32)],
        ids,
        field,
        perms,
        gain,
        w_in,
        w_qkv,
        scratch=[
            pltpu.VMEM((rows, 6 * half), bf16),
            pltpu.VMEM((rows, 6 * full), bf16),
            pltpu.VMEM(w_in.shape[1:], f32),
            pltpu.VMEM(w_qkv.shape[1:], f32),
            pltpu.VMEM(perms.shape, jnp.int32),
            pltpu.VMEM(gain.shape, f32),
            pltpu.SemaphoreType.DMA((4,)),
        ],
        smem=1,
        left=4,
        flops=3 << 30,
    )


def attend_kernel(count, first, last, q_ref, *refs):
    kv_refs, refs = refs[:count], refs[count:]
    if not first:
        (acc0_ref, stat0_ref), refs = refs[:2], refs[2:]
    rows, hd = q_ref.shape
    s_ref = refs[-1]
    block = s_ref.shape[1]

    def some_rows(i, carry):
        at = pl.ds(pl.multiple_of(i * block, block), block)
        q1, q2, q3 = split3(q_ref[at, :] * (hd ** (-0.5)))
        qs = jnp.concatenate([q1, q1, q2, q1, q2, q3], axis=1)
        top = None if first else stat0_ref[at, :1]
        for j, kv_ref in enumerate(kv_refs):
            k1, k2, k3 = split3(kv_ref[:, :hd])
            ks = jnp.concatenate([k1, k2, k1, k3, k2, k1], axis=1)
            s = lax.dot_general(qs, ks, (((1,), (1,)), ((), ())), preferred_element_type=f32)
            s_ref[j] = s
            m = jnp.max(s, axis=1, keepdims=True)
            top = m if top is None else jnp.maximum(top, m)
        total = acc = None
        if not first:
            factor = jnp.exp(stat0_ref[at, :1] - top)
            total, acc = stat0_ref[at, hd : hd + 1] * factor, acc0_ref[at, :] * factor
        for j, kv_ref in enumerate(kv_refs):
            p = jnp.exp(s_ref[j] - top)
            t = jnp.sum(p, axis=1, keepdims=True)
            v1, v2, v3 = split3(kv_ref[:, hd:])
            p1, p2 = split2(p)
            a = dot(p1, jnp.concatenate([v1, v2, v3], axis=1))
            b = dot(p2, jnp.concatenate([v1, v2], axis=1))
            a = a[:, :hd] + (a[:, hd : 2 * hd] + b[:, :hd]) + (a[:, 2 * hd :] + b[:, hd:])
            total = t if total is None else total + t
            acc = a if acc is None else acc + a
        if last:
            refs[0][at, :] = acc / total
        else:
            refs[0][at, :] = acc
            refs[1][at, :] = jnp.concatenate(
                [jnp.broadcast_to(top, (block, hd)), jnp.broadcast_to(total, (block, hd))], axis=1
            )
        return carry

    lax.fori_loop(0, rows // block, some_rows, 0)


def attend(query, pieces, state, last):
    rows, hd = query.shape
    keys = pieces[0].shape[0]
    count = len(pieces)
    outs = [((rows, hd), f32)] if last else [((rows, hd), f32), ((rows, 2 * hd), f32)]
    return call(
        functools.partial(attend_kernel, count, not state, last),
        outs,
        query,
        *pieces,
        *state,
        scratch=[pltpu.VMEM((count, 256, keys), f32)],
        flops=count << 30,
    )


def post_kernel(ids, m_ref, perms_ref, gain_ref, *refs):
    own_refs, far_refs, refs = refs[:NT], refs[NT : 2 * NT], refs[2 * NT :]
    hidden_all, field_all, out_ref, det_ref, left_ref, sum_ref, field_ref, oth_ref, sems = refs
    copies, at = [pltpu.make_async_copy(hidden_all, sum_ref, sems.at[NT])], 0
    for j, far in enumerate(far_refs):
        target = oth_ref.at[at : at + far.shape[0], :]
        copies.append(pltpu.make_async_copy(far, target, sems.at[j]))
        at += far.shape[0]
    copy_field = pltpu.make_async_copy(field_all, field_ref, sems.at[NT + 1])
    for copy in (*copies, copy_field):
        copy.start()
    blk, even = ids[2], ids[0] == 0
    _, _, lanes = m_ref.shape
    full, width = sum_ref.shape[1], field_ref.shape[1]
    half, mid = width // 2, full // 2
    order = ring_order(ids[1])
    cuts = [(at, TILE) for at in range(0, mid, TILE)] + [(mid, half)]

    def right(side, k):
        cut = slice(cuts[k][0], sum(cuts[k]))
        high, low = (
            [
                ref[at + i * lanes : at + (i + 1) * lanes, cut]
                for ref in side
                for at in range(0, ref.shape[0], 2 * lanes)
            ]
            for i in range(2)
        )
        return jnp.concatenate(high + low + high, axis=0)

    def product(side, k):
        return dot(left_ref[...], right(side, k))

    oth_refs = [oth_ref]
    left_ref[...] = left3(jnp.concatenate([m_ref[t] for t in order], axis=1))
    near = [product(own_refs, k) for k in range(len(cuts) - 1)]
    for copy in copies:
        copy.wait()
    for k, (at, cols) in enumerate(cuts[:-1]):
        far = product(oth_refs, k)
        cut = slice(at, at + cols)
        sum_ref[:, cut] = sum_ref[:, cut] + jnp.where(even, near[k], far)
        cut = slice(at + mid, at + mid + cols)
        sum_ref[:, cut] = sum_ref[:, cut] + jnp.where(even, far, near[k])
    sum_ref[...] = normed(sum_ref[...], gain_ref[pl.ds(blk, 1), :])
    parts = [sum_ref[:, pl.ds(pl.multiple_of(t * lanes, lanes), lanes)] for t in order]
    left_ref[...] = left3(jnp.concatenate(parts, axis=1))
    k = len(cuts) - 1
    both = dot(left_ref[...], jnp.concatenate([right(own_refs, k), right(oth_refs, k)], axis=1))
    near, far = both[:, :half], both[:, half:]
    raw, shift = jnp.where(even, near, far), jnp.where(even, far, near)
    log_scale = jnp.tanh(raw)
    det_ref[...] = jnp.sum(log_scale, axis=1, keepdims=True)
    row = lax.broadcasted_iota(jnp.int32, (width, half), 0)
    put = jnp.where(row == perms_ref[pl.ds(blk, 1), half:], 1.0, 0.0).astype(bf16)
    log_scale, shift = select([log_scale, shift], put, (1, 1))
    copy_field.wait()
    out_ref[...] = field_ref[...] * jnp.exp(log_scale) + shift


def post(ids, mixed, own, oth, hidden, field, perms, gain):
    rows, width = field.shape
    full = hidden.shape[1]
    return call(
        post_kernel,
        [((rows, width), f32), ((rows, 1), f32)],
        ids,
        mixed,
        perms,
        gain,
        *own,
        *oth,
        in_hbm(hidden),
        in_hbm(field),
        scratch=[
            pltpu.VMEM((rows, 3 * full), bf16),
            pltpu.VMEM((rows, full), f32),
            pltpu.VMEM((rows, width), f32),
            pltpu.VMEM((2 * full, oth[0].shape[1]), bf16),
            pltpu.SemaphoreType.DMA((NT + 2,)),
        ],
        smem=1,
        left=NT + 2,
        limit=20,
        flops=4 << 30,
    )


def enter_kernel(emb_ref, gain_ref, w_query_ref, w_keyval_ref, q_ref, kv_ref):
    start = jnp.concatenate([emb_ref[t] for t in range(emb_ref.shape[0])], axis=1)
    unit = normed(start.astype(f32), gain_ref[...]).astype(bf16)
    kv_ref[...] = jnp.dot(unit, w_keyval_ref[...], preferred_element_type=f32).astype(bf16)
    q_ref[...] = jnp.dot(unit, w_query_ref[...], preferred_element_type=f32).astype(bf16)


def causal_kernel(ids, q_ref, order_ref, order_row_ref, *refs):
    kv_refs, (w_all, o_ref, s_ref, w_ref, sem) = refs[:-5], refs[-5:]
    copy_w = pltpu.make_async_copy(w_all, w_ref, sem)
    copy_w.start()
    rows = q_ref.shape[0]
    kv_refs = [
        ref.at[at : at + rows, :] for ref in kv_refs for at in range(0, ref.shape[0], rows)
    ]
    dh = q_ref.shape[1]
    patch = ids[1]
    own = order_row_ref[...] <= order_ref[...]
    top = None
    for j, kv_ref in enumerate(kv_refs):
        owner = ids[2 + j]
        s = lax.dot_general(
            q_ref[...], kv_ref[:, :dh], (((1,), (1,)), ((), ())), preferred_element_type=f32
        ) * (dh ** (-0.5))
        if j == 0:
            s = jnp.where(own, s, -jnp.inf)
        else:
            s = jnp.where(owner < patch, s, -jnp.inf)
        s_ref[j] = s
        m = jnp.max(s, axis=1, keepdims=True)
        top = m if top is None else jnp.maximum(top, m)
    total = acc = None
    for j, kv_ref in enumerate(kv_refs):
        p = jnp.exp(s_ref[j] - top)
        t = jnp.sum(p, axis=1, keepdims=True)
        a = jnp.dot(p.astype(bf16), kv_ref[:, dh:], preferred_element_type=f32)
        total = t if total is None else total + t
        acc = a if acc is None else acc + a
    attended = (acc / total).astype(bf16)
    copy_w.wait()
    for at in range(0, w_ref.shape[1], 512):
        o_ref[:, at : at + 512] = dot(attended, w_ref[:, at : at + 512]).astype(bf16)


def resid_kernel(ids, parts_ref, emb_ref, gain_ref, resid_ref, unit_ref):
    nt, part, _ = parts_ref.shape
    at = pl.ds(pl.multiple_of(ids[1] * part, part), part)
    start = jnp.concatenate([emb_ref[t, at, :] for t in range(nt)], axis=1).astype(f32)
    resid = start + sum(parts_ref[t].astype(f32) for t in range(nt))
    resid_ref[...] = resid
    unit = normed(resid, gain_ref[...]).astype(bf16)
    for t in range(nt):
        unit_ref[t] = unit


def mlp_kernel(
    ids, unit_ref, resid_ref, gate_ref, up_ref, down_ref, out_ref, inner_ref, sum_ref
):
    model, hidden = gate_ref.shape
    lanes, part = out_ref.shape[2], resid_ref.shape[0]
    unit = unit_ref.reshape(NT * part, model)

    def expand(at):
        cut = pl.ds(at, TILE)
        gate = dot(unit[...], gate_ref[:, cut])
        up = dot(unit[...], up_ref[:, cut])
        inner_ref[:, cut] = (jax.nn.gelu(gate, approximate=True) * up).astype(bf16)

    tiles(hidden // TILE, expand)
    mine = pl.ds(pl.multiple_of(ids[1] * part, part), part)

    def contract(at):
        cut = pl.ds(at, TILE)
        sum_ref[...] = dot(inner_ref[...], down_ref[:, cut])
        sum_ref[mine, :] = sum_ref[mine, :] + resid_ref[:, cut]
        out_ref[at // lanes] = sum_ref[...].astype(bf16)

    tiles(model // TILE, contract)


def in_hbm(value):
    return pltpu.with_memory_space_constraint(value, pltpu.HBM)


def tied(value, *others):
    return lax.optimization_barrier((value, *others))[0]


def on_device(
    patches,
    perms,
    w_in,
    gain_mix,
    w_qkv,
    w_mix,
    gain_out,
    w_head,
    order,
    w_embed,
    gain_attn,
    w_query,
    w_keyval,
    w_attn,
    gain_mlp,
    w_gate,
    w_up,
    w_down,
):
    rows = patches.shape[0]
    local_w = w_qkv.shape[3]
    where = lax.axis_index("tensor")
    patch = lax.axis_index("patch")
    core = patch % 2
    even = core == 0
    ids = jnp.stack([core, where, 0]).astype(jnp.int32)

    w_qkv = w_qkv.transpose(0, 2, 1, 3)
    w_in, w_qkv, w_mix, w_head, perms, gain_mix = map(
        in_hbm, (w_in, w_qkv, w_mix, w_head, perms, gain_mix)
    )
    own_weights = [cut(ids, w_mix, w_head), None]
    side_weights = [lax.ppermute(own_weights[0], "tensor", ACROSS), None]
    field = patches
    logdet = 0.0
    for blk in range(BLOCKS):
        at_blk = jnp.stack([core, where, blk]).astype(jnp.int32)
        hidden, query, keyval, other = pre(at_blk, field, perms, w_in, gain_mix, w_qkv)
        hd = local_w // 2
        got = over(other, CORE)
        query = jnp.concatenate([query, got[:, :hd]], axis=0)
        keyval = jnp.concatenate([keyval, got[:, hd:]], axis=0)
        own = tied(own_weights[blk], keyval) if blk else own_weights[blk]
        own_w = spread(own, side_weights[blk])
        oth_w = [in_hbm(over(w, CORE)) for w in own_w]
        pieces = gather_chips(keyval, False)
        state = attend(query, pieces[:4], [], False)
        state = attend(query, pieces[4:7], state, False)
        (out,) = attend(query, pieces[7:], state, True)
        back = over(out[rows:], CORE)
        front = out[:rows]
        mixed = jnp.concatenate(
            [jnp.where(even, front, back), jnp.where(even, back, front)], axis=1
        )
        mixed = exchange(jnp.broadcast_to(mixed, (NT,) + mixed.shape))
        if blk + 1 < BLOCKS:
            next_blk = tied(jnp.stack([core, where, blk + 1]).astype(jnp.int32), out)
            own_weights[blk + 1] = tied(cut(next_blk, w_mix, w_head), mixed)
            side_weights[blk + 1] = lax.ppermute(own_weights[blk + 1], "tensor", ACROSS)
        field, det = post(at_blk, mixed, own_w, oth_w, hidden, field, perms, gain_out)
        logdet = logdet + det[:, 0]
    embed_part = jnp.dot(field.astype(bf16), w_embed, preferred_element_type=f32).astype(bf16)
    embedded = exchange(jnp.broadcast_to(embed_part, (NT,) + embed_part.shape))
    query_dec, keyval = call(
        enter_kernel,
        [((rows, DH), bf16), ((rows, 2 * DH), bf16)],
        embedded,
        gain_attn[None],
        w_query,
        w_keyval,
        flops=1 << 30,
    )
    pieces = gather_chips(keyval, True)
    pieces = pieces + [over(x, CORE) for x in pieces]

    y, x = patch // 4, (patch // 2) % 2
    owners = [core, patch]
    for dc in (0, 1):
        for dy, dx in ((0, 0), (-1, 0), (1, 0), (0, 1), (-1, 1), (1, 1), (2, 0), (2, 1)):
            owners.append((((y + dy) % 4) * 2 + (x + dx) % 2) * 2 + (core + dc) % 2)
    model_w = w_attn.shape[1]
    (partial_value,) = call(
        causal_kernel,
        [((rows, model_w), bf16)],
        jnp.stack(owners).astype(jnp.int32),
        query_dec,
        order[:, None],
        order[None],
        *pieces,
        in_hbm(w_attn),
        scratch=[
            pltpu.VMEM((NP, rows, rows), f32),
            pltpu.VMEM(w_attn.shape, bf16),
            pltpu.SemaphoreType.DMA,
        ],
        smem=1,
        left=1,
        flops=2 << 30,
    )
    part, cols = rows // NT, model_w // NT
    resid, unit = call(
        resid_kernel,
        [((part, model_w), f32), ((NT, part, model_w), bf16)],
        ids,
        exchange(partial_value.reshape(NT, part, model_w)),
        embedded,
        gain_mlp[None],
        smem=1,
    )
    (down,) = call(
        mlp_kernel,
        [((NT, rows, cols), bf16)],
        ids,
        exchange(unit),
        resid,
        w_gate,
        w_up,
        w_down,
        scratch=[
            pltpu.VMEM((rows, w_gate.shape[1]), bf16),
            pltpu.VMEM((rows, cols), f32),
        ],
        smem=1,
        limit=8,
        flops=4 << 30,
    )
    decoded = jnp.sum(exchange(down).astype(f32), axis=0).astype(bf16)
    return (decoded, logdet)


def solution(mesh):
    return jax.shard_map(
        on_device,
        mesh=mesh,
        in_specs=(
            P("patch", None),
            P(),
            P(),
            P(),
            P(None, None, None, "tensor"),
            P(None, "tensor", None),
            P(),
            P(None, "tensor", None),
            P("patch"),
            P(None, "tensor"),
            P(),
            P(None, "tensor"),
            P(),
            P("tensor", None),
            P(),
            P(None, "tensor"),
            P(None, "tensor"),
            P("tensor", None),
        ),
        out_specs=(P("patch", "tensor"), P("patch")),
        check_vma=False,
    )
```
